256 devices in a mesh: head: 4 (over y), seq: 64 (over z, x, core).
Axes of the slice: x: 4, y: 4, z: 8, core: 2. Of those that a mesh axis runs over, the one named last changes fastest.
Arguments:
- queries: bfloat16 [2, 4, 8192, 640], P(None, 'head', 'seq'), may hold values from -6 to 6
- key_vectors: bfloat16 [2, 4, 8192, 640], P(None, 'head', 'seq'), may hold values from -6 to 6
- value_vectors: bfloat16 [2, 4, 8192, 640], P(None, 'head', 'seq'), may hold values from -6 to 6
- step_sizes: float32 [2, 4, 8192], P(None, 'head', 'seq'), may hold values from 0.1 to 1
- valid_rows: int32 [2, 64], replicated, may hold values from 1 to 128, as said below
- fast_init: bfloat16 [4, 640, 1920], P('head'), may hold values from -0.25 to 0.25
Outputs:
- responses: bfloat16 [2, 4, 8192, 640], P(None, 'head', 'seq')
The draws below stay inside these ranges and needn't reach their ends.
Inputs may be any that keep to these rules, and one draw needn't show every extreme that they name: The live rows of a block are its first valid_rows[c, j] rows; in each group at least one block is entirely live.
All inputs are finite; a program needn't handle non-finite values.
Results may differ from the reference program's by a relative error of at most 0.009.
Values may be sent and summed in bfloat16 or wider, within the bound.
No kernel may reach another device: no remote copies, remote signals or barrier semaphores. Data moves between devices by JAX's collectives and lax.ppermute only.
A program may use at most 64 MiB of HBM per device.

```python
import math
import jax
import jax.numpy as jnp
from jax import lax

HEAD = 640
HEADS = 4
TOK_DEV = 128
GROUP = 8192
N_SEQ = 64


def draw_valid_rows(key, part):
    first_key, second_key, third_key = jax.random.split(key, 3)
    shifts = jax.random.randint(first_key, (2, N_SEQ), 0, 4)
    base_rows = jnp.right_shift(jnp.full((2, N_SEQ), TOK_DEV, jnp.int32), shifts.astype(jnp.int32))
    jitter = jax.random.randint(second_key, (2, N_SEQ), 0, 8)
    counts = base_rows - jitter.astype(jnp.int32) * (base_rows // 16)
    full_block = jax.random.randint(third_key, (2, 1), 0, N_SEQ)
    counts = jnp.where(jnp.arange(N_SEQ)[None, :] == full_block, TOK_DEV, counts)
    return jnp.maximum(counts, 1).astype(jnp.int32)


def level_of(own_key, dims, cuts, low, high):
    factor_of = 1.0
    for position, blocks in cuts:
        draws = jax.random.uniform(jax.random.fold_in(jax.random.fold_in(own_key, 6), position), (blocks,), jnp.float32, low / len(cuts), high / len(cuts))
        factor_of = factor_of * jnp.repeat(jnp.exp(draws), dims[position] // blocks).reshape((-1,) + (1,) * (len(dims) - 1 - position))
    return factor_of


def gaussian(own_key, dims, scale, most, cuts=(), held_as=jnp.bfloat16):
    values = jax.random.normal(own_key, dims, jnp.float32) * scale
    if len(cuts) > 0:
        values = level_of(own_key, dims, cuts, -0.22, 0.18) * values
    return jnp.clip(values, min=-most, max=most).astype(held_as)


def setup_inputs(seed: int = 0) -> dict:
    keys = jax.random.split(jax.random.key(seed), 7)
    queries = gaussian(keys[0], (2, HEADS, GROUP, HEAD), 1.0, 6.0, ((1, 4), (2, 64)))
    key_vectors = gaussian(keys[1], (2, HEADS, GROUP, HEAD), 1.0, 6.0, ((1, 4), (2, 64)))
    value_vectors = gaussian(keys[2], (2, HEADS, GROUP, HEAD), 1.0, 6.0, ((1, 4), (2, 64)))
    step_sizes = jnp.clip(jnp.exp(math.log(1.0) - 2.3025851 * jax.random.uniform(keys[3], (2, HEADS, GROUP), jnp.float32) ** level_of(keys[3], (2, HEADS, GROUP), ((1, 4), (2, 64)), -0.2, 0.2)), 0.1, 1.0)
    valid_rows = draw_valid_rows(jax.random.fold_in(keys[6], 71), 0)
    fast_init = gaussian(keys[5], (HEADS, HEAD, 3 * HEAD), HEAD ** -0.5, 0.25, ((0, 4),))
    return dict(queries=queries, key_vectors=key_vectors, value_vectors=value_vectors, step_sizes=step_sizes, valid_rows=valid_rows, fast_init=fast_init)


step_factor = 0.5
epsilon = 1e-06

def update_weights(weights, key_rows, value_rows, sizes, live_rows):
    width = weights.shape[0]
    gate_weight = weights[:, :width]
    up_weight = weights[:, width:2 * width]
    down_weight = weights[:, 2 * width:]
    scaled = jnp.where(live_rows, sizes, jnp.float32(0.0))
    out_grad = (-(scaled[:, None] * value_rows.astype(jnp.float32))).astype(jnp.bfloat16)
    gate_pre = jnp.dot(key_rows, gate_weight, preferred_element_type=jnp.float32)
    up_proj = jnp.dot(key_rows, up_weight, preferred_element_type=jnp.float32)
    sigmoid_gate = jax.nn.sigmoid(gate_pre)
    hidden = (gate_pre * sigmoid_gate * up_proj).astype(jnp.bfloat16)
    d_hidden = lax.dot_general(out_grad, down_weight, (((1,), (1,)), ((), ())), preferred_element_type=jnp.float32)
    d_up = (d_hidden * gate_pre * sigmoid_gate).astype(jnp.bfloat16)
    d_gate = (d_hidden * up_proj * sigmoid_gate * (1.0 + gate_pre * (1.0 - sigmoid_gate))).astype(jnp.bfloat16)
    grad_in = lax.dot_general(key_rows, jnp.concatenate([d_gate, d_up], 1), (((0,), (0,)), ((), ())), preferred_element_type=jnp.float32)
    grad_down = lax.dot_general(hidden, out_grad, (((0,), (0,)), ((), ())), preferred_element_type=jnp.float32)
    gradient = jnp.concatenate([grad_in, grad_down], 1)
    grad_scale = jnp.sqrt(jnp.sum(gradient * gradient) / (3 * width * width) + epsilon)
    old_weights = weights.astype(jnp.float32)
    moved = old_weights - step_factor / width ** 0.5 / grad_scale * gradient
    norm_ratio = jnp.sqrt(lax.optimization_barrier(jnp.sum(old_weights * old_weights, 0))) / jnp.sqrt(lax.optimization_barrier(jnp.sum(moved * moved, 0)) + epsilon)
    return (moved * norm_ratio[None, :]).astype(jnp.bfloat16)

def apply_weights(weights, query_rows, live_rows):
    width = weights.shape[0]
    gate_pre = jnp.dot(query_rows, weights[:, :width], preferred_element_type=jnp.float32)
    up_proj = jnp.dot(query_rows, weights[:, width:2 * width], preferred_element_type=jnp.float32)
    hidden = (gate_pre * jax.nn.sigmoid(gate_pre) * up_proj).astype(jnp.bfloat16)
    result = jnp.dot(hidden, weights[:, 2 * width:], preferred_element_type=jnp.float32).astype(jnp.bfloat16)
    return jnp.where(live_rows[:, None], result, jnp.zeros_like(result))

def reference(queries, key_vectors, value_vectors, step_sizes, valid_rows, fast_init):
    positions = jnp.arange(GROUP, dtype=jnp.int32)
    live_lists = []
    for group_index in range(2):
        limits = jnp.repeat(valid_rows[group_index], TOK_DEV, total_repeat_length=GROUP)
        live_lists.append(positions % TOK_DEV < limits)
    per_group = [[], []]
    for head_index in range(HEADS):
        weights = fast_init[head_index]
        for group_index in range(2):
            weights = update_weights(weights, key_vectors[group_index, head_index], value_vectors[group_index, head_index], step_sizes[group_index, head_index], live_lists[group_index])
            per_group[group_index].append(apply_weights(weights, queries[group_index, head_index], live_lists[group_index]))
    return jnp.stack([jnp.stack(per_group[0]), jnp.stack(per_group[1])])
```

```python
import jax
import jax.numpy as jnp
from jax import lax
from jax.sharding import Mesh
from jax.sharding import PartitionSpec as P

step_factor = 0.5
epsilon = 1e-06
NX = 4
NZ = 8
F32 = jnp.float32
BF16 = jnp.bfloat16


def dot(a, b, ca, cb):
    return lax.dot_general(a, b, (((ca,), (cb,)), ((), ())), preferred_element_type=F32)


def partial_gradient(half, keys, out_grad):
    gate = dot(keys, half[0], 1, 1)
    up = dot(keys, half[1], 1, 1)
    d_hidden = dot(out_grad, half[2], 1, 1)
    sig = jax.nn.sigmoid(gate)
    hidden = (gate * sig * up).astype(BF16)
    d_up = (d_hidden * gate * sig).astype(BF16)
    d_gate = (d_hidden * up * sig * (1.0 + gate * (1.0 - sig))).astype(BF16)
    parts = [dot(d_gate, keys, 0, 0), dot(d_up, keys, 0, 0), dot(hidden, out_grad, 0, 0)]
    parts = [p.astype(BF16).reshape(NX, -1, p.shape[1]) for p in parts]
    return jnp.concatenate(parts, 1)


def reduced(partial):
    rows = partial.shape[1]
    got = lax.all_to_all(partial, "x", 0, 0, tiled=True)
    mine = jnp.sum(got.astype(F32), 0).astype(BF16)
    mine = jnp.pad(mine, ((0, 256 - rows), (0, 0))).reshape(NZ, 32, -1)
    got = lax.all_to_all(mine, "z", 0, 0, tiled=True)
    shard = jnp.sum(got.astype(F32), 0).astype(BF16)
    got = lax.all_to_all(jnp.broadcast_to(shard[None], (NZ,) + shard.shape), "z", 0, 0, tiled=True)
    block = got.reshape(256, -1)[:rows]
    own = lax.all_to_all(jnp.broadcast_to(block[None], (NX,) + block.shape), "x", 0, 0, tiled=True)
    other = lax.ppermute(own, "c", [(0, 1), (1, 0)])
    first = lax.axis_index("c") == 0
    return jnp.where(first, own, other), jnp.where(first, other, own)


def refreshed(weights, gradient):
    width = weights.shape[1]
    old = weights.astype(F32)
    scale = jnp.sqrt(jnp.sum(gradient * gradient) / (3 * width * width) + epsilon)
    moved = old - step_factor / width**0.5 / scale * gradient

    def norms(w):
        return jnp.sum(w[:2] * w[:2], 2, keepdims=True), jnp.sum(w[2:] * w[2:], 1, keepdims=True)

    old_in, old_out = norms(old)
    new_in, new_out = norms(moved)
    ratio_in = jnp.sqrt(old_in) / jnp.sqrt(new_in + epsilon)
    ratio_out = jnp.sqrt(old_out) / jnp.sqrt(new_out + epsilon)
    return jnp.concatenate([moved[:2] * ratio_in, moved[2:] * ratio_out], 0).astype(BF16)


def answer(weights, queries, live):
    gate = dot(queries, weights[0], 1, 1)
    up = dot(queries, weights[1], 1, 1)
    hidden = (gate * jax.nn.sigmoid(gate) * up).astype(BF16)
    result = dot(hidden, weights[2], 1, 0).astype(BF16)
    return jnp.where(live[:, None], result, jnp.zeros_like(result))


def body(queries, key_vectors, value_vectors, step_sizes, valid_rows, fast_init):
    width = queries.shape[-1]
    rank = (lax.axis_index("z") * NX + lax.axis_index("x")) * 2 + lax.axis_index("c")
    core = lax.axis_index("c")
    rank_ids = jnp.arange(valid_rows.shape[1], dtype=jnp.int32)
    own_rows = jnp.sum(jnp.where(rank_ids == rank, valid_rows, 0), 1)
    live = jnp.arange(queries.shape[2], dtype=jnp.int32)[None] < own_rows[:, None]
    scaled = jnp.where(live, step_sizes[:, 0], F32(0.0))
    out_grad = (-(scaled[..., None] * value_vectors[:, 0].astype(F32))).astype(BF16)
    tokens = jnp.concatenate([key_vectors[:, 0][:, None], out_grad[:, None]], 1)
    other = lax.ppermute(tokens, "c", [(0, 1), (1, 0)])
    tokens = jnp.concatenate([tokens, other], 2)
    first = fast_init[0]
    weights = jnp.stack([first[:, :width].T, first[:, width : 2 * width].T, first[:, 2 * width :]])
    outputs = []
    for group in range(2):
        half = lax.dynamic_slice_in_dim(weights, core * (width // 2), width // 2, 1)
        partial = partial_gradient(half, tokens[group, 0], tokens[group, 1])
        halves = reduced(partial)
        gradient = jnp.stack(halves).reshape(2, NX, 3, -1, width)
        gradient = gradient.transpose(2, 0, 1, 3, 4).reshape(3, width, width).astype(F32)
        weights = refreshed(weights, gradient)
        outputs.append(answer(weights, queries[group, 0], live[group]))
    return jnp.stack(outputs)[:, None]


def solution(mesh):
    split = Mesh(mesh.devices.reshape(mesh.shape["head"], NZ, NX, 2), ("head", "z", "x", "c"))
    seq = ("z", "x", "c")
    rows = P(None, "head", seq, None)
    placed = (rows, rows, rows, P(None, "head", seq), P(), P("head", None, None))
    return jax.shard_map(body, mesh=split, in_specs=placed, out_specs=rows, check_vma=False)
```

```python
import functools

import jax
import jax.numpy as jnp
from jax import lax
from jax.experimental import pallas as pl
from jax.experimental.pallas import tpu as pltpu
from jax.sharding import Mesh
from jax.sharding import PartitionSpec as P

step_factor = 0.5
epsilon = 1e-06
NX = 4
NZ = 8
ROWS = 128
WIDTH = 640
UNITS = 80
PART = 3 * UNITS
PADDED = 256
RATE = step_factor / WIDTH**0.5
COUNT = 3 * WIDTH * WIDTH
F32 = jnp.float32
BF16 = jnp.bfloat16
VMEM = pl.BlockSpec(memory_space=pltpu.VMEM)
SMEM = pl.BlockSpec(memory_space=pltpu.SMEM)


def dot(a, b, ca=1, cb=0):
    return lax.dot_general(a, b, (((ca,), (cb,)), ((), ())), preferred_element_type=F32)


def shape(*dims, dtype=BF16):
    return jax.ShapeDtypeStruct(dims, dtype)


def kernel_call(body, outs, ins):
    return pl.pallas_call(
        body,
        out_shape=outs,
        in_specs=ins,
        out_specs=jax.tree.map(lambda _: VMEM, outs),
        compiler_params=pltpu.CompilerParams(vmem_limit_bytes=40 * 1024 * 1024),
    )


def own_count(valid, group):
    rank = (lax.axis_index("z") * NX + lax.axis_index("x")) * 2 + lax.axis_index("c")
    return valid[group, rank]


def prepare(valid, keys, values, sizes, first, second):
    row = lax.broadcasted_iota(jnp.int32, (ROWS, ROWS), 0)
    col = lax.broadcasted_iota(jnp.int32, (ROWS, ROWS), 1)
    for group, out in ((0, first), (1, second)):
        size = jnp.sum(jnp.where(row == col, sizes[group : group + 1, :], 0.0), 1, keepdims=True)
        scaled = jnp.where(row[:, :1] < own_count(valid, group), size, 0.0)
        out[0] = keys[group]
        out[1] = (-(scaled * values[group].astype(F32))).astype(BF16)


def write_partial(weights, keys, grads, out):
    pre = dot(weights[: 2 * UNITS], keys, 1, 1)
    gate, up = pre[:UNITS], pre[UNITS:]
    d_hidden = dot(weights[2 * UNITS :], grads, 1, 1)
    sig = jax.nn.sigmoid(gate)
    hidden = (gate * sig * up).astype(BF16)
    d_up = (d_hidden * gate * sig).astype(BF16)
    d_gate = (d_hidden * up * sig * (1.0 + gate * (1.0 - sig))).astype(BF16)
    out[0 : 2 * UNITS] = dot(jnp.concatenate([d_gate, d_up], 0), keys).astype(BF16)
    out[2 * UNITS : PART] = dot(hidden, grads).astype(BF16)
    out[PART:] = jnp.zeros((PADDED - PART, WIDTH), BF16)


def first_partial(weights, *refs):
    blocks, out = refs[:-1], refs[-1]
    keys = jnp.concatenate([b[0] for b in blocks], 0)
    grads = jnp.concatenate([b[1] for b in blocks], 0)
    write_partial(weights[...], keys, grads, out)


def summed(got, out):
    total = got[0].astype(F32)
    for i in range(1, NZ):
        total += got[i].astype(F32)
    total = total.astype(BF16)
    for i in range(NZ):
        out[i] = total


def statistics(weights, gradient, out):
    grad = gradient[...].astype(F32)
    old = weights[2 * UNITS :].astype(F32)
    down = grad[2 * UNITS : PART]
    squares = jnp.sum(grad * grad, 0, keepdims=True)
    lines = [
        jnp.sum(old * old, 0, keepdims=True),
        jnp.sum(old * down, 0, keepdims=True),
        jnp.sum(down * down, 0, keepdims=True),
        squares,
    ]
    lines = jnp.concatenate(lines + [jnp.zeros((4, WIDTH), F32)], 0)
    for i in range(2 * NX):
        out[i] = lines


def second_partial(weights, gradient, stats, tokens, fresh, out):
    total = stats[0]
    for i in range(1, 2 * NX):
        total += stats[i]
    rate = RATE / jnp.sqrt(jnp.sum(total[3:4], 1, keepdims=True) / COUNT + epsilon)
    old = weights[...].astype(F32)
    moved = old - rate * gradient[:PART].astype(F32)
    old_in, moved_in = old[: 2 * UNITS], moved[: 2 * UNITS]
    ratio_in = jnp.sqrt(jnp.sum(old_in * old_in, 1, keepdims=True)) / jnp.sqrt(
        jnp.sum(moved_in * moved_in, 1, keepdims=True) + epsilon
    )
    new_out = total[0:1] - 2.0 * rate * total[1:2] + rate * rate * total[2:3]
    ratio_out = jnp.sqrt(total[0:1]) / jnp.sqrt(jnp.maximum(new_out, 0.0) + epsilon)
    new = jnp.concatenate([moved_in * ratio_in, moved[2 * UNITS :] * ratio_out], 0).astype(BF16)
    fresh[...] = new
    keys = jnp.concatenate([tokens[i, 0] for i in range(2 * NX)], 0)
    grads = jnp.concatenate([tokens[i, 1] for i in range(2 * NX)], 0)
    write_partial(new, keys, grads, out)


def respond(rows, live_rows, gate_w, up_w, down_w):
    gate = dot(rows, gate_w, 1, 1)
    up = dot(rows, up_w, 1, 1)
    hidden = (gate * jax.nn.sigmoid(gate) * up).astype(BF16)
    result = dot(hidden, down_w).astype(BF16)
    live = lax.broadcasted_iota(jnp.int32, result.shape, 0) < live_rows
    return jnp.where(live, result, jnp.zeros_like(result))


def first_answer(valid, queries, weights, out):
    parts = [
        jnp.concatenate([weights[b, i * UNITS : (i + 1) * UNITS] for b in range(2 * NX)], 0)
        for i in range(3)
    ]
    out[...] = respond(queries[0], own_count(valid, 0), *parts)


def second_answer(valid, queries, weights, *refs):
    blocks, out, spare = refs[:8], refs[8], refs[9]
    x, c = lax.axis_index("x"), lax.axis_index("c")
    where = [
        lax.rem(x + NX - shift, NX) * 2 + (c if core == 0 else 1 - c)
        for core in range(2)
        for shift in (0, 1, 3, 2)
    ]
    squares = jnp.zeros((1, WIDTH), F32)
    for block in blocks:
        grad = block[:PART].astype(F32)
        squares += jnp.sum(grad * grad, 0, keepdims=True)
    rate = RATE / jnp.sqrt(jnp.sum(squares, 1, keepdims=True) / COUNT + epsilon)
    old_out = jnp.zeros((1, WIDTH), F32)
    new_out = jnp.zeros((1, WIDTH), F32)
    for i, block in enumerate(blocks):
        old = weights[where[i]].astype(F32)
        moved = old - rate * block[:PART].astype(F32)
        old_in, moved_in = old[: 2 * UNITS], moved[: 2 * UNITS]
        ratio_in = jnp.sqrt(jnp.sum(old_in * old_in, 1, keepdims=True)) / jnp.sqrt(
            jnp.sum(moved_in * moved_in, 1, keepdims=True) + epsilon
        )
        fresh = (moved_in * ratio_in).astype(BF16)
        spare[0, i * UNITS : (i + 1) * UNITS] = fresh[:UNITS]
        spare[1, i * UNITS : (i + 1) * UNITS] = fresh[UNITS:]
        old_down, moved_down = old[2 * UNITS :], moved[2 * UNITS :]
        old_out += jnp.sum(old_down * old_down, 0, keepdims=True)
        new_out += jnp.sum(moved_down * moved_down, 0, keepdims=True)
    ratio_out = jnp.sqrt(old_out) / jnp.sqrt(new_out + epsilon)
    for i, block in enumerate(blocks):
        old = weights[where[i], 2 * UNITS :].astype(F32)
        moved = old - rate * block[2 * UNITS : PART].astype(F32)
        spare[2, i * UNITS : (i + 1) * UNITS] = (moved * ratio_out).astype(BF16)
    out[...] = respond(queries[1], own_count(valid, 1), spare[0], spare[1], spare[2])


def shifted(value, axis, size, shift):
    return lax.ppermute(value, axis, [(i, (i + shift) % size) for i in range(size)])


def spread(block):
    near = [block] + [shifted(block, "x", NX, shift) for shift in (1, 3, 2)]
    return near + [shifted(b, "c", 2, 1) for b in near]


def over_z(partial):
    got = lax.all_to_all(partial.reshape(NZ, PADDED // NZ, WIDTH), "z", 0, 0, tiled=True)
    mine = kernel_call(summed, shape(*got.shape), [VMEM])(got)
    got = lax.all_to_all(mine, "z", 0, 0, tiled=True)
    return got.reshape(PADDED, WIDTH)


def body(queries, key_vectors, value_vectors, step_sizes, valid_rows, fast_init):
    queries = queries[:, 0]
    pair = shape(2, ROWS, WIDTH)
    first_tokens, second_tokens = kernel_call(prepare, (pair, pair), [SMEM, VMEM, VMEM, VMEM])(
        valid_rows, key_vectors[:, 0], value_vectors[:, 0], step_sizes[:, 0]
    )
    blocks = spread(first_tokens)
    tokens = lax.all_gather(second_tokens, ("x", "c"), axis=0)
    start = (lax.axis_index("x") * 2 + lax.axis_index("c")) * UNITS
    whole = fast_init[0]
    weights = jnp.concatenate(
        [
            lax.dynamic_slice_in_dim(whole[:, :WIDTH], start, UNITS, 1).T,
            lax.dynamic_slice_in_dim(whole[:, WIDTH : 2 * WIDTH], start, UNITS, 1).T,
            lax.dynamic_slice_in_dim(whole[:, 2 * WIDTH :], start, UNITS, 0),
        ],
        0,
    )
    padded = shape(PADDED, WIDTH)
    partial = kernel_call(first_partial, padded, [VMEM] * 9)(weights, *blocks)
    gradient = over_z(partial)
    stats = kernel_call(statistics, shape(2 * NX, 8, WIDTH, dtype=F32), [VMEM] * 2)(
        weights, gradient
    )
    stats = lax.all_to_all(stats, ("x", "c"), 0, 0, tiled=True)
    fresh, partial = kernel_call(second_partial, (shape(PART, WIDTH), padded), [VMEM] * 4)(
        weights, gradient, stats, tokens
    )
    everyone = lax.all_gather(fresh, ("x", "c"), axis=0)
    gradient = over_z(partial)
    answer = shape(ROWS, WIDTH)
    one = kernel_call(first_answer, answer, [SMEM, VMEM, VMEM])(valid_rows, queries, everyone)
    two = pl.pallas_call(
        second_answer,
        out_shape=answer,
        in_specs=[SMEM] + [VMEM] * 10,
        out_specs=VMEM,
        scratch_shapes=[pltpu.VMEM((3, WIDTH, WIDTH), BF16)],
        compiler_params=pltpu.CompilerParams(vmem_limit_bytes=40 * 1024 * 1024),
    )(valid_rows, queries, everyone, *spread(gradient))
    return jnp.stack([one, two])[:, None]


def solution(mesh):
    split = Mesh(mesh.devices.reshape(mesh.shape["head"], NZ, NX, 2), ("head", "z", "x", "c"))
    seq = ("z", "x", "c")
    rows = P(None, "head", seq, None)
    placed = (rows, rows, rows, P(None, "head", seq), P(), P("head", None, None))
    return jax.shard_map(body, mesh=split, in_specs=placed, out_specs=rows, check_vma=False)
```

```python
import jax
import jax.numpy as jnp
from jax import lax
from jax.experimental import pallas as pl
from jax.experimental.pallas import tpu as pltpu
from jax.sharding import Mesh
from jax.sharding import PartitionSpec as P

step_factor = 0.5
epsilon = 1e-06
NX = 4
NZ = 8
ROWS = 128
WIDTH = 640
UNITS = 80
PART = 3 * UNITS
PADDED = 256
RATE = step_factor / WIDTH**0.5
COUNT = 3 * WIDTH * WIDTH
F32 = jnp.float32
BF16 = jnp.bfloat16
VMEM = pl.BlockSpec(memory_space=pltpu.VMEM)
SMEM = pl.BlockSpec(memory_space=pltpu.SMEM)
HBM = pl.BlockSpec(memory_space=pltpu.HBM)


def dot(a, b, ca=1, cb=0):
    return lax.dot_general(a, b, (((ca,), (cb,)), ((), ())), preferred_element_type=F32)


def shape(*dims, dtype=BF16):
    return jax.ShapeDtypeStruct(dims, dtype)


def kernel_call(body, outs, ins, scratch=()):
    return pl.pallas_call(
        body,
        out_shape=outs,
        in_specs=ins,
        out_specs=jax.tree.map(lambda _: VMEM, outs),
        scratch_shapes=list(scratch),
        compiler_params=pltpu.CompilerParams(vmem_limit_bytes=40 * 1024 * 1024),
    )


def own_count(valid, group):
    rank = (lax.axis_index("z") * NX + lax.axis_index("x")) * 2 + lax.axis_index("c")
    return valid[group, rank]


def fetch(pairs, sems):
    copies = [pltpu.make_async_copy(src, dst, sems.at[i]) for i, (src, dst) in enumerate(pairs)]
    for copy in copies:
        copy.start()
    for copy in copies:
        copy.wait()


def write_grads(live_rows, sizes, values, out):
    row = lax.broadcasted_iota(jnp.int32, (ROWS, ROWS), 0)
    col = lax.broadcasted_iota(jnp.int32, (ROWS, ROWS), 1)
    size = jnp.sum(jnp.where(row == col, sizes[...], 0.0), 1, keepdims=True)
    scaled = jnp.where(row[:, :1] < live_rows, size, 0.0)
    out[1] = (-(scaled * values[...].astype(F32))).astype(BF16)


def prepare_first(valid, keys, values, sizes, out, valid_s, value_s, size_s, sems):
    pairs = [
        (keys.at[0], out.at[0]),
        (values.at[0], value_s),
        (sizes.at[0], size_s),
        (valid, valid_s),
    ]
    fetch(pairs, sems)
    write_grads(own_count(valid_s, 0), size_s, value_s, out)


def prepare_second(
    valid, keys, values, sizes, fast, out, weights, valid_s, value_s, size_s, gate_s, up_s, sems
):
    start = (lax.axis_index("x") * 2 + lax.axis_index("c")) * UNITS
    tile = start // 128
    edge = pl.multiple_of(tile * 128, 128)
    first = pl.multiple_of(start, UNITS)
    pairs = [
        (keys.at[1], out.at[0]),
        (values.at[1], value_s),
        (sizes.at[1], size_s),
        (valid, valid_s),
        (fast.at[:, pl.ds(edge, 256)], gate_s),
        (fast.at[:, pl.ds(WIDTH + edge, 256)], up_s),
        (
            fast.at[pl.ds(first, UNITS), pl.ds(2 * WIDTH, WIDTH)],
            weights.at[pl.ds(2 * UNITS, UNITS)],
        ),
    ]
    fetch(pairs, sems)
    write_grads(own_count(valid_s, 1), size_s, value_s, out)
    row = lax.broadcasted_iota(jnp.int32, (UNITS, 256), 0)
    col = lax.broadcasted_iota(jnp.int32, (UNITS, 256), 1)
    chosen = jnp.where(col == row + (start - edge), 1.0, 0.0).astype(BF16)
    weights[0:UNITS] = dot(chosen, gate_s[...], 1, 1).astype(BF16)
    weights[UNITS : 2 * UNITS] = dot(chosen, up_s[...], 1, 1).astype(BF16)


def write_partial(weights, keys, grads, out):
    pre = dot(weights[: 2 * UNITS], keys, 1, 1)
    gate, up = pre[:UNITS], pre[UNITS:]
    d_hidden = dot(weights[2 * UNITS :], grads, 1, 1)
    sig = jax.nn.sigmoid(gate)
    hidden = (gate * sig * up).astype(BF16)
    d_up = (d_hidden * gate * sig).astype(BF16)
    d_gate = (d_hidden * up * sig * (1.0 + gate * (1.0 - sig))).astype(BF16)
    out[0 : 2 * UNITS] = dot(jnp.concatenate([d_gate, d_up], 0), keys).astype(BF16)
    out[2 * UNITS : PART] = dot(hidden, grads).astype(BF16)
    out[PART:] = jnp.zeros((PADDED - PART, WIDTH), BF16)


def first_partial(weights, *refs):
    blocks, out = refs[:-1], refs[-1]
    keys = jnp.concatenate([b[0] for b in blocks], 0)
    grads = jnp.concatenate([b[1] for b in blocks], 0)
    write_partial(weights[...], keys, grads, out)


def summed(got, out):
    total = got[0].astype(F32)
    for i in range(1, NZ):
        total += got[i].astype(F32)
    total = total.astype(BF16)
    for i in range(NZ):
        out[i] = total


def statistics(weights, gradient, out):
    grad = gradient[...].astype(F32)
    old = weights[2 * UNITS :].astype(F32)
    down = grad[2 * UNITS : PART]
    squares = jnp.sum(grad * grad, 0, keepdims=True)
    lines = [
        jnp.sum(old * old, 0, keepdims=True),
        jnp.sum(old * down, 0, keepdims=True),
        jnp.sum(down * down, 0, keepdims=True),
        squares,
    ]
    lines = jnp.concatenate(lines + [jnp.zeros((4, WIDTH), F32)], 0)
    for i in range(2 * NX):
        out[i] = lines


def second_partial(weights, gradient, stats, *refs):
    blocks, fresh, out = refs[:-2], refs[-2], refs[-1]
    total = stats[0]
    for i in range(1, 2 * NX):
        total += stats[i]
    rate = RATE / jnp.sqrt(jnp.sum(total[3:4], 1, keepdims=True) / COUNT + epsilon)
    old = weights[...].astype(F32)
    moved = old - rate * gradient[:PART].astype(F32)
    old_in, moved_in = old[: 2 * UNITS], moved[: 2 * UNITS]
    ratio_in = jnp.sqrt(jnp.sum(old_in * old_in, 1, keepdims=True)) / jnp.sqrt(
        jnp.sum(moved_in * moved_in, 1, keepdims=True) + epsilon
    )
    new_out = total[0:1] - 2.0 * rate * total[1:2] + rate * rate * total[2:3]
    ratio_out = jnp.sqrt(total[0:1]) / jnp.sqrt(jnp.maximum(new_out, 0.0) + epsilon)
    new = jnp.concatenate([moved_in * ratio_in, moved[2 * UNITS :] * ratio_out], 0).astype(BF16)
    fresh[...] = new
    keys = jnp.concatenate([b[0] for b in blocks], 0)
    grads = jnp.concatenate([b[1] for b in blocks], 0)
    write_partial(new, keys, grads, out)


def respond(rows, live_rows, gate_w, up_w, down_w):
    gate = dot(rows, gate_w, 1, 1)
    up = dot(rows, up_w, 1, 1)
    hidden = (gate * jax.nn.sigmoid(gate) * up).astype(BF16)
    result = dot(hidden, down_w).astype(BF16)
    live = lax.broadcasted_iota(jnp.int32, result.shape, 0) < live_rows
    return jnp.where(live, result, jnp.zeros_like(result))


def first_answer(valid, queries, *refs):
    blocks, out = refs[:-1], refs[-1]
    parts = [
        jnp.concatenate([b[i * UNITS : (i + 1) * UNITS] for b in blocks], 0) for i in range(3)
    ]
    out[...] = respond(queries[0], own_count(valid, 0), *parts)


def second_answer(valid, queries, one, *refs):
    held, blocks, out, spare = refs[:8], refs[8:16], refs[16], refs[17]
    squares = jnp.zeros((1, WIDTH), F32)
    for block in blocks:
        grad = block[:PART].astype(F32)
        squares += jnp.sum(grad * grad, 0, keepdims=True)
    rate = RATE / jnp.sqrt(jnp.sum(squares, 1, keepdims=True) / COUNT + epsilon)
    old_out = jnp.zeros((1, WIDTH), F32)
    new_out = jnp.zeros((1, WIDTH), F32)
    for i, (weights, block) in enumerate(zip(held, blocks)):
        old = weights[...].astype(F32)
        moved = old - rate * block[:PART].astype(F32)
        old_in, moved_in = old[: 2 * UNITS], moved[: 2 * UNITS]
        ratio_in = jnp.sqrt(jnp.sum(old_in * old_in, 1, keepdims=True)) / jnp.sqrt(
            jnp.sum(moved_in * moved_in, 1, keepdims=True) + epsilon
        )
        fresh = (moved_in * ratio_in).astype(BF16)
        spare[0, i * UNITS : (i + 1) * UNITS] = fresh[:UNITS]
        spare[1, i * UNITS : (i + 1) * UNITS] = fresh[UNITS:]
        old_down, moved_down = old[2 * UNITS :], moved[2 * UNITS :]
        old_out += jnp.sum(old_down * old_down, 0, keepdims=True)
        new_out += jnp.sum(moved_down * moved_down, 0, keepdims=True)
    ratio_out = jnp.sqrt(old_out) / jnp.sqrt(new_out + epsilon)
    for i, (weights, block) in enumerate(zip(held, blocks)):
        old = weights[2 * UNITS :].astype(F32)
        moved = old - rate * block[2 * UNITS : PART].astype(F32)
        spare[2, i * UNITS : (i + 1) * UNITS] = (moved * ratio_out).astype(BF16)
    out[0] = one[...]
    out[1] = respond(queries[1], own_count(valid, 1), spare[0], spare[1], spare[2])


def shifted(value, axis, size, shift):
    return lax.ppermute(value, axis, [(i, (i + shift) % size) for i in range(size)])


def along_x(block):
    return [block] + [shifted(block, "x", NX, shift) for shift in (1, 3, 2)]


def with_core(near):
    return near + [shifted(b, "c", 2, 1) for b in near]


def reduce_z(partial):
    got = lax.all_to_all(partial.reshape(NZ, PADDED // NZ, WIDTH), "z", 0, 0, tiled=True)
    return kernel_call(summed, shape(*got.shape), [VMEM])(got)


def gather_z(shards):
    return lax.all_to_all(shards, "z", 0, 0, tiled=True).reshape(PADDED, WIDTH)


def body(queries, key_vectors, value_vectors, step_sizes, valid_rows, fast_init):
    queries = queries[:, 0]
    held_inputs = (valid_rows, key_vectors[:, 0], value_vectors[:, 0], step_sizes, fast_init[0])
    inputs = [pltpu.with_memory_space_constraint(i, pltpu.HBM) for i in held_inputs]
    pair, padded = shape(2, ROWS, WIDTH), shape(PADDED, WIDTH)
    scratch = [
        pltpu.SMEM(valid_rows.shape, jnp.int32),
        pltpu.VMEM((ROWS, WIDTH), BF16),
        pltpu.VMEM((1, ROWS), F32),
    ]
    first = kernel_call(prepare_first, pair, [HBM] * 4, scratch + [pltpu.SemaphoreType.DMA((4,))])(
        *inputs[:4]
    )
    near = along_x(first)
    windows = [pltpu.VMEM((WIDTH, 256), BF16)] * 2
    second, weights = kernel_call(
        prepare_second,
        (pair, shape(PART, WIDTH)),
        [HBM] * 5,
        scratch + windows + [pltpu.SemaphoreType.DMA((7,))],
    )(*inputs)
    near[3], second, weights = lax.optimization_barrier((near[3], second, weights))
    near_two = along_x(second)
    partial = kernel_call(first_partial, padded, [VMEM] * 9)(weights, *with_core(near))
    shards = reduce_z(partial)
    shards, near_two = lax.optimization_barrier((shards, near_two))
    tokens = with_core(near_two)
    gradient = gather_z(shards)
    stats = kernel_call(statistics, shape(2 * NX, 8, WIDTH, dtype=F32), [VMEM] * 2)(
        weights, gradient
    )
    stats = lax.all_to_all(stats, ("x", "c"), 0, 0, tiled=True)
    fresh, partial = kernel_call(second_partial, (shape(PART, WIDTH), padded), [VMEM] * 11)(
        weights, gradient, stats, *tokens
    )
    near_weights = along_x(fresh)
    shards = reduce_z(partial)
    shards, near_weights = lax.optimization_barrier((shards, near_weights))
    held = with_core(near_weights)
    gradient = gather_z(shards)
    one = kernel_call(first_answer, shape(ROWS, WIDTH), [SMEM] + [VMEM] * 9)(
        valid_rows, queries, *held
    )
    out = kernel_call(
        second_answer,
        shape(2, ROWS, WIDTH),
        [SMEM] + [VMEM] * 18,
        [pltpu.VMEM((3, WIDTH, WIDTH), BF16)],
    )(valid_rows, queries, one, *held, *with_core(along_x(gradient)))
    return out[:, None]


def solution(mesh):
    split = Mesh(mesh.devices.reshape(mesh.shape["head"], NZ, NX, 2), ("head", "z", "x", "c"))
    seq = ("z", "x", "c")
    rows = P(None, "head", seq, None)
    placed = (rows, rows, rows, P(None, "head", seq), P(), P("head", None, None))
    return jax.shard_map(body, mesh=split, in_specs=placed, out_specs=rows, check_vma=False)
```

```python
import jax
import jax.numpy as jnp
from jax import lax
from jax.experimental import pallas as pl
from jax.experimental.pallas import tpu as pltpu
from jax.sharding import Mesh
from jax.sharding import PartitionSpec as P

step_factor = 0.5
epsilon = 1e-06
NX = 4
NZ = 8
ROWS = 128
WIDTH = 640
UNITS = 80
PART = 3 * UNITS
PADDED = 256
RATE = step_factor / WIDTH**0.5
COUNT = 3 * WIDTH * WIDTH
F32 = jnp.float32
BF16 = jnp.bfloat16
VMEM = pl.BlockSpec(memory_space=pltpu.VMEM)
SMEM = pl.BlockSpec(memory_space=pltpu.SMEM)
HBM = pl.BlockSpec(memory_space=pltpu.HBM)


def dot(a, b, ca=1, cb=0):
    return lax.dot_general(a, b, (((ca,), (cb,)), ((), ())), preferred_element_type=F32)


def shape(*dims, dtype=BF16):
    return jax.ShapeDtypeStruct(dims, dtype)


def kernel_call(body, outs, ins, scratch=()):
    return pl.pallas_call(
        body,
        out_shape=outs,
        in_specs=ins,
        out_specs=jax.tree.map(lambda _: VMEM, outs),
        scratch_shapes=list(scratch),
        compiler_params=pltpu.CompilerParams(vmem_limit_bytes=40 * 1024 * 1024),
    )


def own_count(valid, group):
    rank = (lax.axis_index("z") * NX + lax.axis_index("x")) * 2 + lax.axis_index("c")
    return valid[group, rank]


def fetch(pairs, sems):
    copies = [pltpu.make_async_copy(src, dst, sems.at[i]) for i, (src, dst) in enumerate(pairs)]
    for copy in copies:
        copy.start()
    for copy in copies:
        copy.wait()


def write_grads(live_rows, sizes, values, out):
    row = lax.broadcasted_iota(jnp.int32, (ROWS, ROWS), 0)
    col = lax.broadcasted_iota(jnp.int32, (ROWS, ROWS), 1)
    size = jnp.sum(jnp.where(row == col, sizes[...], 0.0), 1, keepdims=True)
    scaled = jnp.where(row[:, :1] < live_rows, size, 0.0)
    out[1] = (-(scaled * values[...].astype(F32))).astype(BF16)


def prepare_first(valid, keys, values, sizes, out, valid_s, value_s, size_s, sems):
    pairs = [
        (keys.at[0], out.at[0]),
        (values.at[0], value_s),
        (sizes.at[0], size_s),
        (valid, valid_s),
    ]
    fetch(pairs, sems)
    write_grads(own_count(valid_s, 0), size_s, value_s, out)


def prepare_second(
    valid, keys, values, sizes, fast, out, weights, valid_s, value_s, size_s, gate_s, up_s, sems
):
    start = (lax.axis_index("x") * 2 + lax.axis_index("c")) * UNITS
    tile = start // 128
    edge = pl.multiple_of(tile * 128, 128)
    first = pl.multiple_of(start, UNITS)
    pairs = [
        (keys.at[1], out.at[0]),
        (values.at[1], value_s),
        (sizes.at[1], size_s),
        (valid, valid_s),
        (fast.at[:, pl.ds(edge, 256)], gate_s),
        (fast.at[:, pl.ds(WIDTH + edge, 256)], up_s),
        (
            fast.at[pl.ds(first, UNITS), pl.ds(2 * WIDTH, WIDTH)],
            weights.at[pl.ds(2 * UNITS, UNITS)],
        ),
    ]
    fetch(pairs, sems)
    write_grads(own_count(valid_s, 1), size_s, value_s, out)
    row = lax.broadcasted_iota(jnp.int32, (UNITS, 256), 0)
    col = lax.broadcasted_iota(jnp.int32, (UNITS, 256), 1)
    chosen = jnp.where(col == row + (start - edge), 1.0, 0.0).astype(BF16)
    weights[0:UNITS] = dot(chosen, gate_s[...], 1, 1).astype(BF16)
    weights[UNITS : 2 * UNITS] = dot(chosen, up_s[...], 1, 1).astype(BF16)


def write_partial(weights, keys, grads, out):
    pre = dot(weights[: 2 * UNITS], keys, 1, 1)
    gate, up = pre[:UNITS], pre[UNITS:]
    d_hidden = dot(weights[2 * UNITS :], grads, 1, 1)
    sig = jax.nn.sigmoid(gate)
    hidden = (gate * sig * up).astype(BF16)
    d_up = (d_hidden * gate * sig).astype(BF16)
    d_gate = (d_hidden * up * sig * (1.0 + gate * (1.0 - sig))).astype(BF16)
    out[0 : 2 * UNITS] = dot(jnp.concatenate([d_gate, d_up], 0), keys).astype(BF16)
    out[2 * UNITS : PART] = dot(hidden, grads).astype(BF16)
    out[PART:] = jnp.zeros((PADDED - PART, WIDTH), BF16)


def first_partial(weights, *refs):
    blocks, out = refs[:-1], refs[-1]
    keys = jnp.concatenate([b[0] for b in blocks], 0)
    grads = jnp.concatenate([b[1] for b in blocks], 0)
    write_partial(weights[...], keys, grads, out)


def summed(got, out):
    total = got[0].astype(F32)
    for i in range(1, NZ):
        total += got[i].astype(F32)
    total = total.astype(BF16)
    for i in range(NZ):
        out[i] = total


def statistics(weights, gradient, out):
    grad = gradient[...].astype(F32)
    old = weights[2 * UNITS :].astype(F32)
    down = grad[2 * UNITS : PART]
    squares = jnp.sum(grad * grad, 0, keepdims=True)
    lines = [
        jnp.sum(old * old, 0, keepdims=True),
        jnp.sum(old * down, 0, keepdims=True),
        jnp.sum(down * down, 0, keepdims=True),
        squares,
    ]
    lines = jnp.concatenate(lines + [jnp.zeros((4, WIDTH), F32)], 0)
    for i in range(2 * NX):
        out[i] = lines


def second_partial(weights, gradient, stats, *refs):
    blocks, fresh, out = refs[:-2], refs[-2], refs[-1]
    total = stats[0]
    for i in range(1, 2 * NX):
        total += stats[i]
    rate = RATE / jnp.sqrt(jnp.sum(total[3:4], 1, keepdims=True) / COUNT + epsilon)
    old = weights[...].astype(F32)
    moved = old - rate * gradient[:PART].astype(F32)
    old_in, moved_in = old[: 2 * UNITS], moved[: 2 * UNITS]
    ratio_in = jnp.sqrt(jnp.sum(old_in * old_in, 1, keepdims=True)) / jnp.sqrt(
        jnp.sum(moved_in * moved_in, 1, keepdims=True) + epsilon
    )
    new_out = total[0:1] - 2.0 * rate * total[1:2] + rate * rate * total[2:3]
    ratio_out = jnp.sqrt(total[0:1]) / jnp.sqrt(jnp.maximum(new_out, 0.0) + epsilon)
    new = jnp.concatenate([moved_in * ratio_in, moved[2 * UNITS :] * ratio_out], 0).astype(BF16)
    fresh[...] = new
    keys = jnp.concatenate([b[0] for b in blocks], 0)
    grads = jnp.concatenate([b[1] for b in blocks], 0)
    write_partial(new, keys, grads, out)


def respond(rows, live_rows, gate_w, up_w, down_w):
    gate = dot(rows, gate_w, 1, 1)
    up = dot(rows, up_w, 1, 1)
    hidden = (gate * jax.nn.sigmoid(gate) * up).astype(BF16)
    result = dot(hidden, down_w).astype(BF16)
    live = lax.broadcasted_iota(jnp.int32, result.shape, 0) < live_rows
    return jnp.where(live, result, jnp.zeros_like(result))


def first_answer(valid, queries, *refs):
    blocks, out = refs[:-1], refs[-1]
    parts = [
        jnp.concatenate([b[i * UNITS : (i + 1) * UNITS] for b in blocks], 0) for i in range(3)
    ]
    out[...] = respond(queries[0], own_count(valid, 0), *parts)


def second_answer(valid, queries, one, *refs):
    held, blocks, out, spare = refs[:8], refs[8:16], refs[16], refs[17]
    squares = jnp.zeros((1, WIDTH), F32)
    for block in blocks:
        grad = block[:PART].astype(F32)
        squares += jnp.sum(grad * grad, 0, keepdims=True)
    rate = RATE / jnp.sqrt(jnp.sum(squares, 1, keepdims=True) / COUNT + epsilon)
    old_out = jnp.zeros((1, WIDTH), F32)
    new_out = jnp.zeros((1, WIDTH), F32)
    for i, (weights, block) in enumerate(zip(held, blocks)):
        old = weights[...].astype(F32)
        moved = old - rate * block[:PART].astype(F32)
        old_in, moved_in = old[: 2 * UNITS], moved[: 2 * UNITS]
        ratio_in = jnp.sqrt(jnp.sum(old_in * old_in, 1, keepdims=True)) / jnp.sqrt(
            jnp.sum(moved_in * moved_in, 1, keepdims=True) + epsilon
        )
        fresh = (moved_in * ratio_in).astype(BF16)
        spare[0, i * UNITS : (i + 1) * UNITS] = fresh[:UNITS]
        spare[1, i * UNITS : (i + 1) * UNITS] = fresh[UNITS:]
        old_down, moved_down = old[2 * UNITS :], moved[2 * UNITS :]
        old_out += jnp.sum(old_down * old_down, 0, keepdims=True)
        new_out += jnp.sum(moved_down * moved_down, 0, keepdims=True)
    ratio_out = jnp.sqrt(old_out) / jnp.sqrt(new_out + epsilon)
    for i, (weights, block) in enumerate(zip(held, blocks)):
        old = weights[2 * UNITS :].astype(F32)
        moved = old - rate * block[2 * UNITS : PART].astype(F32)
        spare[2, i * UNITS : (i + 1) * UNITS] = (moved * ratio_out).astype(BF16)
    out[0] = one[...]
    out[1] = respond(queries[1], own_count(valid, 1), spare[0], spare[1], spare[2])


def shifted(value, axis, size, shift):
    return lax.ppermute(value, axis, [(i, (i + shift) % size) for i in range(size)])


def along_x(block):
    return [block] + [shifted(block, "x", NX, shift) for shift in (1, 3, 2)]


def with_core(near):
    return near + [shifted(b, "c", 2, 1) for b in near]


def reduce_z(partial):
    got = lax.all_to_all(partial.reshape(NZ, PADDED // NZ, WIDTH), "z", 0, 0, tiled=True)
    return kernel_call(summed, shape(*got.shape), [VMEM])(got)


def gather_z(shards):
    return lax.all_to_all(shards, "z", 0, 0, tiled=True).reshape(PADDED, WIDTH)


def body(queries, key_vectors, value_vectors, step_sizes, valid_rows, fast_init):
    queries = queries[:, 0]
    held_inputs = (valid_rows, key_vectors[:, 0], value_vectors[:, 0], step_sizes, fast_init[0])
    inputs = [pltpu.with_memory_space_constraint(i, pltpu.HBM) for i in held_inputs]
    pair, padded = shape(2, ROWS, WIDTH), shape(PADDED, WIDTH)
    scratch = [
        pltpu.SMEM(valid_rows.shape, jnp.int32),
        pltpu.VMEM((ROWS, WIDTH), BF16),
        pltpu.VMEM((1, ROWS), F32),
    ]
    first = kernel_call(prepare_first, pair, [HBM] * 4, scratch + [pltpu.SemaphoreType.DMA((4,))])(
        *inputs[:4]
    )
    near = along_x(first)
    windows = [pltpu.VMEM((WIDTH, 256), BF16)] * 2
    second, weights = kernel_call(
        prepare_second,
        (pair, shape(PART, WIDTH)),
        [HBM] * 5,
        scratch + windows + [pltpu.SemaphoreType.DMA((7,))],
    )(*inputs)
    near[3], second, weights = lax.optimization_barrier((near[3], second, weights))
    near_two = along_x(second)
    partial = kernel_call(first_partial, padded, [VMEM] * 9)(weights, *with_core(near))
    shards = reduce_z(partial)
    shards, *near_two[:3] = lax.optimization_barrier((shards, *near_two[:3]))
    gradient, near_two = lax.optimization_barrier((gather_z(shards), near_two))
    tokens = with_core(near_two)
    stats = kernel_call(statistics, shape(2 * NX, 8, WIDTH, dtype=F32), [VMEM] * 2)(
        weights, gradient
    )
    stats = lax.all_to_all(stats, ("x", "c"), 0, 0, tiled=True)
    fresh, partial = kernel_call(second_partial, (shape(PART, WIDTH), padded), [VMEM] * 11)(
        weights, gradient, stats, *tokens
    )
    near_weights = along_x(fresh)
    shards = reduce_z(partial)
    shards, *near_weights[:3] = lax.optimization_barrier((shards, *near_weights[:3]))
    gradient, near_weights = lax.optimization_barrier((gather_z(shards), near_weights))
    near = along_x(gradient)
    held = with_core(near_weights)
    one = kernel_call(first_answer, shape(ROWS, WIDTH), [SMEM] + [VMEM] * 9)(
        valid_rows, queries, *held
    )
    near[3], one = lax.optimization_barrier((near[3], one))
    out = kernel_call(
        second_answer,
        shape(2, ROWS, WIDTH),
        [SMEM] + [VMEM] * 18,
        [pltpu.VMEM((3, WIDTH, WIDTH), BF16)],
    )(valid_rows, queries, one, *held, *with_core(near))
    return out[:, None]


def solution(mesh):
    split = Mesh(mesh.devices.reshape(mesh.shape["head"], NZ, NX, 2), ("head", "z", "x", "c"))
    seq = ("z", "x", "c")
    rows = P(None, "head", seq, None)
    placed = (rows, rows, rows, P(None, "head", seq), P(), P("head", None, None))
    return jax.shard_map(body, mesh=split, in_specs=placed, out_specs=rows, check_vma=False)
```

```python
import jax
import jax.numpy as jnp
from jax import lax
from jax.experimental import pallas as pl
from jax.experimental.pallas import tpu as pltpu
from jax.sharding import Mesh
from jax.sharding import PartitionSpec as P

step_factor = 0.5
epsilon = 1e-06
NX = 4
NZ = 8
ROWS = 128
WIDTH = 640
UNITS = 80
HALF = NX * UNITS
SHIFTS = (0, 1, 3, 2)
PART = 3 * UNITS
PADDED = 256
RATE = step_factor / WIDTH**0.5
COUNT = 3 * WIDTH * WIDTH
F32 = jnp.float32
BF16 = jnp.bfloat16
VMEM = pl.BlockSpec(memory_space=pltpu.VMEM)
SMEM = pl.BlockSpec(memory_space=pltpu.SMEM)
HBM = pl.BlockSpec(memory_space=pltpu.HBM)


def dot(a, b, ca=1, cb=0):
    return lax.dot_general(a, b, (((ca,), (cb,)), ((), ())), preferred_element_type=F32)


def shape(*dims, dtype=BF16):
    return jax.ShapeDtypeStruct(dims, dtype)


def kernel_call(body, outs, ins, scratch=()):
    return pl.pallas_call(
        body,
        out_shape=outs,
        in_specs=ins,
        out_specs=jax.tree.map(lambda _: VMEM, outs),
        scratch_shapes=list(scratch),
        compiler_params=pltpu.CompilerParams(vmem_limit_bytes=20 * 1024 * 1024),
    )


def own_count(valid, group):
    rank = (lax.axis_index("z") * NX + lax.axis_index("x")) * 2 + lax.axis_index("c")
    return valid[group, rank]


def fetch(pairs, sems):
    copies = [pltpu.make_async_copy(src, dst, sems.at[i]) for i, (src, dst) in enumerate(pairs)]
    for copy in copies:
        copy.start()
    for copy in copies:
        copy.wait()


def write_grads(live_rows, sizes, values, out):
    row = lax.broadcasted_iota(jnp.int32, (ROWS, ROWS), 0)
    col = lax.broadcasted_iota(jnp.int32, (ROWS, ROWS), 1)
    size = jnp.sum(jnp.where(row == col, sizes[...], 0.0), 1, keepdims=True)
    scaled = jnp.where(row[:, :1] < live_rows, size, 0.0)
    out[1] = (-(scaled * values[...].astype(F32))).astype(BF16)


def prepare_first(valid, keys, values, sizes, out, valid_s, value_s, size_s, sems):
    pairs = [
        (keys.at[0], out.at[0]),
        (values.at[0], value_s),
        (sizes.at[0], size_s),
        (valid, valid_s),
    ]
    fetch(pairs, sems)
    write_grads(own_count(valid_s, 0), size_s, value_s, out)


def prepare_second(valid, keys, values, sizes, out, valid_s, value_s, size_s, sems):
    pairs = [
        (keys.at[1], out.at[0]),
        (values.at[1], value_s),
        (sizes.at[1], size_s),
        (valid, valid_s),
    ]
    fetch(pairs, sems)
    write_grads(own_count(valid_s, 1), size_s, value_s, out)


def half_weights(fast, weights, gate_s, up_s, sems):
    x, c = lax.axis_index("x"), lax.axis_index("c")
    start = c * HALF
    edge = pl.multiple_of(c * 256, 128)
    pairs = [
        (fast.at[:, pl.ds(edge, 384)], gate_s),
        (fast.at[:, pl.ds(WIDTH + edge, 384)], up_s),
    ]
    row = lax.broadcasted_iota(jnp.int32, (HALF, 384), 0)
    col = lax.broadcasted_iota(jnp.int32, (HALF, 384), 1)
    wanted = row
    for i, shift in enumerate(SHIFTS):
        block = lax.rem(x + shift, NX)
        first = pl.multiple_of(start + block * UNITS, UNITS)
        source = fast.at[pl.ds(first, UNITS), pl.ds(2 * WIDTH, WIDTH)]
        pairs.append((source, weights.at[2, pl.ds(i * UNITS, UNITS)]))
        inside = (row >= i * UNITS) & (row < (i + 1) * UNITS)
        wanted = jnp.where(inside, first - edge + row - i * UNITS, wanted)
    chosen = jnp.where(col == wanted, 1.0, 0.0).astype(BF16)
    fetch(pairs, sems)
    weights[0] = dot(chosen, gate_s[...], 1, 1).astype(BF16)
    weights[1] = dot(chosen, up_s[...], 1, 1).astype(BF16)


def gradients(into, down, keys, grads):
    units = down.shape[0]
    pre = dot(into, keys, 1, 1)
    gate, up = pre[:units], pre[units:]
    d_hidden = dot(down, grads, 1, 1)
    sig = jax.nn.sigmoid(gate)
    hidden = (gate * sig * up).astype(BF16)
    d_up = (d_hidden * gate * sig).astype(BF16)
    d_gate = (d_hidden * up * sig * (1.0 + gate * (1.0 - sig))).astype(BF16)
    inner = dot(jnp.concatenate([d_gate, d_up], 0), keys).astype(BF16)
    return inner, dot(hidden, grads).astype(BF16)


def first_partial(weights, own, other, *outs):
    keys = jnp.concatenate([own[0], other[0]], 0)
    grads = jnp.concatenate([own[1], other[1]], 0)
    into = jnp.concatenate([weights[0], weights[1]], 0)
    inner, outer = gradients(into, weights[2], keys, grads)
    for i, out in enumerate(outs):
        rows = slice(i * UNITS, (i + 1) * UNITS)
        out[0:UNITS] = inner[rows]
        out[UNITS : 2 * UNITS] = inner[HALF:][rows]
        out[2 * UNITS :] = outer[rows]


def summed_x(*refs):
    blocks, out = refs[:-1], refs[-1]
    total = blocks[0][...].astype(F32)
    for block in blocks[1:]:
        total += block[...].astype(F32)
    out[0:PART] = total.astype(BF16)
    out[PART:] = jnp.zeros((PADDED - PART, WIDTH), BF16)


def own_weights(weights):
    return jnp.concatenate([weights[i, :UNITS] for i in range(3)], 0)


def summed(got, out):
    total = got[0].astype(F32)
    for i in range(1, NZ):
        total += got[i].astype(F32)
    total = total.astype(BF16)
    for i in range(NZ):
        out[i] = total


def statistics(weights, gradient, out):
    grad = gradient[...].astype(F32)
    old = weights[2, :UNITS].astype(F32)
    down = grad[2 * UNITS : PART]
    squares = jnp.sum(grad * grad, 0, keepdims=True)
    lines = [
        jnp.sum(old * old, 0, keepdims=True),
        jnp.sum(old * down, 0, keepdims=True),
        jnp.sum(down * down, 0, keepdims=True),
        squares,
    ]
    lines = jnp.concatenate(lines + [jnp.zeros((4, WIDTH), F32)], 0)
    for i in range(2 * NX):
        out[i] = lines


def second_partial(weights, gradient, stats, *refs):
    blocks, fresh, out = refs[:-2], refs[-2], refs[-1]
    total = stats[0]
    for i in range(1, 2 * NX):
        total += stats[i]
    rate = RATE / jnp.sqrt(jnp.sum(total[3:4], 1, keepdims=True) / COUNT + epsilon)
    old = own_weights(weights).astype(F32)
    moved = old - rate * gradient[:PART].astype(F32)
    old_in, moved_in = old[: 2 * UNITS], moved[: 2 * UNITS]
    ratio_in = jnp.sqrt(jnp.sum(old_in * old_in, 1, keepdims=True)) / jnp.sqrt(
        jnp.sum(moved_in * moved_in, 1, keepdims=True) + epsilon
    )
    new_out = total[0:1] - 2.0 * rate * total[1:2] + rate * rate * total[2:3]
    ratio_out = jnp.sqrt(total[0:1]) / jnp.sqrt(jnp.maximum(new_out, 0.0) + epsilon)
    new = jnp.concatenate([moved_in * ratio_in, moved[2 * UNITS :] * ratio_out], 0).astype(BF16)
    fresh[...] = new
    keys = jnp.concatenate([b[0] for b in blocks], 0)
    grads = jnp.concatenate([b[1] for b in blocks], 0)
    inner, outer = gradients(new[: 2 * UNITS], new[2 * UNITS :], keys, grads)
    out[0 : 2 * UNITS] = inner
    out[2 * UNITS : PART] = outer
    out[PART:] = jnp.zeros((PADDED - PART, WIDTH), BF16)


def respond(rows, live_rows, gate_w, up_w, down_w):
    gate = dot(rows, gate_w, 1, 1)
    up = dot(rows, up_w, 1, 1)
    hidden = (gate * jax.nn.sigmoid(gate) * up).astype(BF16)
    result = dot(hidden, down_w).astype(BF16)
    live = lax.broadcasted_iota(jnp.int32, result.shape, 0) < live_rows
    return jnp.where(live, result, jnp.zeros_like(result))


def first_answer(valid, queries, *refs):
    blocks, out = refs[:-1], refs[-1]
    parts = [
        jnp.concatenate([b[i * UNITS : (i + 1) * UNITS] for b in blocks], 0) for i in range(3)
    ]
    out[...] = respond(queries[0], own_count(valid, 0), *parts)


def second_answer(valid, queries, one, *refs):
    held, blocks, out, spare = refs[:8], refs[8:16], refs[16], refs[17]
    squares = jnp.zeros((1, WIDTH), F32)
    for block in blocks:
        grad = block[:PART].astype(F32)
        squares += jnp.sum(grad * grad, 0, keepdims=True)
    rate = RATE / jnp.sqrt(jnp.sum(squares, 1, keepdims=True) / COUNT + epsilon)
    old_out = jnp.zeros((1, WIDTH), F32)
    new_out = jnp.zeros((1, WIDTH), F32)
    for i, (weights, block) in enumerate(zip(held, blocks)):
        old = weights[...].astype(F32)
        moved = old - rate * block[:PART].astype(F32)
        old_in, moved_in = old[: 2 * UNITS], moved[: 2 * UNITS]
        ratio_in = jnp.sqrt(jnp.sum(old_in * old_in, 1, keepdims=True)) / jnp.sqrt(
            jnp.sum(moved_in * moved_in, 1, keepdims=True) + epsilon
        )
        fresh = (moved_in * ratio_in).astype(BF16)
        spare[0, i * UNITS : (i + 1) * UNITS] = fresh[:UNITS]
        spare[1, i * UNITS : (i + 1) * UNITS] = fresh[UNITS:]
        old_down, moved_down = old[2 * UNITS :], moved[2 * UNITS :]
        old_out += jnp.sum(old_down * old_down, 0, keepdims=True)
        new_out += jnp.sum(moved_down * moved_down, 0, keepdims=True)
    ratio_out = jnp.sqrt(old_out) / jnp.sqrt(new_out + epsilon)
    for i, (weights, block) in enumerate(zip(held, blocks)):
        old = weights[2 * UNITS :].astype(F32)
        moved = old - rate * block[2 * UNITS : PART].astype(F32)
        spare[2, i * UNITS : (i + 1) * UNITS] = (moved * ratio_out).astype(BF16)
    out[0] = one[...]
    out[1] = respond(queries[1], own_count(valid, 1), spare[0], spare[1], spare[2])


def shifted(value, axis, size, shift):
    return lax.ppermute(value, axis, [(i, (i + shift) % size) for i in range(size)])


def along_x(block):
    return [block] + [shifted(block, "x", NX, shift) for shift in SHIFTS[1:]]


def from_core(near):
    return [shifted(b, "c", 2, 1) for b in near]


def reduce_z(partial):
    got = lax.all_to_all(partial.reshape(NZ, PADDED // NZ, WIDTH), "z", 0, 0, tiled=True)
    return kernel_call(summed, shape(*got.shape), [VMEM])(got)


def gather_z(shards):
    return lax.all_to_all(shards, "z", 0, 0, tiled=True).reshape(PADDED, WIDTH)


def under_z(partial, block, count):
    near = along_x(block)
    shards, *near[:3] = lax.optimization_barrier((reduce_z(partial), *near[:3]))
    far = from_core(near[:count])
    total, near[3], far = lax.optimization_barrier((gather_z(shards), near[3], far))
    return total, near + far + from_core(near[count:])


def body(queries, key_vectors, value_vectors, step_sizes, valid_rows, fast_init):
    queries = queries[:, 0]
    held_inputs = (valid_rows, key_vectors[:, 0], value_vectors[:, 0], step_sizes, fast_init[0])
    inputs = [pltpu.with_memory_space_constraint(i, pltpu.HBM) for i in held_inputs]
    pair, padded = shape(2, ROWS, WIDTH), shape(PADDED, WIDTH)
    scratch = [
        pltpu.SMEM(valid_rows.shape, jnp.int32),
        pltpu.VMEM((ROWS, WIDTH), BF16),
        pltpu.VMEM((1, ROWS), F32),
        pltpu.SemaphoreType.DMA((4,)),
    ]
    first = kernel_call(prepare_first, pair, [HBM] * 4, scratch)(*inputs[:4])
    other = shifted(first, "c", 2, 1)
    weights = kernel_call(
        half_weights,
        shape(3, HALF, WIDTH),
        [HBM],
        [pltpu.VMEM((WIDTH, 384), BF16)] * 2 + [pltpu.SemaphoreType.DMA((6,))],
    )(inputs[4])
    parts = kernel_call(first_partial, (shape(PART, WIDTH),) * NX, [VMEM] * 3)(
        weights, first, other
    )
    parts = [parts[0]] + [shifted(p, "x", NX, s) for p, s in zip(parts[1:], SHIFTS[1:])]
    second = kernel_call(prepare_second, pair, [HBM] * 4, scratch)(*inputs[:4])
    *parts, second = lax.optimization_barrier((*parts, second))
    partial = kernel_call(summed_x, padded, [VMEM] * NX)(*parts)
    gradient, tokens = under_z(partial, second, 0)
    stats = kernel_call(statistics, shape(2 * NX, 8, WIDTH, dtype=F32), [VMEM] * 2)(
        weights, gradient
    )
    stats = lax.all_to_all(stats, ("x", "c"), 0, 0, tiled=True)
    fresh, partial = kernel_call(second_partial, (shape(PART, WIDTH), padded), [VMEM] * 11)(
        weights, gradient, stats, *tokens
    )
    gradient, held = under_z(partial, fresh, 3)
    near = along_x(gradient)
    one = kernel_call(first_answer, shape(ROWS, WIDTH), [SMEM] + [VMEM] * 9)(
        valid_rows, queries, *held
    )
    near[3], one = lax.optimization_barrier((near[3], one))
    out = kernel_call(
        second_answer,
        shape(2, ROWS, WIDTH),
        [SMEM] + [VMEM] * 18,
        [pltpu.VMEM((3, WIDTH, WIDTH), BF16)],
    )(valid_rows, queries, one, *held, *near, *from_core(near))
    return out[:, None]


def solution(mesh):
    split = Mesh(mesh.devices.reshape(mesh.shape["head"], NZ, NX, 2), ("head", "z", "x", "c"))
    seq = ("z", "x", "c")
    rows = P(None, "head", seq, None)
    placed = (rows, rows, rows, P(None, "head", seq), P(), P("head", None, None))
    return jax.shard_map(body, mesh=split, in_specs=placed, out_specs=rows, check_vma=False)
```

```python
import jax
import jax.numpy as jnp
from jax import lax
from jax.experimental import pallas as pl
from jax.experimental.pallas import tpu as pltpu
from jax.sharding import Mesh
from jax.sharding import PartitionSpec as P

step_factor = 0.5
epsilon = 1e-06
NX = 4
NZ = 8
ROWS = 128
WIDTH = 640
UNITS = 80
HALF = NX * UNITS
SHIFTS = (0, 1, 3, 2)
EARLY = (0, 3, 4)
PART = 3 * UNITS
PADDED = 256
RATE = step_factor / WIDTH**0.5
COUNT = 3 * WIDTH * WIDTH
F32 = jnp.float32
BF16 = jnp.bfloat16
VMEM = pl.BlockSpec(memory_space=pltpu.VMEM)
SMEM = pl.BlockSpec(memory_space=pltpu.SMEM)
HBM = pl.BlockSpec(memory_space=pltpu.HBM)


def dot(a, b, ca=1, cb=0):
    return lax.dot_general(a, b, (((ca,), (cb,)), ((), ())), preferred_element_type=F32)


def shape(*dims, dtype=BF16):
    return jax.ShapeDtypeStruct(dims, dtype)


def kernel_call(body, outs, ins, scratch=()):
    return pl.pallas_call(
        body,
        out_shape=outs,
        in_specs=ins,
        out_specs=jax.tree.map(lambda o: HBM if isinstance(o, pl.MemoryRef) else VMEM, outs),
        scratch_shapes=list(scratch),
        compiler_params=pltpu.CompilerParams(vmem_limit_bytes=20 * 1024 * 1024),
    )


def own_count(valid, group):
    rank = (lax.axis_index("z") * NX + lax.axis_index("x")) * 2 + lax.axis_index("c")
    return valid[group, rank]


def fetch(pairs, sems):
    copies = [pltpu.make_async_copy(src, dst, sems.at[i]) for i, (src, dst) in enumerate(pairs)]
    for copy in copies:
        copy.start()
    for copy in copies:
        copy.wait()


def write_grads(live_rows, sizes, values, out):
    row = lax.broadcasted_iota(jnp.int32, (ROWS, ROWS), 0)
    col = lax.broadcasted_iota(jnp.int32, (ROWS, ROWS), 1)
    size = jnp.sum(jnp.where(row == col, sizes[...], 0.0), 1, keepdims=True)
    scaled = jnp.where(row[:, :1] < live_rows, size, 0.0)
    out[1] = (-(scaled * values[...].astype(F32))).astype(BF16)


def prepare_first(valid, keys, values, sizes, out, valid_s, value_s, size_s, sems):
    pairs = [
        (keys.at[0], out.at[0]),
        (values.at[0], value_s),
        (sizes.at[0], size_s),
        (valid, valid_s),
    ]
    fetch(pairs, sems)
    write_grads(own_count(valid_s, 0), size_s, value_s, out)


def prepare_second(valid, keys, values, sizes, out, valid_s, value_s, size_s, sems):
    pairs = [
        (keys.at[1], out.at[0]),
        (values.at[1], value_s),
        (sizes.at[1], size_s),
        (valid, valid_s),
    ]
    fetch(pairs, sems)
    write_grads(own_count(valid_s, 1), size_s, value_s, out)


def half_weights(fast, weights, own, gate_s, up_s, sems):
    x, c = lax.axis_index("x"), lax.axis_index("c")
    start = c * HALF
    edge = pl.multiple_of(c * 256, 128)
    pairs = [
        (fast.at[:, pl.ds(edge, 384)], gate_s),
        (fast.at[:, pl.ds(WIDTH + edge, 384)], up_s),
    ]
    row = lax.broadcasted_iota(jnp.int32, (HALF, 384), 0)
    col = lax.broadcasted_iota(jnp.int32, (HALF, 384), 1)
    wanted = row
    for i, shift in enumerate(SHIFTS):
        block = lax.rem(x + shift, NX)
        first = pl.multiple_of(start + block * UNITS, UNITS)
        source = fast.at[pl.ds(first, UNITS), pl.ds(2 * WIDTH, WIDTH)]
        pairs.append((source, weights.at[2, pl.ds(i * UNITS, UNITS)]))
        inside = (row >= i * UNITS) & (row < (i + 1) * UNITS)
        wanted = jnp.where(inside, first - edge + row - i * UNITS, wanted)
    chosen = jnp.where(col == wanted, 1.0, 0.0).astype(BF16)
    fetch(pairs, sems)
    for i, window in enumerate((gate_s, up_s)):
        weights[i] = dot(chosen, window[...], 1, 1).astype(BF16)
    for i in range(3):
        own[i * UNITS : (i + 1) * UNITS] = weights[i, :UNITS]


def gradients(into, down, keys, grads):
    units = down.shape[0]
    pre = dot(into, keys, 1, 1)
    gate, up = pre[:units], pre[units:]
    d_hidden = dot(down, grads, 1, 1)
    sig = jax.nn.sigmoid(gate)
    hidden = (gate * sig * up).astype(BF16)
    d_up = (d_hidden * gate * sig).astype(BF16)
    d_gate = (d_hidden * up * sig * (1.0 + gate * (1.0 - sig))).astype(BF16)
    inner = dot(jnp.concatenate([d_gate, d_up], 0), keys).astype(BF16)
    return inner, dot(hidden, grads).astype(BF16)


def first_partial(weights, own, other, *outs):
    keys = jnp.concatenate([own[0], other[0]], 0)
    grads = jnp.concatenate([own[1], other[1]], 0)
    into = jnp.concatenate([weights[0], weights[1]], 0)
    inner, outer = gradients(into, weights[2], keys, grads)
    for i, out in enumerate(outs):
        rows = slice(i * UNITS, (i + 1) * UNITS)
        out[0:UNITS] = inner[rows]
        out[UNITS : 2 * UNITS] = inner[HALF:][rows]
        out[2 * UNITS :] = outer[rows]


def summed_x(*refs):
    blocks, (out, total_s, sems) = refs[:NX], refs[NX:]
    copies = []
    for i in range(2):
        rows = slice(i * PADDED // 2, (i + 1) * PADDED // 2)
        used = slice(rows.start, min(rows.stop, PART))
        total = blocks[0][used].astype(F32)
        for block in blocks[1:]:
            total += block[used].astype(F32)
        total_s[used] = total.astype(BF16)
        if rows.stop > PART:
            total_s[PART:] = jnp.zeros((PADDED - PART, WIDTH), BF16)
        copies.append(pltpu.make_async_copy(total_s.at[rows], out.at[rows], sems.at[i]))
        copies[-1].start()
    for copy in copies:
        copy.wait()


def to_all(source, out, sems):
    fetch([(source, out.at[i]) for i in range(out.shape[0])], sems)


def summed(got, out, total_s, sems):
    total = got[0].astype(F32)
    for i in range(1, NZ):
        total += got[i].astype(F32)
    total_s[...] = total.astype(BF16)
    to_all(total_s, out, sems)


def statistics(weights, gradient, out, lines_s, sems):
    grad = gradient[...].astype(F32)
    old = weights[2 * UNITS :].astype(F32)
    down = grad[2 * UNITS : PART]
    lines = [old * old, old * down, down * down, grad * grad]
    lines = [jnp.sum(line, 0, keepdims=True) for line in lines]
    lines_s[...] = jnp.concatenate(lines + [jnp.zeros((4, WIDTH), F32)], 0)
    to_all(lines_s, out, sems)


def rate_of(squares):
    return RATE / jnp.sqrt(jnp.sum(squares, 1, keepdims=True) / COUNT + epsilon)


def ratio_of(rate, old, cross, grad):
    moved = jnp.maximum(old - 2.0 * rate * cross + rate * rate * grad, 0.0)
    return jnp.sqrt(old) / jnp.sqrt(moved + epsilon)


def second_partial(weights, gradient, stats, *refs):
    blocks, (fresh, out, partial_s, sems) = refs[: 2 * NX], refs[2 * NX :]
    total = stats[0]
    for i in range(1, 2 * NX):
        total += stats[i]
    rate = rate_of(total[3:4])
    old = weights[...].astype(F32)
    moved = old - rate * gradient[:PART].astype(F32)
    old_in, moved_in = old[: 2 * UNITS], moved[: 2 * UNITS]
    ratio_in = jnp.sqrt(jnp.sum(old_in * old_in, 1, keepdims=True)) / jnp.sqrt(
        jnp.sum(moved_in * moved_in, 1, keepdims=True) + epsilon
    )
    ratio_out = ratio_of(rate, total[0:1], total[1:2], total[2:3])
    new = jnp.concatenate([moved_in * ratio_in, moved[2 * UNITS :] * ratio_out], 0).astype(BF16)
    fresh[...] = new
    keys = jnp.concatenate([b[0] for b in blocks], 0)
    grads = jnp.concatenate([b[1] for b in blocks], 0)
    inner, outer = gradients(new[: 2 * UNITS], new[2 * UNITS :], keys, grads)
    partial_s[0 : 2 * UNITS] = inner
    partial_s[2 * UNITS : PART] = outer
    partial_s[PART:] = jnp.zeros((PADDED - PART, WIDTH), BF16)
    fetch([(partial_s, out)], sems)


def respond(rows, live_rows, gate_w, up_w, down_w):
    gate = dot(rows, gate_w, 1, 1)
    up = dot(rows, up_w, 1, 1)
    hidden = (gate * jax.nn.sigmoid(gate) * up).astype(BF16)
    result = dot(hidden, down_w).astype(BF16)
    live = lax.broadcasted_iota(jnp.int32, result.shape, 0) < live_rows
    return jnp.where(live, result, jnp.zeros_like(result))


def first_answer(valid, queries, *refs):
    blocks, out = refs[:-1], refs[-1]
    parts = [
        jnp.concatenate([b[i * UNITS : (i + 1) * UNITS] for b in blocks], 0) for i in range(3)
    ]
    out[...] = respond(queries[0], own_count(valid, 0), *parts)


def sums(weights, gradient, inner, lines):
    old, grad = weights[...].astype(F32), gradient[:PART].astype(F32)
    products = [old * old, old * grad, grad * grad]
    squares = jnp.sum(products[2], 0, keepdims=True)
    for i, product in enumerate(products):
        inner[i] = jnp.sum(product[: 2 * UNITS], 1, keepdims=True)
        lines[i] = jnp.sum(product[2 * UNITS :], 0, keepdims=True)
    lines[3] = squares


def digest(*refs):
    count = len(EARLY)
    inner, lines = refs[2 * count :]
    for i in range(count):
        sums(refs[i], refs[count + i], inner.at[i], lines.at[i])


def second_answer(valid, queries, one, early_in, early_lines, *refs):
    held, blocks = refs[:8], refs[8:16]
    out, spare, late_in, late_lines = refs[16:]
    where = {}
    late = [i for i in range(8) if i not in EARLY]
    for i, block in enumerate(EARLY):
        where[block] = early_in.at[i], early_lines.at[i]
    for i, block in enumerate(late):
        where[block] = late_in.at[i], late_lines.at[i]
        sums(held[block], blocks[block], *where[block])
    lines = [sum(where[i][1][k] for i in range(8)) for k in range(4)]
    rate = rate_of(lines[3])
    ratio_out = ratio_of(rate, *lines[:3])
    for i, (weights, block) in enumerate(zip(held, blocks)):
        moved = weights[...].astype(F32) - rate * block[:PART].astype(F32)
        inner = where[i][0]
        fresh = (moved[: 2 * UNITS] * ratio_of(rate, inner[0], inner[1], inner[2])).astype(BF16)
        spare[0, i * UNITS : (i + 1) * UNITS] = fresh[:UNITS]
        spare[1, i * UNITS : (i + 1) * UNITS] = fresh[UNITS:]
        spare[2, i * UNITS : (i + 1) * UNITS] = (moved[2 * UNITS :] * ratio_out).astype(BF16)
    out[0] = one[...]
    out[1] = respond(queries[1], own_count(valid, 1), spare[0], spare[1], spare[2])


def shifted(value, axis, size, shift):
    return lax.ppermute(value, axis, [(i, (i + shift) % size) for i in range(size)])


def along_x(block):
    return [block] + [shifted(block, "x", NX, shift) for shift in SHIFTS[1:]]


def from_core(near):
    return [shifted(b, "c", 2, 1) for b in near]


def reduce_z(partial):
    got = lax.all_to_all(partial.reshape(NZ, PADDED // NZ, WIDTH), "z", 0, 0, tiled=True)
    scratch = [pltpu.VMEM(got.shape[1:], BF16), pltpu.SemaphoreType.DMA((NZ,))]
    return kernel_call(summed, pltpu.HBM(got.shape, BF16), [VMEM], scratch)(got)


def gather_z(shards):
    return lax.all_to_all(shards, "z", 0, 0, tiled=True).reshape(PADDED, WIDTH)


def under_z(partial, block, count):
    near = along_x(block)
    shards, *near[:3] = lax.optimization_barrier((reduce_z(partial), *near[:3]))
    far = from_core(near[:count])
    total, near[3], far = lax.optimization_barrier((gather_z(shards), near[3], far))
    return total, near + far + from_core(near[count:])


def body(queries, key_vectors, value_vectors, step_sizes, valid_rows, fast_init):
    queries = queries[:, 0]
    held_inputs = (valid_rows, key_vectors[:, 0], value_vectors[:, 0], step_sizes, fast_init[0])
    inputs = [pltpu.with_memory_space_constraint(i, pltpu.HBM) for i in held_inputs]
    pair, padded = shape(2, ROWS, WIDTH), pltpu.HBM((PADDED, WIDTH), BF16)
    padded_s = pltpu.VMEM((PADDED, WIDTH), BF16)
    scratch = [
        pltpu.SMEM(valid_rows.shape, jnp.int32),
        pltpu.VMEM((ROWS, WIDTH), BF16),
        pltpu.VMEM((1, ROWS), F32),
        pltpu.SemaphoreType.DMA((4,)),
    ]
    first = kernel_call(prepare_first, pair, [HBM] * 4, scratch)(*inputs[:4])
    other = shifted(first, "c", 2, 1)
    weights, own = kernel_call(
        half_weights,
        (shape(3, HALF, WIDTH), shape(PART, WIDTH)),
        [HBM],
        [pltpu.VMEM((WIDTH, 384), BF16)] * 2 + [pltpu.SemaphoreType.DMA((6,))],
    )(inputs[4])
    parts = kernel_call(first_partial, (shape(PART, WIDTH),) * NX, [VMEM] * 3)(
        weights, first, other
    )
    parts = [parts[0]] + [shifted(p, "x", NX, s) for p, s in zip(parts[1:], SHIFTS[1:])]
    second = kernel_call(prepare_second, pair, [HBM] * 4, scratch)(*inputs[:4])
    *parts, second = lax.optimization_barrier((*parts, second))
    partial = kernel_call(
        summed_x, padded, [VMEM] * NX, [padded_s, pltpu.SemaphoreType.DMA((2,))]
    )(*parts)
    gradient, tokens = under_z(partial, second, 0)
    stats = kernel_call(
        statistics,
        pltpu.HBM((2 * NX, 8, WIDTH), F32),
        [VMEM] * 2,
        [pltpu.VMEM((8, WIDTH), F32), pltpu.SemaphoreType.DMA((2 * NX,))],
    )(own, gradient)
    stats = lax.all_to_all(stats, ("x", "c"), 0, 0, tiled=True)
    fresh, partial = kernel_call(
        second_partial,
        (shape(PART, WIDTH), padded),
        [VMEM] * 11,
        [padded_s, pltpu.SemaphoreType.DMA((1,))],
    )(own, gradient, stats, *tokens)
    gradient, held = under_z(partial, fresh, 3)
    near = along_x(gradient)
    one = kernel_call(first_answer, shape(ROWS, WIDTH), [SMEM] + [VMEM] * 9)(
        valid_rows, queries, *held
    )
    far = from_core(near[:1])
    near[3], one = lax.optimization_barrier((near[3], one))
    last = from_core(near[3:])
    early = [near[0], near[3], far[0]]
    found = kernel_call(
        digest,
        (shape(3, 3, 2 * UNITS, 1, dtype=F32), shape(3, 4, 1, WIDTH, dtype=F32)),
        [VMEM] * 6,
    )(*[held[i] for i in EARLY], *early)
    *near[1:3], found, last = lax.optimization_barrier((*near[1:3], found, last))
    far += from_core(near[1:3]) + last
    out = kernel_call(
        second_answer,
        shape(2, ROWS, WIDTH),
        [SMEM] + [VMEM] * 20,
        [
            pltpu.VMEM((3, WIDTH, WIDTH), BF16),
            pltpu.VMEM((5, 3, 2 * UNITS, 1), F32),
            pltpu.VMEM((5, 4, 1, WIDTH), F32),
        ],
    )(valid_rows, queries, one, *found, *held, *near, *far)
    return out[:, None]


def solution(mesh):
    split = Mesh(mesh.devices.reshape(mesh.shape["head"], NZ, NX, 2), ("head", "z", "x", "c"))
    seq = ("z", "x", "c")
    rows = P(None, "head", seq, None)
    placed = (rows, rows, rows, P(None, "head", seq), P(), P("head", None, None))
    return jax.shard_map(body, mesh=split, in_specs=placed, out_specs=rows, check_vma=False)
```

```python
import jax
import jax.numpy as jnp
from jax import lax
from jax.experimental import pallas as pl
from jax.experimental.pallas import tpu as pltpu
from jax.sharding import Mesh
from jax.sharding import PartitionSpec as P

step_factor = 0.5
epsilon = 1e-06
NX = 4
NZ = 8
ROWS = 128
WIDTH = 640
UNITS = 80
HALF = NX * UNITS
SHIFTS = (0, 1, 3, 2)
PART = 3 * UNITS
PADDED = 256
RATE = step_factor / WIDTH**0.5
COUNT = 3 * WIDTH * WIDTH
F32 = jnp.float32
BF16 = jnp.bfloat16
VMEM = pl.BlockSpec(memory_space=pltpu.VMEM)
SMEM = pl.BlockSpec(memory_space=pltpu.SMEM)
HBM = pl.BlockSpec(memory_space=pltpu.HBM)


def dot(a, b, ca=1, cb=0):
    return lax.dot_general(a, b, (((ca,), (cb,)), ((), ())), preferred_element_type=F32)


def shape(*dims, dtype=BF16):
    return jax.ShapeDtypeStruct(dims, dtype)


def kernel_call(body, outs, ins, scratch=()):
    return pl.pallas_call(
        body,
        out_shape=outs,
        in_specs=ins,
        out_specs=jax.tree.map(lambda _: VMEM, outs),
        scratch_shapes=list(scratch),
        compiler_params=pltpu.CompilerParams(vmem_limit_bytes=20 * 1024 * 1024),
    )


def own_count(valid, group):
    rank = (lax.axis_index("z") * NX + lax.axis_index("x")) * 2 + lax.axis_index("c")
    return valid[group, rank]


def fetch(pairs, sems):
    copies = [pltpu.make_async_copy(src, dst, sems.at[i]) for i, (src, dst) in enumerate(pairs)]
    for copy in copies:
        copy.start()
    for copy in copies:
        copy.wait()


def write_grads(live_rows, sizes, values, out):
    row = lax.broadcasted_iota(jnp.int32, (ROWS, ROWS), 0)
    col = lax.broadcasted_iota(jnp.int32, (ROWS, ROWS), 1)
    size = jnp.sum(jnp.where(row == col, sizes[...], 0.0), 1, keepdims=True)
    scaled = jnp.where(row[:, :1] < live_rows, size, 0.0)
    out[1] = (-(scaled * values[...].astype(F32))).astype(BF16)


def prepare_first(valid, keys, values, sizes, out, valid_s, value_s, size_s, sems):
    pairs = [
        (keys.at[0], out.at[0]),
        (values.at[0], value_s),
        (sizes.at[0], size_s),
        (valid, valid_s),
    ]
    fetch(pairs, sems)
    write_grads(own_count(valid_s, 0), size_s, value_s, out)


def prepare_second(valid, keys, values, sizes, out, valid_s, value_s, size_s, sems):
    pairs = [
        (keys.at[1], out.at[0]),
        (values.at[1], value_s),
        (sizes.at[1], size_s),
        (valid, valid_s),
    ]
    fetch(pairs, sems)
    write_grads(own_count(valid_s, 1), size_s, value_s, out)


def half_weights(fast, weights, own, gate_s, up_s, sems):
    x, c = lax.axis_index("x"), lax.axis_index("c")
    start = c * HALF
    edge = pl.multiple_of(c * 256, 128)
    pairs = [
        (fast.at[:, pl.ds(edge, 384)], gate_s),
        (fast.at[:, pl.ds(WIDTH + edge, 384)], up_s),
    ]
    row = lax.broadcasted_iota(jnp.int32, (HALF, 384), 0)
    col = lax.broadcasted_iota(jnp.int32, (HALF, 384), 1)
    wanted = row
    for i, shift in enumerate(SHIFTS):
        block = lax.rem(x + shift, NX)
        first = pl.multiple_of(start + block * UNITS, UNITS)
        source = fast.at[pl.ds(first, UNITS), pl.ds(2 * WIDTH, WIDTH)]
        pairs.append((source, weights.at[2, pl.ds(i * UNITS, UNITS)]))
        inside = (row >= i * UNITS) & (row < (i + 1) * UNITS)
        wanted = jnp.where(inside, first - edge + row - i * UNITS, wanted)
    chosen = jnp.where(col == wanted, 1.0, 0.0).astype(BF16)
    fetch(pairs, sems)
    for i, window in enumerate((gate_s, up_s)):
        weights[i] = dot(chosen, window[...], 1, 1).astype(BF16)
    for i in range(3):
        own[i * UNITS : (i + 1) * UNITS] = weights[i, :UNITS]


def gradients(into, down, keys, grads):
    units = down.shape[0]
    pre = dot(into, keys, 1, 1)
    gate, up = pre[:units], pre[units:]
    d_hidden = dot(down, grads, 1, 1)
    sig = jax.nn.sigmoid(gate)
    hidden = (gate * sig * up).astype(BF16)
    d_up = (d_hidden * gate * sig).astype(BF16)
    d_gate = (d_hidden * up * sig * (1.0 + gate * (1.0 - sig))).astype(BF16)
    inner = dot(jnp.concatenate([d_gate, d_up], 0), keys).astype(BF16)
    return inner, dot(hidden, grads).astype(BF16)


def first_partial(weights, own, other, *outs):
    keys = jnp.concatenate([own[0], other[0]], 0)
    grads = jnp.concatenate([own[1], other[1]], 0)
    into = jnp.concatenate([weights[0], weights[1]], 0)
    inner, outer = gradients(into, weights[2], keys, grads)
    for i, out in enumerate(outs):
        rows = slice(i * UNITS, (i + 1) * UNITS)
        out[0:UNITS] = inner[rows]
        out[UNITS : 2 * UNITS] = inner[HALF:][rows]
        out[2 * UNITS :] = outer[rows]


def summed_x(*refs):
    blocks, out = refs[:-1], refs[-1]
    total = blocks[0][...].astype(F32)
    for block in blocks[1:]:
        total += block[...].astype(F32)
    out[0:PART] = total.astype(BF16)
    out[PART:] = jnp.zeros((PADDED - PART, WIDTH), BF16)


def summed(got, out):
    total = got[0].astype(F32)
    for i in range(1, NZ):
        total += got[i].astype(F32)
    total = total.astype(BF16)
    for i in range(NZ):
        out[i] = total


def statistics(weights, gradient, out):
    grad = gradient[...].astype(F32)
    old = weights[2 * UNITS :].astype(F32)
    down = grad[2 * UNITS : PART]
    squares = jnp.sum(grad * grad, 0, keepdims=True)
    lines = [
        jnp.sum(old * old, 0, keepdims=True),
        jnp.sum(old * down, 0, keepdims=True),
        jnp.sum(down * down, 0, keepdims=True),
        squares,
    ]
    lines = jnp.concatenate(lines + [jnp.zeros((4, WIDTH), F32)], 0)
    for i in range(2 * NX):
        out[i] = lines


def second_partial(weights, gradient, stats, *refs):
    blocks, fresh, out = refs[:-2], refs[-2], refs[-1]
    total = stats[0]
    for i in range(1, 2 * NX):
        total += stats[i]
    rate = rate_of(total[3:4])
    old = weights[...].astype(F32)
    moved = old - rate * gradient[:PART].astype(F32)
    old_in, moved_in = old[: 2 * UNITS], moved[: 2 * UNITS]
    ratio_in = jnp.sqrt(jnp.sum(old_in * old_in, 1, keepdims=True)) / jnp.sqrt(
        jnp.sum(moved_in * moved_in, 1, keepdims=True) + epsilon
    )
    ratio_out = ratio_of(rate, total[0:1], total[1:2], total[2:3])
    new = jnp.concatenate([moved_in * ratio_in, moved[2 * UNITS :] * ratio_out], 0).astype(BF16)
    fresh[...] = new
    keys = jnp.concatenate([b[0] for b in blocks], 0)
    grads = jnp.concatenate([b[1] for b in blocks], 0)
    inner, outer = gradients(new[: 2 * UNITS], new[2 * UNITS :], keys, grads)
    out[0 : 2 * UNITS] = inner
    out[2 * UNITS : PART] = outer
    out[PART:] = jnp.zeros((PADDED - PART, WIDTH), BF16)


def rate_of(squares):
    return RATE / jnp.sqrt(jnp.sum(squares, 1, keepdims=True) / COUNT + epsilon)


def ratio_of(rate, old, cross, grad):
    moved = jnp.maximum(old - 2.0 * rate * cross + rate * rate * grad, 0.0)
    return jnp.sqrt(old) / jnp.sqrt(moved + epsilon)


def respond(group, queries, others, into, down, mine, theirs):
    rows = jnp.concatenate([queries[group], others[group]], 0)
    pre = dot(rows, into, 1, 1)
    gate, up = pre[:, :HALF], pre[:, HALF:]
    hidden = (gate * jax.nn.sigmoid(gate) * up).astype(BF16)
    result = dot(hidden, down)
    mine[...] = result[:ROWS]
    theirs[...] = result[ROWS:].astype(BF16)


def first_answer(queries, others, *refs):
    blocks, (mine, theirs) = refs[:NX], refs[NX:]
    parts = [
        jnp.concatenate([b[i * UNITS : (i + 1) * UNITS] for b in blocks], 0) for i in range(3)
    ]
    respond(0, queries, others, jnp.concatenate(parts[:2], 0), parts[2], mine, theirs)


def sums(weights, gradient, inner):
    old, grad = weights[...].astype(F32), gradient[:PART].astype(F32)
    products = [old * old, old * grad, grad * grad]
    for i, product in enumerate(products):
        inner[i] = jnp.sum(product[: 2 * UNITS], 1, keepdims=True)
    lines = [jnp.sum(p[2 * UNITS :], 0, keepdims=True) for p in products]
    return jnp.concatenate(lines + [jnp.sum(products[2], 0, keepdims=True)], 0)


def early_sums(*refs):
    held, blocks, (inner, lines) = refs[:2], refs[2:4], refs[4:]
    lines[0:4] = sum(sums(held[i], blocks[i], inner.at[i]) for i in range(2))
    lines[4:] = jnp.zeros((4, WIDTH), F32)


def late_sums(early, *refs):
    held, blocks, (inner, lines) = refs[:2], refs[2:4], refs[4:]
    lines[0:4] = early[0:4] + sum(sums(held[i], blocks[i], inner.at[i]) for i in range(2))
    lines[4:] = jnp.zeros((4, WIDTH), F32)


def second_answer(queries, others, own_lines, other_lines, early_in, late_in, *refs):
    held, blocks, (mine, theirs, into, down) = refs[:NX], refs[NX : 2 * NX], refs[2 * NX :]
    lines = own_lines[...] + other_lines[...]
    rate = rate_of(lines[3:4])
    ratio_out = ratio_of(rate, lines[0:1], lines[1:2], lines[2:3])
    inner = [early_in.at[0], late_in.at[0], late_in.at[1], early_in.at[1]]
    for i, (weights, block) in enumerate(zip(held, blocks)):
        moved = weights[...].astype(F32) - rate * block[:PART].astype(F32)
        ratio_in = ratio_of(rate, inner[i][0], inner[i][1], inner[i][2])
        fresh = (moved[: 2 * UNITS] * ratio_in).astype(BF16)
        into[i * UNITS : (i + 1) * UNITS] = fresh[:UNITS]
        into[HALF + i * UNITS : HALF + (i + 1) * UNITS] = fresh[UNITS:]
        down[i * UNITS : (i + 1) * UNITS] = (moved[2 * UNITS :] * ratio_out).astype(BF16)
    respond(1, queries, others, into[...], down[...], mine, theirs)


def joined(valid, *refs):
    parts, out = refs[:4], refs[4]
    row = lax.broadcasted_iota(jnp.int32, (ROWS, WIDTH), 0)
    for group in range(2):
        result = parts[group][...] + parts[2 + group][...].astype(F32)
        out[group] = jnp.where(row < own_count(valid, group), result, 0.0).astype(BF16)


def shifted(value, axis, size, shift):
    return lax.ppermute(value, axis, [(i, (i + shift) % size) for i in range(size)])


def along_x(block):
    return [block] + [shifted(block, "x", NX, shift) for shift in SHIFTS[1:]]


def from_core(near):
    return [shifted(b, "c", 2, 1) for b in near]


def reduce_z(partial):
    got = lax.all_to_all(partial.reshape(NZ, PADDED // NZ, WIDTH), "z", 0, 0, tiled=True)
    return kernel_call(summed, shape(*got.shape), [VMEM])(got)


def gather_z(shards):
    return lax.all_to_all(shards, "z", 0, 0, tiled=True).reshape(PADDED, WIDTH)


def under_z(partial, block, *more):
    near = along_x(block)
    shards, near[:3], more = lax.optimization_barrier((reduce_z(partial), near[:3], more))
    total, near[3] = lax.optimization_barrier((gather_z(shards), near[3]))
    return total, near, *more


def body(queries, key_vectors, value_vectors, step_sizes, valid_rows, fast_init):
    queries = queries[:, 0]
    held_inputs = (valid_rows, key_vectors[:, 0], value_vectors[:, 0], step_sizes, fast_init[0])
    inputs = [pltpu.with_memory_space_constraint(i, pltpu.HBM) for i in held_inputs]
    pair, padded = shape(2, ROWS, WIDTH), shape(PADDED, WIDTH)
    scratch = [
        pltpu.SMEM(valid_rows.shape, jnp.int32),
        pltpu.VMEM((ROWS, WIDTH), BF16),
        pltpu.VMEM((1, ROWS), F32),
        pltpu.SemaphoreType.DMA((4,)),
    ]
    first = kernel_call(prepare_first, pair, [HBM] * 4, scratch)(*inputs[:4])
    other = shifted(first, "c", 2, 1)
    weights, own = kernel_call(
        half_weights,
        (shape(3, HALF, WIDTH), shape(PART, WIDTH)),
        [HBM],
        [pltpu.VMEM((WIDTH, 384), BF16)] * 2 + [pltpu.SemaphoreType.DMA((6,))],
    )(inputs[4])
    parts = kernel_call(first_partial, (shape(PART, WIDTH),) * NX, [VMEM] * 3)(
        weights, first, other
    )
    parts = [parts[0]] + [shifted(p, "x", NX, s) for p, s in zip(parts[1:], SHIFTS[1:])]
    second = kernel_call(prepare_second, pair, [HBM] * 4, scratch)(*inputs[:4])
    *parts, second = lax.optimization_barrier((*parts, second))
    partial = kernel_call(summed_x, padded, [VMEM] * NX)(*parts)
    gradient, tokens, others = under_z(partial, second, shifted(queries, "c", 2, 1))
    tokens += from_core(tokens)
    stats = kernel_call(statistics, shape(2 * NX, 8, WIDTH, dtype=F32), [VMEM] * 2)(
        own, gradient
    )
    stats = lax.all_to_all(stats, ("x", "c"), 0, 0, tiled=True)
    fresh, partial = kernel_call(second_partial, (shape(PART, WIDTH), padded), [VMEM] * 11)(
        own, gradient, stats, *tokens
    )
    gradient, held = under_z(partial, fresh)
    near = along_x(gradient)
    share = (shape(ROWS, WIDTH, dtype=F32), shape(ROWS, WIDTH))
    one, theirs = kernel_call(first_answer, share, [VMEM] * 6)(queries, others, *held)
    found = (shape(2, 3, 2 * UNITS, 1, dtype=F32), shape(8, WIDTH, dtype=F32))
    early, lines = kernel_call(early_sums, found, [VMEM] * 4)(held[0], held[3], near[0], near[3])
    other_one = shifted(theirs, "c", 2, 1)
    near[1], near[2], lines, other_one = lax.optimization_barrier(
        (near[1], near[2], lines, other_one)
    )
    late, lines = kernel_call(late_sums, found, [VMEM] * 5)(lines, *held[1:3], *near[1:3])
    two, theirs = kernel_call(
        second_answer,
        share,
        [VMEM] * 14,
        [pltpu.VMEM((WIDTH, WIDTH), BF16), pltpu.VMEM((HALF, WIDTH), BF16)],
    )(queries, others, lines, shifted(lines, "c", 2, 1), early, late, *held, *near)
    other_two = shifted(theirs, "c", 2, 1)
    out = kernel_call(joined, shape(2, ROWS, WIDTH), [SMEM] + [VMEM] * 4)(
        valid_rows, one, two, other_one, other_two
    )
    return out[:, None]


def solution(mesh):
    split = Mesh(mesh.devices.reshape(mesh.shape["head"], NZ, NX, 2), ("head", "z", "x", "c"))
    seq = ("z", "x", "c")
    rows = P(None, "head", seq, None)
    placed = (rows, rows, rows, P(None, "head", seq), P(), P("head", None, None))
    return jax.shard_map(body, mesh=split, in_specs=placed, out_specs=rows, check_vma=False)
```

```python
import jax
import jax.numpy as jnp
from jax import lax
from jax.experimental import pallas as pl
from jax.experimental.pallas import tpu as pltpu
from jax.sharding import Mesh
from jax.sharding import PartitionSpec as P

step_factor = 0.5
epsilon = 1e-06
NX = 4
NZ = 8
ROWS = 128
WIDTH = 640
UNITS = 80
HALF = NX * UNITS
SHIFTS = (0, 1, 3, 2)
PART = 3 * UNITS
PADDED = 256
RATE = step_factor / WIDTH**0.5
COUNT = 3 * WIDTH * WIDTH
F32 = jnp.float32
BF16 = jnp.bfloat16
VMEM = pl.BlockSpec(memory_space=pltpu.VMEM)
HBM = pl.BlockSpec(memory_space=pltpu.HBM)


def dot(a, b, ca=1, cb=0):
    return lax.dot_general(a, b, (((ca,), (cb,)), ((), ())), preferred_element_type=F32)


def shape(*dims, dtype=BF16):
    return jax.ShapeDtypeStruct(dims, dtype)


def kernel_call(body, outs, ins, scratch=()):
    return pl.pallas_call(
        body,
        out_shape=outs,
        in_specs=ins,
        out_specs=jax.tree.map(lambda _: VMEM, outs),
        scratch_shapes=list(scratch),
        compiler_params=pltpu.CompilerParams(vmem_limit_bytes=20 * 1024 * 1024),
    )


def own_count(valid, group):
    rank = (lax.axis_index("z") * NX + lax.axis_index("x")) * 2 + lax.axis_index("c")
    return valid[group, rank]


def fetch(pairs, sems):
    copies = [pltpu.make_async_copy(src, dst, sems.at[i]) for i, (src, dst) in enumerate(pairs)]
    for copy in copies:
        copy.start()
    for copy in copies:
        copy.wait()


def write_grads(live_rows, sizes, values, out):
    row = lax.broadcasted_iota(jnp.int32, (ROWS, ROWS), 0)
    col = lax.broadcasted_iota(jnp.int32, (ROWS, ROWS), 1)
    size = jnp.sum(jnp.where(row == col, sizes[...], 0.0), 1, keepdims=True)
    scaled = jnp.where(row[:, :1] < live_rows, size, 0.0)
    out[1] = (-(scaled * values[...].astype(F32))).astype(BF16)


def prepare_first(valid, keys, values, sizes, out, valid_s, value_s, size_s, sems):
    pairs = [
        (keys.at[0], out.at[0]),
        (values.at[0], value_s),
        (sizes.at[0], size_s),
        (valid, valid_s),
    ]
    fetch(pairs, sems)
    write_grads(own_count(valid_s, 0), size_s, value_s, out)


def prepare_second(valid, keys, values, sizes, out, valid_s, value_s, size_s, sems):
    pairs = [
        (keys.at[1], out.at[0]),
        (values.at[1], value_s),
        (sizes.at[1], size_s),
        (valid, valid_s),
    ]
    fetch(pairs, sems)
    write_grads(own_count(valid_s, 1), size_s, value_s, out)


def half_weights(valid, queries, fast, weights, own, live, valid_s, query_s, gate_s, up_s, sems):
    x, c = lax.axis_index("x"), lax.axis_index("c")
    start = c * HALF
    edge = pl.multiple_of(c * 256, 128)
    pairs = [
        (fast.at[:, pl.ds(edge, 384)], gate_s),
        (fast.at[:, pl.ds(WIDTH + edge, 384)], up_s),
        (valid, valid_s),
        (queries, query_s),
    ]
    row = lax.broadcasted_iota(jnp.int32, (HALF, 384), 0)
    col = lax.broadcasted_iota(jnp.int32, (HALF, 384), 1)
    wanted = row
    for i, shift in enumerate(SHIFTS):
        block = lax.rem(x + shift, NX)
        first = pl.multiple_of(start + block * UNITS, UNITS)
        source = fast.at[pl.ds(first, UNITS), pl.ds(2 * WIDTH, WIDTH)]
        pairs.append((source, weights.at[2, pl.ds(i * UNITS, UNITS)]))
        inside = (row >= i * UNITS) & (row < (i + 1) * UNITS)
        wanted = jnp.where(inside, first - edge + row - i * UNITS, wanted)
    chosen = jnp.where(col == wanted, 1.0, 0.0).astype(BF16)
    fetch(pairs, sems)
    for i, window in enumerate((gate_s, up_s)):
        weights[i] = dot(chosen, window[...], 1, 1).astype(BF16)
    for i in range(3):
        own[i * UNITS : (i + 1) * UNITS] = weights[i, :UNITS]
    row = lax.broadcasted_iota(jnp.int32, (ROWS, WIDTH), 0)
    for group in range(2):
        rows = query_s[group].astype(F32)
        live[group] = jnp.where(row < own_count(valid_s, group), rows, 0.0).astype(BF16)


def gradients(into, down, keys, grads):
    units = down.shape[0]
    pre = dot(into, keys, 1, 1)
    gate, up = pre[:units], pre[units:]
    d_hidden = dot(down, grads, 1, 1)
    sig = jax.nn.sigmoid(gate)
    hidden = (gate * sig * up).astype(BF16)
    d_up = (d_hidden * gate * sig).astype(BF16)
    d_gate = (d_hidden * up * sig * (1.0 + gate * (1.0 - sig))).astype(BF16)
    inner = dot(jnp.concatenate([d_gate, d_up], 0), keys).astype(BF16)
    return inner, dot(hidden, grads).astype(BF16)


def first_partial(weights, own, other, *outs):
    keys = jnp.concatenate([own[0], other[0]], 0)
    grads = jnp.concatenate([own[1], other[1]], 0)
    into = jnp.concatenate([weights[0], weights[1]], 0)
    inner, outer = gradients(into, weights[2], keys, grads)
    for i, out in enumerate(outs):
        rows = slice(i * UNITS, (i + 1) * UNITS)
        out[0:UNITS] = inner[rows]
        out[UNITS : 2 * UNITS] = inner[HALF:][rows]
        out[2 * UNITS :] = outer[rows]


def summed_x(*refs):
    blocks, out = refs[:-1], refs[-1]
    total = blocks[0][...].astype(F32)
    for block in blocks[1:]:
        total += block[...].astype(F32)
    out[0:PART] = total.astype(BF16)
    out[PART:] = jnp.zeros((PADDED - PART, WIDTH), BF16)


def summed(got, out):
    total = got[0].astype(F32)
    for i in range(1, NZ):
        total += got[i].astype(F32)
    total = total.astype(BF16)
    for i in range(NZ):
        out[i] = total


def statistics(weights, gradient, out):
    grad = gradient[...].astype(F32)
    old = weights[2 * UNITS :].astype(F32)
    down = grad[2 * UNITS : PART]
    squares = jnp.sum(grad * grad, 0, keepdims=True)
    lines = [
        jnp.sum(old * old, 0, keepdims=True),
        jnp.sum(old * down, 0, keepdims=True),
        jnp.sum(down * down, 0, keepdims=True),
        squares,
    ]
    lines = jnp.concatenate(lines + [jnp.zeros((4, WIDTH), F32)], 0)
    for i in range(2 * NX):
        out[i] = lines


def second_partial(weights, gradient, stats, *refs):
    blocks, fresh, out = refs[:-2], refs[-2], refs[-1]
    total = stats[0]
    for i in range(1, 2 * NX):
        total += stats[i]
    rate = rate_of(total[3:4])
    old = weights[...].astype(F32)
    moved = old - rate * gradient[:PART].astype(F32)
    old_in, moved_in = old[: 2 * UNITS], moved[: 2 * UNITS]
    ratio_in = jnp.sqrt(jnp.sum(old_in * old_in, 1, keepdims=True)) / jnp.sqrt(
        jnp.sum(moved_in * moved_in, 1, keepdims=True) + epsilon
    )
    ratio_out = ratio_of(rate, total[0:1], total[1:2], total[2:3])
    new = jnp.concatenate([moved_in * ratio_in, moved[2 * UNITS :] * ratio_out], 0).astype(BF16)
    fresh[...] = new
    keys = jnp.concatenate([b[0] for b in blocks], 0)
    grads = jnp.concatenate([b[1] for b in blocks], 0)
    inner, outer = gradients(new[: 2 * UNITS], new[2 * UNITS :], keys, grads)
    out[0 : 2 * UNITS] = inner
    out[2 * UNITS : PART] = outer
    out[PART:] = jnp.zeros((PADDED - PART, WIDTH), BF16)


def rate_of(squares):
    return RATE / jnp.sqrt(jnp.sum(squares, 1, keepdims=True) / COUNT + epsilon)


def ratio_of(rate, old, cross, grad):
    moved = jnp.maximum(old - 2.0 * rate * cross + rate * rate * grad, 0.0)
    return jnp.sqrt(old) / jnp.sqrt(moved + epsilon)


def respond(group, queries, others, into, down, mine, theirs):
    rows = jnp.concatenate([queries[group], others[group]], 0)
    pre = dot(rows, into, 1, 1)
    gate, up = pre[:, :HALF], pre[:, HALF:]
    hidden = (gate * jax.nn.sigmoid(gate) * up).astype(BF16)
    result = dot(hidden, down)
    mine[...] = result[:ROWS]
    theirs[...] = result[ROWS:].astype(BF16)


def first_answer(queries, others, *refs):
    blocks, (mine, theirs) = refs[:NX], refs[NX:]
    parts = [
        jnp.concatenate([b[i * UNITS : (i + 1) * UNITS] for b in blocks], 0) for i in range(3)
    ]
    respond(0, queries, others, jnp.concatenate(parts[:2], 0), parts[2], mine, theirs)


def sums(weights, gradient, inner):
    old, grad = weights[...].astype(F32), gradient[:PART].astype(F32)
    products = [old * old, old * grad, grad * grad]
    for i, product in enumerate(products):
        inner[i] = jnp.sum(product[: 2 * UNITS], 1, keepdims=True)
    lines = [jnp.sum(p[2 * UNITS :], 0, keepdims=True) for p in products]
    return jnp.concatenate(lines + [jnp.sum(products[2], 0, keepdims=True)], 0)


def early_sums(*refs):
    held, blocks, (inner, lines) = refs[:2], refs[2:4], refs[4:]
    lines[0:4] = sum(sums(held[i], blocks[i], inner.at[i]) for i in range(2))
    lines[4:] = jnp.zeros((4, WIDTH), F32)


def late_sums(early, *refs):
    held, blocks, (inner, lines) = refs[:2], refs[2:4], refs[4:]
    lines[0:4] = early[0:4] + sum(sums(held[i], blocks[i], inner.at[i]) for i in range(2))
    lines[4:] = jnp.zeros((4, WIDTH), F32)


def second_answer(queries, others, own_lines, other_lines, early_in, late_in, *refs):
    held, blocks, (mine, theirs, into, down) = refs[:NX], refs[NX : 2 * NX], refs[2 * NX :]
    lines = own_lines[...] + other_lines[...]
    rate = rate_of(lines[3:4])
    ratio_out = ratio_of(rate, lines[0:1], lines[1:2], lines[2:3])
    inner = [early_in.at[0], late_in.at[0], late_in.at[1], early_in.at[1]]
    for i, (weights, block) in enumerate(zip(held, blocks)):
        moved = weights[...].astype(F32) - rate * block[:PART].astype(F32)
        ratio_in = ratio_of(rate, inner[i][0], inner[i][1], inner[i][2])
        fresh = (moved[: 2 * UNITS] * ratio_in).astype(BF16)
        into[i * UNITS : (i + 1) * UNITS] = fresh[:UNITS]
        into[HALF + i * UNITS : HALF + (i + 1) * UNITS] = fresh[UNITS:]
        down[i * UNITS : (i + 1) * UNITS] = (moved[2 * UNITS :] * ratio_out).astype(BF16)
    respond(1, queries, others, into[...], down[...], mine, theirs)


def joined(one, two, other_one, other_two, out):
    for group, (mine, theirs) in enumerate(((one, other_one), (two, other_two))):
        out[group] = (mine[...] + theirs[...].astype(F32)).astype(BF16)


def shifted(value, axis, size, shift):
    return lax.ppermute(value, axis, [(i, (i + shift) % size) for i in range(size)])


def along_x(block):
    return [block] + [shifted(block, "x", NX, shift) for shift in SHIFTS[1:]]


def from_core(near):
    return [shifted(b, "c", 2, 1) for b in near]


def reduce_z(partial):
    got = lax.all_to_all(partial.reshape(NZ, PADDED // NZ, WIDTH), "z", 0, 0, tiled=True)
    return kernel_call(summed, shape(*got.shape), [VMEM])(got)


def gather_z(shards):
    return lax.all_to_all(shards, "z", 0, 0, tiled=True).reshape(PADDED, WIDTH)


def under_z(partial, block):
    near = along_x(block)
    shards, near[:3] = lax.optimization_barrier((reduce_z(partial), near[:3]))
    return lax.optimization_barrier((gather_z(shards), near))


def body(queries, key_vectors, value_vectors, step_sizes, valid_rows, fast_init):
    held_inputs = (valid_rows, key_vectors[:, 0], value_vectors[:, 0], step_sizes)
    held_inputs += (queries[:, 0], fast_init[0])
    inputs = [pltpu.with_memory_space_constraint(i, pltpu.HBM) for i in held_inputs]
    pair, padded = shape(2, ROWS, WIDTH), shape(PADDED, WIDTH)
    scratch = [
        pltpu.SMEM(valid_rows.shape, jnp.int32),
        pltpu.VMEM((ROWS, WIDTH), BF16),
        pltpu.VMEM((1, ROWS), F32),
        pltpu.SemaphoreType.DMA((4,)),
    ]
    first = kernel_call(prepare_first, pair, [HBM] * 4, scratch)(*inputs[:4])
    other = shifted(first, "c", 2, 1)
    weights, own, queries = kernel_call(
        half_weights,
        (shape(3, HALF, WIDTH), shape(PART, WIDTH), pair),
        [HBM] * 3,
        [scratch[0], pltpu.VMEM(pair.shape, BF16)]
        + [pltpu.VMEM((WIDTH, 384), BF16)] * 2
        + [pltpu.SemaphoreType.DMA((8,))],
    )(inputs[0], *inputs[4:])
    others = shifted(queries, "c", 2, 1)
    parts = kernel_call(first_partial, (shape(PART, WIDTH),) * NX, [VMEM] * 3)(
        weights, first, other
    )
    parts = [parts[0]] + [shifted(p, "x", NX, s) for p, s in zip(parts[1:], SHIFTS[1:])]
    second = kernel_call(prepare_second, pair, [HBM] * 4, scratch)(*inputs[:4])
    *parts, second, others = lax.optimization_barrier((*parts, second, others))
    partial = kernel_call(summed_x, padded, [VMEM] * NX)(*parts)
    gradient, tokens = under_z(partial, second)
    tokens += from_core(tokens)
    stats = kernel_call(statistics, shape(2 * NX, 8, WIDTH, dtype=F32), [VMEM] * 2)(
        own, gradient
    )
    stats = lax.all_to_all(stats, ("x", "c"), 0, 0, tiled=True)
    fresh, partial = kernel_call(second_partial, (shape(PART, WIDTH), padded), [VMEM] * 11)(
        own, gradient, stats, *tokens
    )
    gradient, held = under_z(partial, fresh)
    near = along_x(gradient)
    share = (shape(ROWS, WIDTH, dtype=F32), shape(ROWS, WIDTH))
    one, theirs = kernel_call(first_answer, share, [VMEM] * 6)(queries, others, *held)
    found = (shape(2, 3, 2 * UNITS, 1, dtype=F32), shape(8, WIDTH, dtype=F32))
    early, lines = kernel_call(early_sums, found, [VMEM] * 4)(held[0], held[3], near[0], near[3])
    other_one = shifted(theirs, "c", 2, 1)
    near[1], near[2], lines, other_one = lax.optimization_barrier(
        (near[1], near[2], lines, other_one)
    )
    late, lines = kernel_call(late_sums, found, [VMEM] * 5)(lines, *held[1:3], *near[1:3])
    two, theirs = kernel_call(
        second_answer,
        share,
        [VMEM] * 14,
        [pltpu.VMEM((WIDTH, WIDTH), BF16), pltpu.VMEM((HALF, WIDTH), BF16)],
    )(queries, others, lines, shifted(lines, "c", 2, 1), early, late, *held, *near)
    other_two = shifted(theirs, "c", 2, 1)
    out = kernel_call(joined, shape(2, ROWS, WIDTH), [VMEM] * 4)(one, two, other_one, other_two)
    return out[:, None]


def solution(mesh):
    split = Mesh(mesh.devices.reshape(mesh.shape["head"], NZ, NX, 2), ("head", "z", "x", "c"))
    seq = ("z", "x", "c")
    rows = P(None, "head", seq, None)
    placed = (rows, rows, rows, P(None, "head", seq), P(), P("head", None, None))
    return jax.shard_map(body, mesh=split, in_specs=placed, out_specs=rows, check_vma=False)
```

```python
import jax
import jax.numpy as jnp
from jax import lax
from jax.experimental import pallas as pl
from jax.experimental.pallas import tpu as pltpu
from jax.sharding import Mesh
from jax.sharding import PartitionSpec as P

step_factor = 0.5
epsilon = 1e-06
NX = 4
NZ = 8
ROWS = 128
WIDTH = 640
UNITS = 80
HALF = NX * UNITS
SHIFTS = (0, 1, 3, 2)
PART = 3 * UNITS
PADDED = 256
RATE = step_factor / WIDTH**0.5
COUNT = 3 * WIDTH * WIDTH
F32 = jnp.float32
BF16 = jnp.bfloat16
VMEM = pl.BlockSpec(memory_space=pltpu.VMEM)
HBM = pl.BlockSpec(memory_space=pltpu.HBM)


def dot(a, b, ca=1, cb=0):
    return lax.dot_general(a, b, (((ca,), (cb,)), ((), ())), preferred_element_type=F32)


def shape(*dims, dtype=BF16):
    return jax.ShapeDtypeStruct(dims, dtype)


def kernel_call(body, outs, ins, scratch=()):
    return pl.pallas_call(
        body,
        out_shape=outs,
        in_specs=ins,
        out_specs=jax.tree.map(lambda _: VMEM, outs),
        scratch_shapes=list(scratch),
        compiler_params=pltpu.CompilerParams(vmem_limit_bytes=20 * 1024 * 1024),
    )


def own_count(valid, group):
    rank = (lax.axis_index("z") * NX + lax.axis_index("x")) * 2 + lax.axis_index("c")
    return valid[group, rank]


def fetch(pairs, sems):
    copies = [pltpu.make_async_copy(src, dst, sems.at[i]) for i, (src, dst) in enumerate(pairs)]
    for copy in copies:
        copy.start()
    for copy in copies:
        copy.wait()


def write_grads(live_rows, sizes, values, out):
    row = lax.broadcasted_iota(jnp.int32, (ROWS, ROWS), 0)
    col = lax.broadcasted_iota(jnp.int32, (ROWS, ROWS), 1)
    size = jnp.sum(jnp.where(row == col, sizes[...], 0.0), 1, keepdims=True)
    scaled = jnp.where(row[:, :1] < live_rows, size, 0.0)
    out[1] = (-(scaled * values[...].astype(F32))).astype(BF16)


def prepare_first(valid, keys, values, sizes, out, valid_s, value_s, size_s, sems):
    pairs = [
        (keys.at[0], out.at[0]),
        (values.at[0], value_s),
        (sizes.at[0], size_s),
        (valid, valid_s),
    ]
    fetch(pairs, sems)
    write_grads(own_count(valid_s, 0), size_s, value_s, out)


def prepare_second(valid, keys, values, sizes, out, valid_s, value_s, size_s, sems):
    pairs = [
        (keys.at[1], out.at[0]),
        (values.at[1], value_s),
        (sizes.at[1], size_s),
        (valid, valid_s),
    ]
    fetch(pairs, sems)
    write_grads(own_count(valid_s, 1), size_s, value_s, out)


def half_weights(valid, queries, fast, weights, own, live, valid_s, query_s, gate_s, up_s, sems):
    x, c = lax.axis_index("x"), lax.axis_index("c")
    start = c * HALF
    edge = pl.multiple_of(c * 256, 128)
    pairs = [
        (fast.at[:, pl.ds(edge, 384)], gate_s),
        (fast.at[:, pl.ds(WIDTH + edge, 384)], up_s),
        (valid, valid_s),
        (queries, query_s),
    ]
    row = lax.broadcasted_iota(jnp.int32, (HALF, 384), 0)
    col = lax.broadcasted_iota(jnp.int32, (HALF, 384), 1)
    wanted = row
    for i, shift in enumerate(SHIFTS):
        block = lax.rem(x + shift, NX)
        first = pl.multiple_of(start + block * UNITS, UNITS)
        source = fast.at[pl.ds(first, UNITS), pl.ds(2 * WIDTH, WIDTH)]
        pairs.append((source, weights.at[2, pl.ds(i * UNITS, UNITS)]))
        inside = (row >= i * UNITS) & (row < (i + 1) * UNITS)
        wanted = jnp.where(inside, first - edge + row - i * UNITS, wanted)
    chosen = jnp.where(col == wanted, 1.0, 0.0).astype(BF16)
    fetch(pairs, sems)
    for i, window in enumerate((gate_s, up_s)):
        weights[i] = dot(chosen, window[...], 1, 1).astype(BF16)
    for i in range(3):
        own[i * UNITS : (i + 1) * UNITS] = weights[i, :UNITS]
    row = lax.broadcasted_iota(jnp.int32, (ROWS, WIDTH), 0)
    for group in range(2):
        rows = query_s[group].astype(F32)
        live[group] = jnp.where(row < own_count(valid_s, group), rows, 0.0).astype(BF16)


def gradients(into, down, keys, grads):
    units = down.shape[0]
    pre = dot(into, keys, 1, 1)
    gate, up = pre[:units], pre[units:]
    d_hidden = dot(down, grads, 1, 1)
    sig = jax.nn.sigmoid(gate)
    hidden = (gate * sig * up).astype(BF16)
    d_up = (d_hidden * gate * sig).astype(BF16)
    d_gate = (d_hidden * up * sig * (1.0 + gate * (1.0 - sig))).astype(BF16)
    inner = dot(jnp.concatenate([d_gate, d_up], 0), keys).astype(BF16)
    return inner, dot(hidden, grads).astype(BF16)


def first_partial(weights, own, other, *outs):
    keys = jnp.concatenate([own[0], other[0]], 0)
    grads = jnp.concatenate([own[1], other[1]], 0)
    into = jnp.concatenate([weights[0], weights[1]], 0)
    inner, outer = gradients(into, weights[2], keys, grads)
    for i, out in enumerate(outs):
        rows = slice(i * UNITS, (i + 1) * UNITS)
        out[0:UNITS] = inner[rows]
        out[UNITS : 2 * UNITS] = inner[HALF:][rows]
        out[2 * UNITS :] = outer[rows]


def summed_x(*refs):
    blocks, out = refs[:-1], refs[-1]
    total = blocks[0][...].astype(F32)
    for block in blocks[1:]:
        total += block[...].astype(F32)
    out[0:PART] = total.astype(BF16)
    out[PART:] = jnp.zeros((PADDED - PART, WIDTH), BF16)


def summed(got, out):
    total = got[0].astype(F32)
    for i in range(1, NZ):
        total += got[i].astype(F32)
    total = total.astype(BF16)
    for i in range(NZ):
        out[i] = total


def statistics(weights, gradient, out):
    grad = gradient[...].astype(F32)
    old = weights[2 * UNITS :].astype(F32)
    down = grad[2 * UNITS : PART]
    squares = jnp.sum(grad * grad, 0, keepdims=True)
    lines = [
        jnp.sum(old * old, 0, keepdims=True),
        jnp.sum(old * down, 0, keepdims=True),
        jnp.sum(down * down, 0, keepdims=True),
        squares,
    ]
    lines = jnp.concatenate(lines + [jnp.zeros((4, WIDTH), F32)], 0)
    for i in range(2 * NX):
        out[i] = lines


def all_sums(stats):
    total = stats[0]
    for i in range(1, 2 * NX):
        total += stats[i]
    old, cross, grad, squares = (total[i : i + 1] for i in range(4))
    rate = RATE / jnp.sqrt(jnp.sum(squares, 1, keepdims=True) / COUNT + epsilon)
    moved = jnp.maximum(old - 2.0 * rate * cross + rate * rate * grad, 0.0)
    return rate, jnp.sqrt(old) / jnp.sqrt(moved + epsilon)


def renewed(weights, gradient, rate, ratio_out):
    old = weights[...].astype(F32)
    moved = old - rate * gradient[:PART].astype(F32)
    old_in, moved_in = old[: 2 * UNITS], moved[: 2 * UNITS]
    ratio_in = jnp.sqrt(jnp.sum(old_in * old_in, 1, keepdims=True)) / jnp.sqrt(
        jnp.sum(moved_in * moved_in, 1, keepdims=True) + epsilon
    )
    return jnp.concatenate([moved_in * ratio_in, moved[2 * UNITS :] * ratio_out], 0).astype(BF16)


def second_partial(weights, gradient, stats, *refs):
    blocks, fresh, out = refs[:-2], refs[-2], refs[-1]
    new = renewed(weights, gradient, *all_sums(stats))
    fresh[...] = new
    keys = jnp.concatenate([b[0] for b in blocks], 0)
    grads = jnp.concatenate([b[1] for b in blocks], 0)
    inner, outer = gradients(new[: 2 * UNITS], new[2 * UNITS :], keys, grads)
    out[0 : 2 * UNITS] = inner
    out[2 * UNITS : PART] = outer
    out[PART:] = jnp.zeros((PADDED - PART, WIDTH), BF16)


def respond(group, queries, others, into, down, mine, theirs):
    rows = jnp.concatenate([queries[group], others[group]], 0)
    pre = dot(rows, into, 1, 1)
    gate, up = pre[:, :HALF], pre[:, HALF:]
    hidden = (gate * jax.nn.sigmoid(gate) * up).astype(BF16)
    result = dot(hidden, down)
    mine[...] = result[:ROWS]
    theirs[...] = result[ROWS:].astype(BF16)


def first_answer(queries, others, *refs):
    blocks, (mine, theirs) = refs[:NX], refs[NX:]
    parts = [
        jnp.concatenate([b[i * UNITS : (i + 1) * UNITS] for b in blocks], 0) for i in range(3)
    ]
    respond(0, queries, others, jnp.concatenate(parts[:2], 0), parts[2], mine, theirs)


def second_answer(queries, others, stats, *refs):
    held, blocks, (mine, theirs, into, down) = refs[:NX], refs[NX : 2 * NX], refs[2 * NX :]
    rate, ratio_out = all_sums(stats)
    for i, (weights, block) in enumerate(zip(held, blocks)):
        fresh = renewed(weights, block, rate, ratio_out)
        into[i * UNITS : (i + 1) * UNITS] = fresh[:UNITS]
        into[HALF + i * UNITS : HALF + (i + 1) * UNITS] = fresh[UNITS : 2 * UNITS]
        down[i * UNITS : (i + 1) * UNITS] = fresh[2 * UNITS :]
    respond(1, queries, others, into[...], down[...], mine, theirs)


def joined(one, two, other_one, other_two, out):
    for group, (mine, theirs) in enumerate(((one, other_one), (two, other_two))):
        out[group] = (mine[...] + theirs[...].astype(F32)).astype(BF16)


def shifted(value, axis, size, shift):
    return lax.ppermute(value, axis, [(i, (i + shift) % size) for i in range(size)])


def along_x(block):
    return [block] + [shifted(block, "x", NX, shift) for shift in SHIFTS[1:]]


def from_core(near):
    return [shifted(b, "c", 2, 1) for b in near]


def reduce_z(partial):
    got = lax.all_to_all(partial.reshape(NZ, PADDED // NZ, WIDTH), "z", 0, 0, tiled=True)
    return kernel_call(summed, shape(*got.shape), [VMEM])(got)


def gather_z(shards):
    return lax.all_to_all(shards, "z", 0, 0, tiled=True).reshape(PADDED, WIDTH)


def exchanged_sums(weights, gradient):
    stats = kernel_call(statistics, shape(2 * NX, 8, WIDTH, dtype=F32), [VMEM] * 2)(
        weights, gradient
    )
    return lax.all_to_all(stats, ("x", "c"), 0, 0, tiled=True)


def under_z(partial, block):
    near = along_x(block)
    shards, near[:3] = lax.optimization_barrier((reduce_z(partial), near[:3]))
    return lax.optimization_barrier((gather_z(shards), near))


def body(queries, key_vectors, value_vectors, step_sizes, valid_rows, fast_init):
    held_inputs = (valid_rows, key_vectors[:, 0], value_vectors[:, 0], step_sizes)
    held_inputs += (queries[:, 0], fast_init[0])
    inputs = [pltpu.with_memory_space_constraint(i, pltpu.HBM) for i in held_inputs]
    pair, padded = shape(2, ROWS, WIDTH), shape(PADDED, WIDTH)
    scratch = [
        pltpu.SMEM(valid_rows.shape, jnp.int32),
        pltpu.VMEM((ROWS, WIDTH), BF16),
        pltpu.VMEM((1, ROWS), F32),
        pltpu.SemaphoreType.DMA((4,)),
    ]
    first = kernel_call(prepare_first, pair, [HBM] * 4, scratch)(*inputs[:4])
    other = shifted(first, "c", 2, 1)
    weights, own, queries = kernel_call(
        half_weights,
        (shape(3, HALF, WIDTH), shape(PART, WIDTH), pair),
        [HBM] * 3,
        [scratch[0], pltpu.VMEM(pair.shape, BF16)]
        + [pltpu.VMEM((WIDTH, 384), BF16)] * 2
        + [pltpu.SemaphoreType.DMA((8,))],
    )(inputs[0], *inputs[4:])
    others = shifted(queries, "c", 2, 1)
    parts = kernel_call(first_partial, (shape(PART, WIDTH),) * NX, [VMEM] * 3)(
        weights, first, other
    )
    parts = [parts[0]] + [shifted(p, "x", NX, s) for p, s in zip(parts[1:], SHIFTS[1:])]
    second = kernel_call(prepare_second, pair, [HBM] * 4, scratch)(*inputs[:4])
    *parts, second, others = lax.optimization_barrier((*parts, second, others))
    partial = kernel_call(summed_x, padded, [VMEM] * NX)(*parts)
    gradient, tokens = under_z(partial, second)
    tokens += from_core(tokens)
    stats = exchanged_sums(own, gradient)
    fresh, partial = kernel_call(second_partial, (shape(PART, WIDTH), padded), [VMEM] * 11)(
        own, gradient, stats, *tokens
    )
    gradient, held = under_z(partial, fresh)
    near = along_x(gradient)
    share = (shape(ROWS, WIDTH, dtype=F32), shape(ROWS, WIDTH))
    stats = exchanged_sums(fresh, gradient)
    stats, queries = lax.optimization_barrier((stats, queries))
    one, theirs = kernel_call(first_answer, share, [VMEM] * 6)(queries, others, *held)
    near[1:], theirs = lax.optimization_barrier((near[1:], theirs))
    other_one = shifted(theirs, "c", 2, 1)
    two, theirs = kernel_call(
        second_answer,
        share,
        [VMEM] * 11,
        [pltpu.VMEM((WIDTH, WIDTH), BF16), pltpu.VMEM((HALF, WIDTH), BF16)],
    )(queries, others, stats, *held, *near)
    other_two = shifted(theirs, "c", 2, 1)
    out = kernel_call(joined, shape(2, ROWS, WIDTH), [VMEM] * 4)(one, two, other_one, other_two)
    return out[:, None]


def solution(mesh):
    split = Mesh(mesh.devices.reshape(mesh.shape["head"], NZ, NX, 2), ("head", "z", "x", "c"))
    seq = ("z", "x", "c")
    rows = P(None, "head", seq, None)
    placed = (rows, rows, rows, P(None, "head", seq), P(), P("head", None, None))
    return jax.shard_map(body, mesh=split, in_specs=placed, out_specs=rows, check_vma=False)
```

```python
import jax
import jax.numpy as jnp
from jax import lax
from jax.experimental import pallas as pl
from jax.experimental.pallas import tpu as pltpu
from jax.sharding import Mesh
from jax.sharding import PartitionSpec as P

step_factor = 0.5
epsilon = 1e-06
NX = 4
NZ = 8
ROWS = 128
WIDTH = 640
UNITS = 80
HALF = NX * UNITS
SHIFTS = (0, 1, 3, 2)
PART = 3 * UNITS
PADDED = 256
RATE = step_factor / WIDTH**0.5
COUNT = 3 * WIDTH * WIDTH
F32 = jnp.float32
BF16 = jnp.bfloat16
VMEM = pl.BlockSpec(memory_space=pltpu.VMEM)
HBM = pl.BlockSpec(memory_space=pltpu.HBM)


def dot(a, b, ca=1, cb=0):
    return lax.dot_general(a, b, (((ca,), (cb,)), ((), ())), preferred_element_type=F32)


def shape(*dims, dtype=BF16):
    return jax.ShapeDtypeStruct(dims, dtype)


def kernel_call(body, outs, ins, scratch=()):
    return pl.pallas_call(
        body,
        out_shape=outs,
        in_specs=ins,
        out_specs=jax.tree.map(lambda _: VMEM, outs),
        scratch_shapes=list(scratch),
        compiler_params=pltpu.CompilerParams(vmem_limit_bytes=20 * 1024 * 1024),
    )


def own_count(valid, group):
    rank = (lax.axis_index("z") * NX + lax.axis_index("x")) * 2 + lax.axis_index("c")
    return valid[group, rank]


def fetch(pairs, sems):
    copies = [pltpu.make_async_copy(src, dst, sems.at[i]) for i, (src, dst) in enumerate(pairs)]
    for copy in copies:
        copy.start()
    for copy in copies:
        copy.wait()


def write_grads(live_rows, sizes, values, out):
    row = lax.broadcasted_iota(jnp.int32, (ROWS, ROWS), 0)
    col = lax.broadcasted_iota(jnp.int32, (ROWS, ROWS), 1)
    size = jnp.sum(jnp.where(row == col, sizes[...], 0.0), 1, keepdims=True)
    scaled = jnp.where(row[:, :1] < live_rows, size, 0.0)
    out[1] = (-(scaled * values[...].astype(F32))).astype(BF16)


def prepare_first(valid, keys, values, sizes, out, valid_s, value_s, size_s, sems):
    pairs = [
        (keys.at[0], out.at[0]),
        (values.at[0], value_s),
        (sizes.at[0], size_s),
        (valid, valid_s),
    ]
    fetch(pairs, sems)
    write_grads(own_count(valid_s, 0), size_s, value_s, out)


def prepare_second(
    valid, keys, values, sizes, queries, out, live, valid_s, value_s, size_s, query_s, sems
):
    pairs = [
        (keys.at[1], out.at[0]),
        (values.at[1], value_s),
        (sizes.at[1], size_s),
        (valid, valid_s),
        (queries, query_s),
    ]
    fetch(pairs, sems)
    write_grads(own_count(valid_s, 1), size_s, value_s, out)
    row = lax.broadcasted_iota(jnp.int32, (ROWS, WIDTH), 0)
    for group in range(2):
        rows = query_s[group].astype(F32)
        live[group] = jnp.where(row < own_count(valid_s, group), rows, 0.0).astype(BF16)


def half_weights(fast, weights, own, gate_s, up_s, sems):
    x, c = lax.axis_index("x"), lax.axis_index("c")
    start = c * HALF
    edge = pl.multiple_of(c * 256, 128)
    pairs = [
        (fast.at[:, pl.ds(edge, 384)], gate_s),
        (fast.at[:, pl.ds(WIDTH + edge, 384)], up_s),
    ]
    row = lax.broadcasted_iota(jnp.int32, (HALF, 384), 0)
    col = lax.broadcasted_iota(jnp.int32, (HALF, 384), 1)
    wanted = row
    for i, shift in enumerate(SHIFTS):
        block = lax.rem(x + shift, NX)
        first = pl.multiple_of(start + block * UNITS, UNITS)
        source = fast.at[pl.ds(first, UNITS), pl.ds(2 * WIDTH, WIDTH)]
        pairs.append((source, weights.at[2, pl.ds(i * UNITS, UNITS)]))
        inside = (row >= i * UNITS) & (row < (i + 1) * UNITS)
        wanted = jnp.where(inside, first - edge + row - i * UNITS, wanted)
    chosen = jnp.where(col == wanted, 1.0, 0.0).astype(BF16)
    fetch(pairs, sems)
    for i, window in enumerate((gate_s, up_s)):
        weights[i] = dot(chosen, window[...], 1, 1).astype(BF16)
    for i in range(3):
        own[i * UNITS : (i + 1) * UNITS] = weights[i, :UNITS]


def gradients(into, down, keys, grads):
    units = down.shape[0]
    pre = dot(into, keys, 1, 1)
    gate, up = pre[:units], pre[units:]
    d_hidden = dot(down, grads, 1, 1)
    sig = jax.nn.sigmoid(gate)
    hidden = (gate * sig * up).astype(BF16)
    d_up = (d_hidden * gate * sig).astype(BF16)
    d_gate = (d_hidden * up * sig * (1.0 + gate * (1.0 - sig))).astype(BF16)
    inner = dot(jnp.concatenate([d_gate, d_up], 0), keys).astype(BF16)
    return inner, dot(hidden, grads).astype(BF16)


def first_partial(weights, own, other, *outs):
    keys = jnp.concatenate([own[0], other[0]], 0)
    grads = jnp.concatenate([own[1], other[1]], 0)
    into = jnp.concatenate([weights[0], weights[1]], 0)
    inner, outer = gradients(into, weights[2], keys, grads)
    for i, out in enumerate(outs):
        rows = slice(i * UNITS, (i + 1) * UNITS)
        out[0:UNITS] = inner[rows]
        out[UNITS : 2 * UNITS] = inner[HALF:][rows]
        out[2 * UNITS :] = outer[rows]


def summed_x(*refs):
    blocks, out = refs[:-1], refs[-1]
    total = blocks[0][...].astype(F32)
    for block in blocks[1:]:
        total += block[...].astype(F32)
    out[0:PART] = total.astype(BF16)
    out[PART:] = jnp.zeros((PADDED - PART, WIDTH), BF16)


def summed(got, out):
    total = got[0].astype(F32)
    for i in range(1, NZ):
        total += got[i].astype(F32)
    total = total.astype(BF16)
    for i in range(NZ):
        out[i] = total


def statistics(weights, gradient, out):
    grad = gradient[...].astype(F32)
    old = weights[2 * UNITS :].astype(F32)
    down = grad[2 * UNITS : PART]
    squares = jnp.sum(grad * grad, 0, keepdims=True)
    lines = [
        jnp.sum(old * old, 0, keepdims=True),
        jnp.sum(old * down, 0, keepdims=True),
        jnp.sum(down * down, 0, keepdims=True),
        squares,
    ]
    lines = jnp.concatenate(lines + [jnp.zeros((4, WIDTH), F32)], 0)
    for i in range(2 * NX):
        out[i] = lines


def second_partial(weights, gradient, stats, *refs):
    blocks, fresh, out = refs[:-2], refs[-2], refs[-1]
    total = stats[0]
    for i in range(1, 2 * NX):
        total += stats[i]
    rate = rate_of(total[3:4])
    old = weights[...].astype(F32)
    moved = old - rate * gradient[:PART].astype(F32)
    old_in, moved_in = old[: 2 * UNITS], moved[: 2 * UNITS]
    ratio_in = jnp.sqrt(jnp.sum(old_in * old_in, 1, keepdims=True)) / jnp.sqrt(
        jnp.sum(moved_in * moved_in, 1, keepdims=True) + epsilon
    )
    ratio_out = ratio_of(rate, total[0:1], total[1:2], total[2:3])
    new = jnp.concatenate([moved_in * ratio_in, moved[2 * UNITS :] * ratio_out], 0).astype(BF16)
    fresh[...] = new
    keys = jnp.concatenate([b[0] for b in blocks], 0)
    grads = jnp.concatenate([b[1] for b in blocks], 0)
    inner, outer = gradients(new[: 2 * UNITS], new[2 * UNITS :], keys, grads)
    out[0 : 2 * UNITS] = inner
    out[2 * UNITS : PART] = outer
    out[PART:] = jnp.zeros((PADDED - PART, WIDTH), BF16)


def rate_of(squares):
    return RATE / jnp.sqrt(jnp.sum(squares, 1, keepdims=True) / COUNT + epsilon)


def ratio_of(rate, old, cross, grad):
    moved = jnp.maximum(old - 2.0 * rate * cross + rate * rate * grad, 0.0)
    return jnp.sqrt(old) / jnp.sqrt(moved + epsilon)


def respond(group, queries, others, into, down, mine, theirs):
    rows = jnp.concatenate([queries[group], others[group]], 0)
    pre = dot(rows, into, 1, 1)
    gate, up = pre[:, :HALF], pre[:, HALF:]
    hidden = (gate * jax.nn.sigmoid(gate) * up).astype(BF16)
    result = dot(hidden, down)
    mine[...] = result[:ROWS]
    theirs[...] = result[ROWS:].astype(BF16)


def first_answer(queries, others, *refs):
    blocks, (mine, theirs) = refs[:NX], refs[NX:]
    parts = [
        jnp.concatenate([b[i * UNITS : (i + 1) * UNITS] for b in blocks], 0) for i in range(3)
    ]
    respond(0, queries, others, jnp.concatenate(parts[:2], 0), parts[2], mine, theirs)


def sums(weights, gradient, inner):
    old, grad = weights[...].astype(F32), gradient[:PART].astype(F32)
    products = [old * old, old * grad, grad * grad]
    for i, product in enumerate(products):
        inner[i] = jnp.sum(product[: 2 * UNITS], 1, keepdims=True)
    lines = [jnp.sum(p[2 * UNITS :], 0, keepdims=True) for p in products]
    return jnp.concatenate(lines + [jnp.sum(products[2], 0, keepdims=True)], 0)


def early_sums(*refs):
    held, blocks, (inner, lines) = refs[:2], refs[2:4], refs[4:]
    lines[0:4] = sum(sums(held[i], blocks[i], inner.at[i]) for i in range(2))
    lines[4:] = jnp.zeros((4, WIDTH), F32)


def late_sums(early, *refs):
    held, blocks, (inner, lines) = refs[:2], refs[2:4], refs[4:]
    lines[0:4] = early[0:4] + sum(sums(held[i], blocks[i], inner.at[i]) for i in range(2))
    lines[4:] = jnp.zeros((4, WIDTH), F32)


def second_answer(queries, others, own_lines, other_lines, early_in, late_in, *refs):
    held, blocks, (mine, theirs, into, down) = refs[:NX], refs[NX : 2 * NX], refs[2 * NX :]
    lines = own_lines[...] + other_lines[...]
    rate = rate_of(lines[3:4])
    ratio_out = ratio_of(rate, lines[0:1], lines[1:2], lines[2:3])
    inner = [early_in.at[0], late_in.at[0], late_in.at[1], early_in.at[1]]
    for i, (weights, block) in enumerate(zip(held, blocks)):
        moved = weights[...].astype(F32) - rate * block[:PART].astype(F32)
        ratio_in = ratio_of(rate, inner[i][0], inner[i][1], inner[i][2])
        fresh = (moved[: 2 * UNITS] * ratio_in).astype(BF16)
        into[i * UNITS : (i + 1) * UNITS] = fresh[:UNITS]
        into[HALF + i * UNITS : HALF + (i + 1) * UNITS] = fresh[UNITS:]
        down[i * UNITS : (i + 1) * UNITS] = (moved[2 * UNITS :] * ratio_out).astype(BF16)
    respond(1, queries, others, into[...], down[...], mine, theirs)


def joined(one, two, other_one, other_two, out):
    for group, (mine, theirs) in enumerate(((one, other_one), (two, other_two))):
        out[group] = (mine[...] + theirs[...].astype(F32)).astype(BF16)


def shifted(value, axis, size, shift):
    return lax.ppermute(value, axis, [(i, (i + shift) % size) for i in range(size)])


def along_x(block):
    return [block] + [shifted(block, "x", NX, shift) for shift in SHIFTS[1:]]


def from_core(near):
    return [shifted(b, "c", 2, 1) for b in near]


def reduce_z(partial):
    got = lax.all_to_all(partial.reshape(NZ, PADDED // NZ, WIDTH), "z", 0, 0, tiled=True)
    return kernel_call(summed, shape(*got.shape), [VMEM])(got)


def gather_z(shards):
    return lax.all_to_all(shards, "z", 0, 0, tiled=True).reshape(PADDED, WIDTH)


def under_z(partial, block):
    near = along_x(block)
    shards, near[:3] = lax.optimization_barrier((reduce_z(partial), near[:3]))
    return lax.optimization_barrier((gather_z(shards), near))


def body(queries, key_vectors, value_vectors, step_sizes, valid_rows, fast_init):
    held_inputs = (valid_rows, key_vectors[:, 0], value_vectors[:, 0], step_sizes)
    held_inputs += (queries[:, 0], fast_init[0])
    inputs = [pltpu.with_memory_space_constraint(i, pltpu.HBM) for i in held_inputs]
    pair, padded = shape(2, ROWS, WIDTH), shape(PADDED, WIDTH)
    scratch = [
        pltpu.SMEM(valid_rows.shape, jnp.int32),
        pltpu.VMEM((ROWS, WIDTH), BF16),
        pltpu.VMEM((1, ROWS), F32),
        pltpu.SemaphoreType.DMA((4,)),
    ]
    first = kernel_call(prepare_first, pair, [HBM] * 4, scratch)(*inputs[:4])
    other = shifted(first, "c", 2, 1)
    weights, own = kernel_call(
        half_weights,
        (shape(3, HALF, WIDTH), shape(PART, WIDTH)),
        [HBM],
        [pltpu.VMEM((WIDTH, 384), BF16)] * 2 + [pltpu.SemaphoreType.DMA((6,))],
    )(inputs[5])
    parts = kernel_call(first_partial, (shape(PART, WIDTH),) * NX, [VMEM] * 3)(
        weights, first, other
    )
    parts = [parts[0]] + [shifted(parts[i], "x", NX, SHIFTS[i]) for i in (3, 1, 2)]
    second, queries = kernel_call(
        prepare_second,
        (pair, pair),
        [HBM] * 5,
        scratch[:3] + [pltpu.VMEM(pair.shape, BF16), pltpu.SemaphoreType.DMA((5,))],
    )(*inputs[:5])
    *parts, second = lax.optimization_barrier((*parts, second))
    partial = kernel_call(summed_x, padded, [VMEM] * NX)(*parts)
    gradient, tokens = under_z(partial, second)
    gradient, queries = lax.optimization_barrier((gradient, queries))
    tokens += from_core(tokens)
    others = shifted(queries, "c", 2, 1)
    stats = kernel_call(statistics, shape(2 * NX, 8, WIDTH, dtype=F32), [VMEM] * 2)(
        own, gradient
    )
    stats = lax.all_to_all(stats, ("x", "c"), 0, 0, tiled=True)
    stats, others = lax.optimization_barrier((stats, others))
    fresh, partial = kernel_call(second_partial, (shape(PART, WIDTH), padded), [VMEM] * 11)(
        own, gradient, stats, *tokens
    )
    gradient, held = under_z(partial, fresh)
    near = along_x(gradient)
    share = (shape(ROWS, WIDTH, dtype=F32), shape(ROWS, WIDTH))
    one, theirs = kernel_call(first_answer, share, [VMEM] * 6)(queries, others, *held)
    found = (shape(2, 3, 2 * UNITS, 1, dtype=F32), shape(8, WIDTH, dtype=F32))
    early, lines = kernel_call(early_sums, found, [VMEM] * 4)(held[0], held[3], near[0], near[3])
    other_one = shifted(theirs, "c", 2, 1)
    near[1], near[2], lines, other_one = lax.optimization_barrier(
        (near[1], near[2], lines, other_one)
    )
    late, lines = kernel_call(late_sums, found, [VMEM] * 5)(lines, *held[1:3], *near[1:3])
    two, theirs = kernel_call(
        second_answer,
        share,
        [VMEM] * 14,
        [pltpu.VMEM((WIDTH, WIDTH), BF16), pltpu.VMEM((HALF, WIDTH), BF16)],
    )(queries, others, lines, shifted(lines, "c", 2, 1), early, late, *held, *near)
    other_two = shifted(theirs, "c", 2, 1)
    out = kernel_call(joined, shape(2, ROWS, WIDTH), [VMEM] * 4)(one, two, other_one, other_two)
    return out[:, None]


def solution(mesh):
    split = Mesh(mesh.devices.reshape(mesh.shape["head"], NZ, NX, 2), ("head", "z", "x", "c"))
    seq = ("z", "x", "c")
    rows = P(None, "head", seq, None)
    placed = (rows, rows, rows, P(None, "head", seq), P(), P("head", None, None))
    return jax.shard_map(body, mesh=split, in_specs=placed, out_specs=rows, check_vma=False)
```

```python
import jax
import jax.numpy as jnp
from jax import lax
from jax.experimental import pallas as pl
from jax.experimental.pallas import tpu as pltpu
from jax.sharding import Mesh
from jax.sharding import PartitionSpec as P

step_factor = 0.5
epsilon = 1e-06
NX = 4
NZ = 8
ROWS = 128
WIDTH = 640
UNITS = 80
HALF = NX * UNITS
SHIFTS = (0, 1, 3, 2)
PART = 3 * UNITS
PADDED = 256
RATE = step_factor / WIDTH**0.5
COUNT = 3 * WIDTH * WIDTH
F32 = jnp.float32
BF16 = jnp.bfloat16
VMEM = pl.BlockSpec(memory_space=pltpu.VMEM)
HBM = pl.BlockSpec(memory_space=pltpu.HBM)


def dot(a, b, ca=1, cb=0):
    return lax.dot_general(a, b, (((ca,), (cb,)), ((), ())), preferred_element_type=F32)


def shape(*dims, dtype=BF16):
    return jax.ShapeDtypeStruct(dims, dtype)


def kernel_call(body, outs, ins, scratch=()):
    return pl.pallas_call(
        body,
        out_shape=outs,
        in_specs=ins,
        out_specs=jax.tree.map(lambda _: VMEM, outs),
        scratch_shapes=list(scratch),
        compiler_params=pltpu.CompilerParams(vmem_limit_bytes=20 * 1024 * 1024),
    )


def own_count(valid, group):
    rank = (lax.axis_index("z") * NX + lax.axis_index("x")) * 2 + lax.axis_index("c")
    return valid[group, rank]


def fetch(pairs, sems):
    copies = [pltpu.make_async_copy(src, dst, sems.at[i]) for i, (src, dst) in enumerate(pairs)]
    for copy in copies:
        copy.start()
    for copy in copies:
        copy.wait()


def write_grads(live_rows, sizes, values, out):
    row = lax.broadcasted_iota(jnp.int32, (ROWS, ROWS), 0)
    col = lax.broadcasted_iota(jnp.int32, (ROWS, ROWS), 1)
    size = jnp.sum(jnp.where(row == col, sizes[...], 0.0), 1, keepdims=True)
    scaled = jnp.where(row[:, :1] < live_rows, size, 0.0)
    out[1] = (-(scaled * values[...].astype(F32))).astype(BF16)


def prepare_first(valid, keys, values, sizes, out, valid_s, value_s, size_s, sems):
    pairs = [
        (keys.at[0], out.at[0]),
        (values.at[0], value_s),
        (sizes.at[0], size_s),
        (valid, valid_s),
    ]
    fetch(pairs, sems)
    write_grads(own_count(valid_s, 0), size_s, value_s, out)


def prepare_second(valid, keys, values, sizes, out, valid_s, value_s, size_s, sems):
    pairs = [
        (keys.at[1], out.at[0]),
        (values.at[1], value_s),
        (sizes.at[1], size_s),
        (valid, valid_s),
    ]
    fetch(pairs, sems)
    write_grads(own_count(valid_s, 1), size_s, value_s, out)


def half_weights(valid, queries, fast, weights, own, live, valid_s, query_s, gate_s, up_s, sems):
    x, c = lax.axis_index("x"), lax.axis_index("c")
    start = c * HALF
    edge = pl.multiple_of(c * 256, 128)
    pairs = [
        (fast.at[:, pl.ds(edge, 384)], gate_s),
        (fast.at[:, pl.ds(WIDTH + edge, 384)], up_s),
        (valid, valid_s),
        (queries, query_s),
    ]
    row = lax.broadcasted_iota(jnp.int32, (HALF, 384), 0)
    col = lax.broadcasted_iota(jnp.int32, (HALF, 384), 1)
    wanted = row
    for i, shift in enumerate(SHIFTS):
        block = lax.rem(x + shift, NX)
        first = pl.multiple_of(start + block * UNITS, UNITS)
        source = fast.at[pl.ds(first, UNITS), pl.ds(2 * WIDTH, WIDTH)]
        pairs.append((source, weights.at[2, pl.ds(i * UNITS, UNITS)]))
        inside = (row >= i * UNITS) & (row < (i + 1) * UNITS)
        wanted = jnp.where(inside, first - edge + row - i * UNITS, wanted)
    chosen = jnp.where(col == wanted, 1.0, 0.0).astype(BF16)
    fetch(pairs, sems)
    for i, window in enumerate((gate_s, up_s)):
        weights[i] = dot(chosen, window[...], 1, 1).astype(BF16)
    for i in range(3):
        own[i * UNITS : (i + 1) * UNITS] = weights[i, :UNITS]
    row = lax.broadcasted_iota(jnp.int32, (ROWS, WIDTH), 0)
    for group in range(2):
        rows = query_s[group].astype(F32)
        live[group] = jnp.where(row < own_count(valid_s, group), rows, 0.0).astype(BF16)


def gradients(into, down, keys, grads):
    units = down.shape[0]
    pre = dot(into, keys, 1, 1)
    gate, up = pre[:units], pre[units:]
    d_hidden = dot(down, grads, 1, 1)
    sig = jax.nn.sigmoid(gate)
    hidden = (gate * sig * up).astype(BF16)
    d_up = (d_hidden * gate * sig).astype(BF16)
    d_gate = (d_hidden * up * sig * (1.0 + gate * (1.0 - sig))).astype(BF16)
    inner = dot(jnp.concatenate([d_gate, d_up], 0), keys).astype(BF16)
    return inner, dot(hidden, grads).astype(BF16)


def first_partial(weights, own, other, *outs):
    keys = jnp.concatenate([own[0], other[0]], 0)
    grads = jnp.concatenate([own[1], other[1]], 0)
    into = jnp.concatenate([weights[0], weights[1]], 0)
    inner, outer = gradients(into, weights[2], keys, grads)
    for i, out in enumerate(outs):
        rows = slice(i * UNITS, (i + 1) * UNITS)
        out[0:UNITS] = inner[rows]
        out[UNITS : 2 * UNITS] = inner[HALF:][rows]
        out[2 * UNITS :] = outer[rows]


def summed_x(*refs):
    blocks, out = refs[:-1], refs[-1]
    total = blocks[0][...].astype(F32)
    for block in blocks[1:]:
        total += block[...].astype(F32)
    out[0:PART] = total.astype(BF16)
    out[PART:] = jnp.zeros((PADDED - PART, WIDTH), BF16)


def summed(got, out):
    total = got[0].astype(F32)
    for i in range(1, NZ):
        total += got[i].astype(F32)
    total = total.astype(BF16)
    for i in range(NZ):
        out[i] = total


def statistics(weights, gradient, out):
    grad = gradient[...].astype(F32)
    old = weights[2 * UNITS :].astype(F32)
    down = grad[2 * UNITS : PART]
    squares = jnp.sum(grad * grad, 0, keepdims=True)
    lines = [
        jnp.sum(old * old, 0, keepdims=True),
        jnp.sum(old * down, 0, keepdims=True),
        jnp.sum(down * down, 0, keepdims=True),
        squares,
    ]
    lines = jnp.concatenate(lines + [jnp.zeros((4, WIDTH), F32)], 0)
    for i in range(2 * NX):
        out[i] = lines


def second_partial(weights, gradient, stats, *refs):
    blocks, fresh, out = refs[:-2], refs[-2], refs[-1]
    total = stats[0]
    for i in range(1, 2 * NX):
        total += stats[i]
    rate = rate_of(total[3:4])
    old = weights[...].astype(F32)
    moved = old - rate * gradient[:PART].astype(F32)
    old_in, moved_in = old[: 2 * UNITS], moved[: 2 * UNITS]
    ratio_in = jnp.sqrt(jnp.sum(old_in * old_in, 1, keepdims=True)) / jnp.sqrt(
        jnp.sum(moved_in * moved_in, 1, keepdims=True) + epsilon
    )
    ratio_out = ratio_of(rate, total[0:1], total[1:2], total[2:3])
    new = jnp.concatenate([moved_in * ratio_in, moved[2 * UNITS :] * ratio_out], 0).astype(BF16)
    fresh[...] = new
    keys = jnp.concatenate([b[0] for b in blocks], 0)
    grads = jnp.concatenate([b[1] for b in blocks], 0)
    inner, outer = gradients(new[: 2 * UNITS], new[2 * UNITS :], keys, grads)
    out[0 : 2 * UNITS] = inner
    out[2 * UNITS : PART] = outer
    out[PART:] = jnp.zeros((PADDED - PART, WIDTH), BF16)


def rate_of(squares):
    return RATE / jnp.sqrt(jnp.sum(squares, 1, keepdims=True) / COUNT + epsilon)


def ratio_of(rate, old, cross, grad):
    moved = jnp.maximum(old - 2.0 * rate * cross + rate * rate * grad, 0.0)
    return jnp.sqrt(old) / jnp.sqrt(moved + epsilon)


def respond(group, queries, others, into, down, mine, theirs):
    rows = jnp.concatenate([queries[group], others[group]], 0)
    pre = dot(rows, into, 1, 1)
    gate, up = pre[:, :HALF], pre[:, HALF:]
    hidden = (gate * jax.nn.sigmoid(gate) * up).astype(BF16)
    result = dot(hidden, down)
    mine[...] = result[:ROWS]
    theirs[...] = result[ROWS:].astype(BF16)


def first_answer(queries, others, *refs):
    blocks, (mine, theirs) = refs[:NX], refs[NX:]
    parts = [
        jnp.concatenate([b[i * UNITS : (i + 1) * UNITS] for b in blocks], 0) for i in range(3)
    ]
    respond(0, queries, others, jnp.concatenate(parts[:2], 0), parts[2], mine, theirs)


def sums(weights, gradient, inner):
    old, grad = weights[...].astype(F32), gradient[:PART].astype(F32)
    products = [old * old, old * grad, grad * grad]
    for i, product in enumerate(products):
        inner[i] = jnp.sum(product[: 2 * UNITS], 1, keepdims=True)
    lines = [jnp.sum(p[2 * UNITS :], 0, keepdims=True) for p in products]
    return jnp.concatenate(lines + [jnp.sum(products[2], 0, keepdims=True)], 0)


def early_sums(*refs):
    held, blocks, (inner, lines) = refs[:2], refs[2:4], refs[4:]
    lines[0:4] = sum(sums(held[i], blocks[i], inner.at[i]) for i in range(2))
    lines[4:] = jnp.zeros((4, WIDTH), F32)


def late_sums(early, *refs):
    held, blocks, (inner, lines) = refs[:2], refs[2:4], refs[4:]
    lines[0:4] = early[0:4] + sum(sums(held[i], blocks[i], inner.at[i]) for i in range(2))
    lines[4:] = jnp.zeros((4, WIDTH), F32)


def second_answer(queries, others, own_lines, other_lines, early_in, late_in, *refs):
    held, blocks, (mine, theirs, into, down) = refs[:NX], refs[NX : 2 * NX], refs[2 * NX :]
    lines = own_lines[...] + other_lines[...]
    rate = rate_of(lines[3:4])
    ratio_out = ratio_of(rate, lines[0:1], lines[1:2], lines[2:3])
    inner = [early_in.at[0], late_in.at[0], late_in.at[1], early_in.at[1]]
    for i, (weights, block) in enumerate(zip(held, blocks)):
        moved = weights[...].astype(F32) - rate * block[:PART].astype(F32)
        ratio_in = ratio_of(rate, inner[i][0], inner[i][1], inner[i][2])
        fresh = (moved[: 2 * UNITS] * ratio_in).astype(BF16)
        into[i * UNITS : (i + 1) * UNITS] = fresh[:UNITS]
        into[HALF + i * UNITS : HALF + (i + 1) * UNITS] = fresh[UNITS:]
        down[i * UNITS : (i + 1) * UNITS] = (moved[2 * UNITS :] * ratio_out).astype(BF16)
    respond(1, queries, others, into[...], down[...], mine, theirs)


def joined(one, two, other_one, other_two, out):
    for group, (mine, theirs) in enumerate(((one, other_one), (two, other_two))):
        out[group] = (mine[...] + theirs[...].astype(F32)).astype(BF16)


def shifted(value, axis, size, shift):
    return lax.ppermute(value, axis, [(i, (i + shift) % size) for i in range(size)])


def along_x(block):
    return [block] + [shifted(block, "x", NX, shift) for shift in SHIFTS[1:]]


def from_core(near):
    return [shifted(b, "c", 2, 1) for b in near]


def reduce_z(partial):
    got = lax.all_to_all(partial.reshape(NZ, PADDED // NZ, WIDTH), "z", 0, 0, tiled=True)
    return kernel_call(summed, shape(*got.shape), [VMEM])(got)


def gather_z(shards):
    return lax.all_to_all(shards, "z", 0, 0, tiled=True).reshape(PADDED, WIDTH)


def under_z(partial, block):
    near = along_x(block)
    shards, near[:3] = lax.optimization_barrier((reduce_z(partial), near[:3]))
    total, near[:3] = lax.optimization_barrier((gather_z(shards), near[:3]))
    return total, near


def body(queries, key_vectors, value_vectors, step_sizes, valid_rows, fast_init):
    held_inputs = (valid_rows, key_vectors[:, 0], value_vectors[:, 0], step_sizes)
    held_inputs += (queries[:, 0], fast_init[0])
    inputs = [pltpu.with_memory_space_constraint(i, pltpu.HBM) for i in held_inputs]
    pair, padded = shape(2, ROWS, WIDTH), shape(PADDED, WIDTH)
    scratch = [
        pltpu.SMEM(valid_rows.shape, jnp.int32),
        pltpu.VMEM((ROWS, WIDTH), BF16),
        pltpu.VMEM((1, ROWS), F32),
        pltpu.SemaphoreType.DMA((4,)),
    ]
    first = kernel_call(prepare_first, pair, [HBM] * 4, scratch)(*inputs[:4])
    other = shifted(first, "c", 2, 1)
    weights, own, queries = kernel_call(
        half_weights,
        (shape(3, HALF, WIDTH), shape(PART, WIDTH), pair),
        [HBM] * 3,
        [scratch[0], pltpu.VMEM(pair.shape, BF16)]
        + [pltpu.VMEM((WIDTH, 384), BF16)] * 2
        + [pltpu.SemaphoreType.DMA((8,))],
    )(inputs[0], *inputs[4:])
    others = shifted(queries, "c", 2, 1)
    parts = kernel_call(first_partial, (shape(PART, WIDTH),) * NX, [VMEM] * 3)(
        weights, first, other
    )
    parts = [parts[0]] + [shifted(p, "x", NX, s) for p, s in zip(parts[1:], SHIFTS[1:])]
    second = kernel_call(prepare_second, pair, [HBM] * 4, scratch)(*inputs[:4])
    *parts, second, others = lax.optimization_barrier((*parts, second, others))
    partial = kernel_call(summed_x, padded, [VMEM] * NX)(*parts)
    gradient, tokens = under_z(partial, second)
    far = from_core(tokens[:3])
    stats = kernel_call(statistics, shape(2 * NX, 8, WIDTH, dtype=F32), [VMEM] * 2)(
        own, gradient
    )
    stats, tokens[3], far = lax.optimization_barrier((stats, tokens[3], far))
    tokens += far + from_core(tokens[3:])
    stats = lax.all_to_all(stats, ("x", "c"), 0, 0, tiled=True)
    fresh, partial = kernel_call(second_partial, (shape(PART, WIDTH), padded), [VMEM] * 11)(
        own, gradient, stats, *tokens
    )
    gradient, held = under_z(partial, fresh)
    near = along_x(gradient)
    share = (shape(ROWS, WIDTH, dtype=F32), shape(ROWS, WIDTH))
    one, theirs = kernel_call(first_answer, share, [VMEM] * 6)(queries, others, *held)
    found = (shape(2, 3, 2 * UNITS, 1, dtype=F32), shape(8, WIDTH, dtype=F32))
    early, lines = kernel_call(early_sums, found, [VMEM] * 4)(held[0], held[3], near[0], near[3])
    other_one = shifted(theirs, "c", 2, 1)
    near[1], near[2], lines, other_one = lax.optimization_barrier(
        (near[1], near[2], lines, other_one)
    )
    late, lines = kernel_call(late_sums, found, [VMEM] * 5)(lines, *held[1:3], *near[1:3])
    two, theirs = kernel_call(
        second_answer,
        share,
        [VMEM] * 14,
        [pltpu.VMEM((WIDTH, WIDTH), BF16), pltpu.VMEM((HALF, WIDTH), BF16)],
    )(queries, others, lines, shifted(lines, "c", 2, 1), early, late, *held, *near)
    other_two = shifted(theirs, "c", 2, 1)
    out = kernel_call(joined, shape(2, ROWS, WIDTH), [VMEM] * 4)(one, two, other_one, other_two)
    return out[:, None]


def solution(mesh):
    split = Mesh(mesh.devices.reshape(mesh.shape["head"], NZ, NX, 2), ("head", "z", "x", "c"))
    seq = ("z", "x", "c")
    rows = P(None, "head", seq, None)
    placed = (rows, rows, rows, P(None, "head", seq), P(), P("head", None, None))
    return jax.shard_map(body, mesh=split, in_specs=placed, out_specs=rows, check_vma=False)
```

```python
import jax
import jax.numpy as jnp
from jax import lax
from jax.experimental import pallas as pl
from jax.experimental.pallas import tpu as pltpu
from jax.sharding import Mesh
from jax.sharding import PartitionSpec as P

step_factor = 0.5
epsilon = 1e-06
NX = 4
NZ = 8
ROWS = 128
WIDTH = 640
UNITS = 80
HALF = NX * UNITS
SHIFTS = (0, 1, 3, 2)
PART = 3 * UNITS
PADDED = 256
RATE = step_factor / WIDTH**0.5
COUNT = 3 * WIDTH * WIDTH
F32 = jnp.float32
BF16 = jnp.bfloat16
VMEM = pl.BlockSpec(memory_space=pltpu.VMEM)
HBM = pl.BlockSpec(memory_space=pltpu.HBM)


def dot(a, b, ca=1, cb=0):
    return lax.dot_general(a, b, (((ca,), (cb,)), ((), ())), preferred_element_type=F32)


def shape(*dims, dtype=BF16):
    return jax.ShapeDtypeStruct(dims, dtype)


def kernel_call(body, outs, ins, scratch=()):
    return pl.pallas_call(
        body,
        out_shape=outs,
        in_specs=ins,
        out_specs=jax.tree.map(lambda _: VMEM, outs),
        scratch_shapes=list(scratch),
        compiler_params=pltpu.CompilerParams(vmem_limit_bytes=20 * 1024 * 1024),
    )


def own_count(valid, group):
    rank = (lax.axis_index("z") * NX + lax.axis_index("x")) * 2 + lax.axis_index("c")
    return valid[group, rank]


def fetch(pairs, sems):
    copies = [pltpu.make_async_copy(src, dst, sems.at[i]) for i, (src, dst) in enumerate(pairs)]
    for copy in copies:
        copy.start()
    for copy in copies:
        copy.wait()


def write_grads(live_rows, sizes, values, out):
    row = lax.broadcasted_iota(jnp.int32, (ROWS, ROWS), 0)
    col = lax.broadcasted_iota(jnp.int32, (ROWS, ROWS), 1)
    size = jnp.sum(jnp.where(row == col, sizes[...], 0.0), 1, keepdims=True)
    scaled = jnp.where(row[:, :1] < live_rows, size, 0.0)
    out[1] = (-(scaled * values[...].astype(F32))).astype(BF16)


def prepare_first(
    valid, keys, values, sizes, fast, out, gate_w, up_w, down_w, valid_s, value_s, size_s, sems
):
    x, c = lax.axis_index("x"), lax.axis_index("c")
    edge = pl.multiple_of(c * 256, 128)
    pairs = [
        (keys.at[0], out.at[0]),
        (values.at[0], value_s),
        (sizes.at[0], size_s),
        (valid, valid_s),
        (fast.at[:, pl.ds(edge, 384)], gate_w),
        (fast.at[:, pl.ds(WIDTH + edge, 384)], up_w),
    ]
    for i, shift in enumerate(SHIFTS):
        first = pl.multiple_of(c * HALF + lax.rem(x + shift, NX) * UNITS, UNITS)
        source = fast.at[pl.ds(first, UNITS), pl.ds(2 * WIDTH, WIDTH)]
        pairs.append((source, down_w.at[pl.ds(i * UNITS, UNITS)]))
    fetch(pairs, sems)
    write_grads(own_count(valid_s, 0), size_s, value_s, out)


def prepare_second(valid, keys, values, sizes, out, valid_s, value_s, size_s, sems):
    pairs = [
        (keys.at[1], out.at[0]),
        (values.at[1], value_s),
        (sizes.at[1], size_s),
        (valid, valid_s),
    ]
    fetch(pairs, sems)
    write_grads(own_count(valid_s, 1), size_s, value_s, out)


def half_weights(valid, queries, gate_w, up_w, down_w, into, own, live, valid_s, query_s, sems):
    copies = [
        pltpu.make_async_copy(valid, valid_s, sems.at[0]),
        pltpu.make_async_copy(queries, query_s, sems.at[1]),
    ]
    for copy in copies:
        copy.start()
    x, c = lax.axis_index("x"), lax.axis_index("c")
    row = lax.broadcasted_iota(jnp.int32, (HALF, 384), 0)
    col = lax.broadcasted_iota(jnp.int32, (HALF, 384), 1)
    wanted = row
    for i, shift in enumerate(SHIFTS):
        first = c * (HALF - 256) + lax.rem(x + shift, NX) * UNITS
        inside = (row >= i * UNITS) & (row < (i + 1) * UNITS)
        wanted = jnp.where(inside, first + row - i * UNITS, wanted)
    chosen = jnp.where(col == wanted, 1.0, 0.0).astype(BF16)
    for i, window in enumerate((gate_w, up_w)):
        found = dot(chosen, window[...], 1, 1).astype(BF16)
        into[i * HALF : (i + 1) * HALF] = found
        own[i * UNITS : (i + 1) * UNITS] = found[:UNITS]
    own[2 * UNITS :] = down_w[:UNITS]
    for copy in copies:
        copy.wait()
    row = lax.broadcasted_iota(jnp.int32, (ROWS, WIDTH), 0)
    for group in range(2):
        rows = query_s[group].astype(F32)
        live[group] = jnp.where(row < own_count(valid_s, group), rows, 0.0).astype(BF16)


def gradients(into, down, keys, grads):
    units = down.shape[0]
    pre = dot(into, keys, 1, 1)
    gate, up = pre[:units], pre[units:]
    d_hidden = dot(down, grads, 1, 1)
    sig = jax.nn.sigmoid(gate)
    hidden = (gate * sig * up).astype(BF16)
    d_up = (d_hidden * gate * sig).astype(BF16)
    d_gate = (d_hidden * up * sig * (1.0 + gate * (1.0 - sig))).astype(BF16)
    inner = dot(jnp.concatenate([d_gate, d_up], 0), keys).astype(BF16)
    return inner, dot(hidden, grads).astype(BF16)


def first_partial(into, down, own, other, *outs):
    keys = jnp.concatenate([own[0], other[0]], 0)
    grads = jnp.concatenate([own[1], other[1]], 0)
    inner, outer = gradients(into[...], down[...], keys, grads)
    for i, out in enumerate(outs):
        rows = slice(i * UNITS, (i + 1) * UNITS)
        out[0:UNITS] = inner[rows]
        out[UNITS : 2 * UNITS] = inner[HALF:][rows]
        out[2 * UNITS :] = outer[rows]


def summed_x(*refs):
    blocks, out = refs[:-1], refs[-1]
    total = blocks[0][...].astype(F32)
    for block in blocks[1:]:
        total += block[...].astype(F32)
    out[0:PART] = total.astype(BF16)
    out[PART:] = jnp.zeros((PADDED - PART, WIDTH), BF16)


def summed(got, out):
    total = got[0].astype(F32)
    for i in range(1, NZ):
        total += got[i].astype(F32)
    total = total.astype(BF16)
    for i in range(NZ):
        out[i] = total


def statistics(weights, gradient, out):
    grad = gradient[...].astype(F32)
    old = weights[2 * UNITS :].astype(F32)
    down = grad[2 * UNITS : PART]
    squares = jnp.sum(grad * grad, 0, keepdims=True)
    lines = [
        jnp.sum(old * old, 0, keepdims=True),
        jnp.sum(old * down, 0, keepdims=True),
        jnp.sum(down * down, 0, keepdims=True),
        squares,
    ]
    lines = jnp.concatenate(lines + [jnp.zeros((4, WIDTH), F32)], 0)
    for i in range(2 * NX):
        out[i] = lines


def second_partial(weights, gradient, stats, *refs):
    blocks, fresh, out = refs[:-2], refs[-2], refs[-1]
    total = stats[0]
    for i in range(1, 2 * NX):
        total += stats[i]
    rate = rate_of(total[3:4])
    old = weights[...].astype(F32)
    moved = old - rate * gradient[:PART].astype(F32)
    old_in, moved_in = old[: 2 * UNITS], moved[: 2 * UNITS]
    ratio_in = jnp.sqrt(jnp.sum(old_in * old_in, 1, keepdims=True)) / jnp.sqrt(
        jnp.sum(moved_in * moved_in, 1, keepdims=True) + epsilon
    )
    ratio_out = ratio_of(rate, total[0:1], total[1:2], total[2:3])
    new = jnp.concatenate([moved_in * ratio_in, moved[2 * UNITS :] * ratio_out], 0).astype(BF16)
    fresh[...] = new
    keys = jnp.concatenate([b[0] for b in blocks], 0)
    grads = jnp.concatenate([b[1] for b in blocks], 0)
    inner, outer = gradients(new[: 2 * UNITS], new[2 * UNITS :], keys, grads)
    out[0 : 2 * UNITS] = inner
    out[2 * UNITS : PART] = outer
    out[PART:] = jnp.zeros((PADDED - PART, WIDTH), BF16)


def rate_of(squares):
    return RATE / jnp.sqrt(jnp.sum(squares, 1, keepdims=True) / COUNT + epsilon)


def ratio_of(rate, old, cross, grad):
    moved = jnp.maximum(old - 2.0 * rate * cross + rate * rate * grad, 0.0)
    return jnp.sqrt(old) / jnp.sqrt(moved + epsilon)


def respond(group, queries, others, into, down, mine, theirs):
    rows = jnp.concatenate([queries[group], others[group]], 0)
    pre = dot(rows, into, 1, 1)
    gate, up = pre[:, :HALF], pre[:, HALF:]
    hidden = (gate * jax.nn.sigmoid(gate) * up).astype(BF16)
    result = dot(hidden, down)
    mine[...] = result[:ROWS]
    theirs[...] = result[ROWS:].astype(BF16)


def first_answer(queries, others, *refs):
    blocks, (mine, theirs) = refs[:NX], refs[NX:]
    parts = [
        jnp.concatenate([b[i * UNITS : (i + 1) * UNITS] for b in blocks], 0) for i in range(3)
    ]
    respond(0, queries, others, jnp.concatenate(parts[:2], 0), parts[2], mine, theirs)


def sums(weights, gradient, inner):
    old, grad = weights[...].astype(F32), gradient[:PART].astype(F32)
    products = [old * old, old * grad, grad * grad]
    for i, product in enumerate(products):
        inner[i] = jnp.sum(product[: 2 * UNITS], 1, keepdims=True)
    lines = [jnp.sum(p[2 * UNITS :], 0, keepdims=True) for p in products]
    return jnp.concatenate(lines + [jnp.sum(products[2], 0, keepdims=True)], 0)


def early_sums(*refs):
    held, blocks, (inner, lines) = refs[:2], refs[2:4], refs[4:]
    lines[0:4] = sum(sums(held[i], blocks[i], inner.at[i]) for i in range(2))
    lines[4:] = jnp.zeros((4, WIDTH), F32)


def late_sums(early, *refs):
    held, blocks, (inner, lines) = refs[:2], refs[2:4], refs[4:]
    lines[0:4] = early[0:4] + sum(sums(held[i], blocks[i], inner.at[i]) for i in range(2))
    lines[4:] = jnp.zeros((4, WIDTH), F32)


def second_answer(queries, others, own_lines, other_lines, early_in, late_in, *refs):
    held, blocks, (mine, theirs, into, down) = refs[:NX], refs[NX : 2 * NX], refs[2 * NX :]
    lines = own_lines[...] + other_lines[...]
    rate = rate_of(lines[3:4])
    ratio_out = ratio_of(rate, lines[0:1], lines[1:2], lines[2:3])
    inner = [early_in.at[0], late_in.at[0], late_in.at[1], early_in.at[1]]
    for i, (weights, block) in enumerate(zip(held, blocks)):
        moved = weights[...].astype(F32) - rate * block[:PART].astype(F32)
        ratio_in = ratio_of(rate, inner[i][0], inner[i][1], inner[i][2])
        fresh = (moved[: 2 * UNITS] * ratio_in).astype(BF16)
        into[i * UNITS : (i + 1) * UNITS] = fresh[:UNITS]
        into[HALF + i * UNITS : HALF + (i + 1) * UNITS] = fresh[UNITS:]
        down[i * UNITS : (i + 1) * UNITS] = (moved[2 * UNITS :] * ratio_out).astype(BF16)
    respond(1, queries, others, into[...], down[...], mine, theirs)


def joined(one, two, other_one, other_two, out):
    for group, (mine, theirs) in enumerate(((one, other_one), (two, other_two))):
        out[group] = (mine[...] + theirs[...].astype(F32)).astype(BF16)


def shifted(value, axis, size, shift):
    return lax.ppermute(value, axis, [(i, (i + shift) % size) for i in range(size)])


def along_x(block):
    return [block] + [shifted(block, "x", NX, shift) for shift in SHIFTS[1:]]


def from_core(near):
    return [shifted(b, "c", 2, 1) for b in near]


def reduce_z(partial):
    got = lax.all_to_all(partial.reshape(NZ, PADDED // NZ, WIDTH), "z", 0, 0, tiled=True)
    return kernel_call(summed, shape(*got.shape), [VMEM])(got)


def gather_z(shards):
    return lax.all_to_all(shards, "z", 0, 0, tiled=True).reshape(PADDED, WIDTH)


def under_z(partial, block):
    near = along_x(block)
    shards, near[:3] = lax.optimization_barrier((reduce_z(partial), near[:3]))
    return lax.optimization_barrier((gather_z(shards), near))


def body(queries, key_vectors, value_vectors, step_sizes, valid_rows, fast_init):
    held_inputs = (valid_rows, key_vectors[:, 0], value_vectors[:, 0], step_sizes)
    held_inputs += (queries[:, 0], fast_init[0])
    inputs = [pltpu.with_memory_space_constraint(i, pltpu.HBM) for i in held_inputs]
    pair, padded = shape(2, ROWS, WIDTH), shape(PADDED, WIDTH)
    scratch = [
        pltpu.SMEM(valid_rows.shape, jnp.int32),
        pltpu.VMEM((ROWS, WIDTH), BF16),
        pltpu.VMEM((1, ROWS), F32),
    ]
    window = shape(WIDTH, 384)
    first, *windows = kernel_call(
        prepare_first,
        (pair, window, window, shape(HALF, WIDTH)),
        [HBM] * 5,
        scratch + [pltpu.SemaphoreType.DMA((10,))],
    )(*inputs[:4], inputs[5])
    other = shifted(first, "c", 2, 1)
    into, own, queries = kernel_call(
        half_weights,
        (shape(2 * HALF, WIDTH), shape(PART, WIDTH), pair),
        [HBM] * 2 + [VMEM] * 3,
        [scratch[0], pltpu.VMEM(pair.shape, BF16), pltpu.SemaphoreType.DMA((2,))],
    )(inputs[0], inputs[4], *windows)
    others = shifted(queries, "c", 2, 1)
    parts = kernel_call(first_partial, (shape(PART, WIDTH),) * NX, [VMEM] * 4)(
        into, windows[2], first, other
    )
    parts = [parts[0]] + [shifted(p, "x", NX, s) for p, s in zip(parts[1:], SHIFTS[1:])]
    scratch += [pltpu.SemaphoreType.DMA((4,))]
    second = kernel_call(prepare_second, pair, [HBM] * 4, scratch)(*inputs[:4])
    *parts, second, others = lax.optimization_barrier((*parts, second, others))
    partial = kernel_call(summed_x, padded, [VMEM] * NX)(*parts)
    gradient, tokens = under_z(partial, second)
    tokens += from_core(tokens)
    stats = kernel_call(statistics, shape(2 * NX, 8, WIDTH, dtype=F32), [VMEM] * 2)(
        own, gradient
    )
    stats = lax.all_to_all(stats, ("x", "c"), 0, 0, tiled=True)
    fresh, partial = kernel_call(second_partial, (shape(PART, WIDTH), padded), [VMEM] * 11)(
        own, gradient, stats, *tokens
    )
    gradient, held = under_z(partial, fresh)
    gradient = gradient[:PART]
    near = along_x(gradient)
    share = (shape(ROWS, WIDTH, dtype=F32), shape(ROWS, WIDTH))
    one, theirs = kernel_call(first_answer, share, [VMEM] * 6)(queries, others, *held)
    found = (shape(2, 3, 2 * UNITS, 1, dtype=F32), shape(8, WIDTH, dtype=F32))
    early, lines = kernel_call(early_sums, found, [VMEM] * 4)(held[0], held[3], near[0], near[3])
    other_one = shifted(theirs, "c", 2, 1)
    near[1], near[2], lines, other_one = lax.optimization_barrier(
        (near[1], near[2], lines, other_one)
    )
    late, lines = kernel_call(late_sums, found, [VMEM] * 5)(lines, *held[1:3], *near[1:3])
    two, theirs = kernel_call(
        second_answer,
        share,
        [VMEM] * 14,
        [pltpu.VMEM((WIDTH, WIDTH), BF16), pltpu.VMEM((HALF, WIDTH), BF16)],
    )(queries, others, lines, shifted(lines, "c", 2, 1), early, late, *held, *near)
    other_two = shifted(theirs, "c", 2, 1)
    out = kernel_call(joined, shape(2, ROWS, WIDTH), [VMEM] * 4)(one, two, other_one, other_two)
    return out[:, None]


def solution(mesh):
    split = Mesh(mesh.devices.reshape(mesh.shape["head"], NZ, NX, 2), ("head", "z", "x", "c"))
    seq = ("z", "x", "c")
    rows = P(None, "head", seq, None)
    placed = (rows, rows, rows, P(None, "head", seq), P(), P("head", None, None))
    return jax.shard_map(body, mesh=split, in_specs=placed, out_specs=rows, check_vma=False)
```

```python
import jax
import jax.numpy as jnp
from jax import lax
from jax.experimental import pallas as pl
from jax.experimental.pallas import tpu as pltpu
from jax.sharding import Mesh
from jax.sharding import PartitionSpec as P

step_factor = 0.5
epsilon = 1e-06
NX = 4
NZ = 8
ROWS = 128
WIDTH = 640
UNITS = 80
HALF = NX * UNITS
SHIFTS = (0, 1, 3, 2)
PART = 3 * UNITS
PADDED = 256
RATE = step_factor / WIDTH**0.5
COUNT = 3 * WIDTH * WIDTH
F32 = jnp.float32
BF16 = jnp.bfloat16
VMEM = pl.BlockSpec(memory_space=pltpu.VMEM)
HBM = pl.BlockSpec(memory_space=pltpu.HBM)


def dot(a, b, ca=1, cb=0):
    return lax.dot_general(a, b, (((ca,), (cb,)), ((), ())), preferred_element_type=F32)


def shape(*dims, dtype=BF16):
    return jax.ShapeDtypeStruct(dims, dtype)


def kernel_call(body, outs, ins, scratch=()):
    return pl.pallas_call(
        body,
        out_shape=outs,
        in_specs=ins,
        out_specs=jax.tree.map(lambda _: VMEM, outs),
        scratch_shapes=list(scratch),
        compiler_params=pltpu.CompilerParams(vmem_limit_bytes=20 * 1024 * 1024),
    )


def own_count(valid, group):
    rank = (lax.axis_index("z") * NX + lax.axis_index("x")) * 2 + lax.axis_index("c")
    return valid[group, rank]


def fetch(pairs, sems):
    copies = [pltpu.make_async_copy(src, dst, sems.at[i]) for i, (src, dst) in enumerate(pairs)]
    for copy in copies:
        copy.start()
    for copy in copies:
        copy.wait()


def write_grads(live_rows, sizes, values, out):
    row = lax.broadcasted_iota(jnp.int32, (ROWS, ROWS), 0)
    col = lax.broadcasted_iota(jnp.int32, (ROWS, ROWS), 1)
    size = jnp.sum(jnp.where(row == col, sizes[...], 0.0), 1, keepdims=True)
    scaled = jnp.where(row[:, :1] < live_rows, size, 0.0)
    out[1] = (-(scaled * values[...].astype(F32))).astype(BF16)


def prepare_first(
    valid, keys, values, sizes, fast, out, gate_w, up_w, down_w, valid_s, value_s, size_s, sems
):
    x, c = lax.axis_index("x"), lax.axis_index("c")
    edge = pl.multiple_of(c * 256, 128)
    pairs = [
        (keys.at[0], out.at[0]),
        (values.at[0], value_s),
        (sizes.at[0], size_s),
        (valid, valid_s),
        (fast.at[:, pl.ds(edge, 384)], gate_w),
        (fast.at[:, pl.ds(WIDTH + edge, 384)], up_w),
    ]
    for i, shift in enumerate(SHIFTS):
        first = pl.multiple_of(c * HALF + lax.rem(x + shift, NX) * UNITS, UNITS)
        source = fast.at[pl.ds(first, UNITS), pl.ds(2 * WIDTH, WIDTH)]
        pairs.append((source, down_w.at[pl.ds(i * UNITS, UNITS)]))
    fetch(pairs, sems)
    write_grads(own_count(valid_s, 0), size_s, value_s, out)


def prepare_second(valid, keys, values, sizes, out, valid_s, value_s, size_s, sems):
    pairs = [
        (keys.at[1], out.at[0]),
        (values.at[1], value_s),
        (sizes.at[1], size_s),
        (valid, valid_s),
    ]
    fetch(pairs, sems)
    write_grads(own_count(valid_s, 1), size_s, value_s, out)


def half_weights(valid, queries, gate_w, up_w, down_w, into, own, live, valid_s, query_s, sems):
    copies = [
        pltpu.make_async_copy(valid, valid_s, sems.at[0]),
        pltpu.make_async_copy(queries, query_s, sems.at[1]),
    ]
    for copy in copies:
        copy.start()
    x, c = lax.axis_index("x"), lax.axis_index("c")
    row = lax.broadcasted_iota(jnp.int32, (HALF, 384), 0)
    col = lax.broadcasted_iota(jnp.int32, (HALF, 384), 1)
    wanted = row
    for i, shift in enumerate(SHIFTS):
        first = c * (HALF - 256) + lax.rem(x + shift, NX) * UNITS
        inside = (row >= i * UNITS) & (row < (i + 1) * UNITS)
        wanted = jnp.where(inside, first + row - i * UNITS, wanted)
    chosen = jnp.where(col == wanted, 1.0, 0.0).astype(BF16)
    for i, window in enumerate((gate_w, up_w)):
        found = dot(chosen, window[...], 1, 1).astype(BF16)
        into[i * HALF : (i + 1) * HALF] = found
        own[i * UNITS : (i + 1) * UNITS] = found[:UNITS]
    own[2 * UNITS :] = down_w[:UNITS]
    for copy in copies:
        copy.wait()
    row = lax.broadcasted_iota(jnp.int32, (ROWS, WIDTH), 0)
    for group in range(2):
        rows = query_s[group].astype(F32)
        live[group] = jnp.where(row < own_count(valid_s, group), rows, 0.0).astype(BF16)


def gradients(into, down, keys, grads):
    units = down.shape[0]
    pre = dot(into, keys, 1, 1)
    gate, up = pre[:units], pre[units:]
    d_hidden = dot(down, grads, 1, 1)
    sig = jax.nn.sigmoid(gate)
    hidden = (gate * sig * up).astype(BF16)
    d_up = (d_hidden * gate * sig).astype(BF16)
    d_gate = (d_hidden * up * sig * (1.0 + gate * (1.0 - sig))).astype(BF16)
    inner = dot(jnp.concatenate([d_gate, d_up], 0), keys).astype(BF16)
    return inner, dot(hidden, grads).astype(BF16)


def first_partial(into, down, own, other, *outs):
    keys = jnp.concatenate([own[0], other[0]], 0)
    grads = jnp.concatenate([own[1], other[1]], 0)
    inner, outer = gradients(into[...], down[...], keys, grads)
    for i, out in enumerate(outs):
        rows = slice(i * UNITS, (i + 1) * UNITS)
        out[0:UNITS] = inner[rows]
        out[UNITS : 2 * UNITS] = inner[HALF:][rows]
        out[2 * UNITS :] = outer[rows]


def summed_x(*refs):
    blocks, out = refs[:-1], refs[-1]
    total = blocks[0][...].astype(F32)
    for block in blocks[1:]:
        total += block[...].astype(F32)
    out[0:PART] = total.astype(BF16)
    out[PART:] = jnp.zeros((PADDED - PART, WIDTH), BF16)


def summed(got, out):
    total = got[0].astype(F32)
    for i in range(1, NZ):
        total += got[i].astype(F32)
    total = total.astype(BF16)
    for i in range(NZ):
        out[i] = total


def statistics(weights, gradient, out):
    grad = gradient[...].astype(F32)
    old = weights[2 * UNITS :].astype(F32)
    down = grad[2 * UNITS : PART]
    lines = [old * old, old * down, down * down, grad * grad]
    lines = jnp.concatenate([jnp.sum(line, 0, keepdims=True) for line in lines], 0)
    for i in range(2 * NX):
        out[i] = lines


def second_partial(weights, gradient, stats, *refs):
    blocks, fresh, out = refs[:-2], refs[-2], refs[-1]
    total = stats[0]
    for i in range(1, 2 * NX):
        total += stats[i]
    rate = rate_of(total[3:4])
    old = weights[...].astype(F32)
    moved = old - rate * gradient[:PART].astype(F32)
    old_in, moved_in = old[: 2 * UNITS], moved[: 2 * UNITS]
    ratio_in = jnp.sqrt(jnp.sum(old_in * old_in, 1, keepdims=True)) / jnp.sqrt(
        jnp.sum(moved_in * moved_in, 1, keepdims=True) + epsilon
    )
    ratio_out = ratio_of(rate, total[0:1], total[1:2], total[2:3])
    new = jnp.concatenate([moved_in * ratio_in, moved[2 * UNITS :] * ratio_out], 0).astype(BF16)
    fresh[...] = new
    keys = jnp.concatenate([b[0] for b in blocks], 0)
    grads = jnp.concatenate([b[1] for b in blocks], 0)
    inner, outer = gradients(new[: 2 * UNITS], new[2 * UNITS :], keys, grads)
    out[0 : 2 * UNITS] = inner
    out[2 * UNITS : PART] = outer
    out[PART:] = jnp.zeros((PADDED - PART, WIDTH), BF16)


def rate_of(squares):
    return RATE / jnp.sqrt(jnp.sum(squares, 1, keepdims=True) / COUNT + epsilon)


def ratio_of(rate, old, cross, grad):
    moved = jnp.maximum(old - 2.0 * rate * cross + rate * rate * grad, 0.0)
    return jnp.sqrt(old) / jnp.sqrt(moved + epsilon)


def respond(group, queries, others, into, down, mine, theirs):
    rows = jnp.concatenate([queries[group], others[group]], 0)
    pre = dot(rows, into, 1, 1)
    gate, up = pre[:, :HALF], pre[:, HALF:]
    hidden = (gate * jax.nn.sigmoid(gate) * up).astype(BF16)
    result = dot(hidden, down)
    mine[...] = result[:ROWS]
    theirs[...] = result[ROWS:].astype(BF16)


def first_answer(queries, others, *refs):
    blocks, (mine, theirs) = refs[:NX], refs[NX:]
    parts = [
        jnp.concatenate([b[i * UNITS : (i + 1) * UNITS] for b in blocks], 0) for i in range(3)
    ]
    respond(0, queries, others, jnp.concatenate(parts[:2], 0), parts[2], mine, theirs)


def sums(weights, gradient, inner):
    old, grad = weights[...].astype(F32), gradient[:PART].astype(F32)
    products = [old * old, old * grad, grad * grad]
    for i, product in enumerate(products):
        inner[i] = jnp.sum(product[: 2 * UNITS], 1, keepdims=True)
    lines = [jnp.sum(p[2 * UNITS :], 0, keepdims=True) for p in products]
    return jnp.concatenate(lines + [jnp.sum(products[2], 0, keepdims=True)], 0)


def early_sums(*refs):
    held, blocks, (inner, lines) = refs[:2], refs[2:4], refs[4:]
    lines[0:4] = sum(sums(held[i], blocks[i], inner.at[i]) for i in range(2))
    lines[4:] = jnp.zeros((4, WIDTH), F32)


def late_sums(early, *refs):
    held, blocks, (inner, lines) = refs[:2], refs[2:4], refs[4:]
    lines[0:4] = early[0:4] + sum(sums(held[i], blocks[i], inner.at[i]) for i in range(2))
    lines[4:] = jnp.zeros((4, WIDTH), F32)


def second_answer(queries, others, own_lines, other_lines, early_in, late_in, *refs):
    held, blocks, (mine, theirs, into, down) = refs[:NX], refs[NX : 2 * NX], refs[2 * NX :]
    lines = own_lines[...] + other_lines[...]
    rate = rate_of(lines[3:4])
    ratio_out = ratio_of(rate, lines[0:1], lines[1:2], lines[2:3])
    inner = [early_in.at[0], late_in.at[0], late_in.at[1], early_in.at[1]]
    for i, (weights, block) in enumerate(zip(held, blocks)):
        moved = weights[...].astype(F32) - rate * block[:PART].astype(F32)
        ratio_in = ratio_of(rate, inner[i][0], inner[i][1], inner[i][2])
        fresh = (moved[: 2 * UNITS] * ratio_in).astype(BF16)
        into[i * UNITS : (i + 1) * UNITS] = fresh[:UNITS]
        into[HALF + i * UNITS : HALF + (i + 1) * UNITS] = fresh[UNITS:]
        down[i * UNITS : (i + 1) * UNITS] = (moved[2 * UNITS :] * ratio_out).astype(BF16)
    respond(1, queries, others, into[...], down[...], mine, theirs)


def joined(one, two, other_one, other_two, out):
    for group, (mine, theirs) in enumerate(((one, other_one), (two, other_two))):
        out[group] = (mine[...] + theirs[...].astype(F32)).astype(BF16)


def shifted(value, axis, size, shift):
    return lax.ppermute(value, axis, [(i, (i + shift) % size) for i in range(size)])


def along_x(block):
    return [block] + [shifted(block, "x", NX, shift) for shift in SHIFTS[1:]]


def from_core(near):
    return [shifted(b, "c", 2, 1) for b in near]


def reduce_z(partial):
    got = lax.all_to_all(partial.reshape(NZ, PADDED // NZ, WIDTH), "z", 0, 0, tiled=True)
    return kernel_call(summed, shape(*got.shape), [VMEM])(got)


def gather_z(shards):
    return lax.all_to_all(shards, "z", 0, 0, tiled=True).reshape(PADDED, WIDTH)


def under_z(partial, block):
    near = along_x(block)
    shards, near[:3] = lax.optimization_barrier((reduce_z(partial), near[:3]))
    return lax.optimization_barrier((gather_z(shards), near))


def body(queries, key_vectors, value_vectors, step_sizes, valid_rows, fast_init):
    held_inputs = (valid_rows, key_vectors[:, 0], value_vectors[:, 0], step_sizes)
    held_inputs += (queries[:, 0], fast_init[0])
    inputs = [pltpu.with_memory_space_constraint(i, pltpu.HBM) for i in held_inputs]
    pair, padded = shape(2, ROWS, WIDTH), shape(PADDED, WIDTH)
    scratch = [
        pltpu.SMEM(valid_rows.shape, jnp.int32),
        pltpu.VMEM((ROWS, WIDTH), BF16),
        pltpu.VMEM((1, ROWS), F32),
    ]
    window = shape(WIDTH, 384)
    first, *windows = kernel_call(
        prepare_first,
        (pair, window, window, shape(HALF, WIDTH)),
        [HBM] * 5,
        scratch + [pltpu.SemaphoreType.DMA((10,))],
    )(*inputs[:4], inputs[5])
    other = shifted(first, "c", 2, 1)
    into, own, queries = kernel_call(
        half_weights,
        (shape(2 * HALF, WIDTH), shape(PART, WIDTH), pair),
        [HBM] * 2 + [VMEM] * 3,
        [scratch[0], pltpu.VMEM(pair.shape, BF16), pltpu.SemaphoreType.DMA((2,))],
    )(inputs[0], inputs[4], *windows)
    others = shifted(queries, "c", 2, 1)
    parts = kernel_call(first_partial, (shape(PART, WIDTH),) * NX, [VMEM] * 4)(
        into, windows[2], first, other
    )
    parts = [parts[0]] + [shifted(p, "x", NX, s) for p, s in zip(parts[1:], SHIFTS[1:])]
    scratch += [pltpu.SemaphoreType.DMA((4,))]
    second = kernel_call(prepare_second, pair, [HBM] * 4, scratch)(*inputs[:4])
    *parts, second, others = lax.optimization_barrier((*parts, second, others))
    partial = kernel_call(summed_x, padded, [VMEM] * NX)(*parts)
    gradient, tokens = under_z(partial, second)
    tokens += from_core(tokens)
    stats = kernel_call(statistics, shape(2 * NX, 4, WIDTH, dtype=F32), [VMEM] * 2)(
        own, gradient
    )
    stats = lax.all_to_all(stats, ("x", "c"), 0, 0, tiled=True)
    fresh, partial = kernel_call(second_partial, (shape(PART, WIDTH), padded), [VMEM] * 11)(
        own, gradient, stats, *tokens
    )
    gradient, held = under_z(partial, fresh)
    gradient = gradient[:PART]
    near = along_x(gradient)
    share = (shape(ROWS, WIDTH, dtype=F32), shape(ROWS, WIDTH))
    one, theirs = kernel_call(first_answer, share, [VMEM] * 6)(queries, others, *held)
    found = (shape(2, 3, 2 * UNITS, 1, dtype=F32), shape(8, WIDTH, dtype=F32))
    early, lines = kernel_call(early_sums, found, [VMEM] * 4)(held[0], held[3], near[0], near[3])
    other_one = shifted(theirs, "c", 2, 1)
    near[1], near[2], lines, other_one = lax.optimization_barrier(
        (near[1], near[2], lines, other_one)
    )
    late, lines = kernel_call(late_sums, found, [VMEM] * 5)(lines, *held[1:3], *near[1:3])
    two, theirs = kernel_call(
        second_answer,
        share,
        [VMEM] * 14,
        [pltpu.VMEM((WIDTH, WIDTH), BF16), pltpu.VMEM((HALF, WIDTH), BF16)],
    )(queries, others, lines, shifted(lines, "c", 2, 1), early, late, *held, *near)
    other_two = shifted(theirs, "c", 2, 1)
    out = kernel_call(joined, shape(2, ROWS, WIDTH), [VMEM] * 4)(one, two, other_one, other_two)
    return out[:, None]


def solution(mesh):
    split = Mesh(mesh.devices.reshape(mesh.shape["head"], NZ, NX, 2), ("head", "z", "x", "c"))
    seq = ("z", "x", "c")
    rows = P(None, "head", seq, None)
    placed = (rows, rows, rows, P(None, "head", seq), P(), P("head", None, None))
    return jax.shard_map(body, mesh=split, in_specs=placed, out_specs=rows, check_vma=False)
```

```python
import jax
import jax.numpy as jnp
from jax import lax
from jax.experimental import pallas as pl
from jax.experimental.pallas import tpu as pltpu
from jax.sharding import Mesh
from jax.sharding import PartitionSpec as P

step_factor = 0.5
epsilon = 1e-06
NX = 4
NZ = 8
ROWS = 128
WIDTH = 640
UNITS = 80
HALF = NX * UNITS
SHIFTS = (0, 1, 3, 2)
PART = 3 * UNITS
PADDED = 256
RATE = step_factor / WIDTH**0.5
COUNT = 3 * WIDTH * WIDTH
F32 = jnp.float32
BF16 = jnp.bfloat16
VMEM = pl.BlockSpec(memory_space=pltpu.VMEM)
HBM = pl.BlockSpec(memory_space=pltpu.HBM)


def dot(a, b, ca=1, cb=0):
    return lax.dot_general(a, b, (((ca,), (cb,)), ((), ())), preferred_element_type=F32)


def shape(*dims, dtype=BF16):
    return jax.ShapeDtypeStruct(dims, dtype)


def kernel_call(body, outs, ins, scratch=()):
    return pl.pallas_call(
        body,
        out_shape=outs,
        in_specs=ins,
        out_specs=jax.tree.map(lambda _: VMEM, outs),
        scratch_shapes=list(scratch),
        compiler_params=pltpu.CompilerParams(vmem_limit_bytes=20 * 1024 * 1024),
    )


def own_count(valid, group):
    rank = (lax.axis_index("z") * NX + lax.axis_index("x")) * 2 + lax.axis_index("c")
    return valid[group, rank]


def fetch(pairs, sems):
    copies = [pltpu.make_async_copy(src, dst, sems.at[i]) for i, (src, dst) in enumerate(pairs)]
    for copy in copies:
        copy.start()
    for copy in copies:
        copy.wait()


def write_grads(live_rows, sizes, values, out):
    row = lax.broadcasted_iota(jnp.int32, (ROWS, ROWS), 0)
    col = lax.broadcasted_iota(jnp.int32, (ROWS, ROWS), 1)
    size = jnp.sum(jnp.where(row == col, sizes[...], 0.0), 1, keepdims=True)
    scaled = jnp.where(row[:, :1] < live_rows, size, 0.0)
    out[1] = (-(scaled * values[...].astype(F32))).astype(BF16)


def prepare_first(
    valid, keys, values, sizes, fast, out, gate_w, up_w, down_w, valid_s, value_s, size_s, sems
):
    x, c = lax.axis_index("x"), lax.axis_index("c")
    edge = pl.multiple_of(c * 256, 128)
    pairs = [
        (keys.at[0], out.at[0]),
        (values.at[0], value_s),
        (sizes.at[0], size_s),
        (valid, valid_s),
        (fast.at[:, pl.ds(edge, 384)], gate_w),
        (fast.at[:, pl.ds(WIDTH + edge, 384)], up_w),
    ]
    for i, shift in enumerate(SHIFTS):
        first = pl.multiple_of(c * HALF + lax.rem(x + shift, NX) * UNITS, UNITS)
        source = fast.at[pl.ds(first, UNITS), pl.ds(2 * WIDTH, WIDTH)]
        pairs.append((source, down_w.at[pl.ds(i * UNITS, UNITS)]))
    fetch(pairs, sems)
    write_grads(own_count(valid_s, 0), size_s, value_s, out)


def prepare_second(valid, keys, values, sizes, out, valid_s, value_s, size_s, sems):
    pairs = [
        (keys.at[1], out.at[0]),
        (values.at[1], value_s),
        (sizes.at[1], size_s),
        (valid, valid_s),
    ]
    fetch(pairs, sems)
    write_grads(own_count(valid_s, 1), size_s, value_s, out)


def half_weights(valid, queries, gate_w, up_w, down_w, into, own, live, valid_s, query_s, sems):
    copies = [
        pltpu.make_async_copy(valid, valid_s, sems.at[0]),
        pltpu.make_async_copy(queries, query_s, sems.at[1]),
    ]
    for copy in copies:
        copy.start()
    x, c = lax.axis_index("x"), lax.axis_index("c")
    row = lax.broadcasted_iota(jnp.int32, (HALF, 384), 0)
    col = lax.broadcasted_iota(jnp.int32, (HALF, 384), 1)
    wanted = row
    for i, shift in enumerate(SHIFTS):
        first = c * (HALF - 256) + lax.rem(x + shift, NX) * UNITS
        inside = (row >= i * UNITS) & (row < (i + 1) * UNITS)
        wanted = jnp.where(inside, first + row - i * UNITS, wanted)
    chosen = jnp.where(col == wanted, 1.0, 0.0).astype(BF16)
    for i, window in enumerate((gate_w, up_w)):
        found = dot(chosen, window[...], 1, 1).astype(BF16)
        into[i * HALF : (i + 1) * HALF] = found
        own[i * UNITS : (i + 1) * UNITS] = found[:UNITS]
    own[2 * UNITS :] = down_w[:UNITS]
    for copy in copies:
        copy.wait()
    row = lax.broadcasted_iota(jnp.int32, (ROWS, WIDTH), 0)
    for group in range(2):
        rows = query_s[group].astype(F32)
        live[group] = jnp.where(row < own_count(valid_s, group), rows, 0.0).astype(BF16)


def gradients(into, down, keys, grads):
    units = down.shape[0]
    pre = dot(into, keys, 1, 1)
    gate, up = pre[:units], pre[units:]
    d_hidden = dot(down, grads, 1, 1)
    sig = jax.nn.sigmoid(gate)
    hidden = (gate * sig * up).astype(BF16)
    d_up = (d_hidden * gate * sig).astype(BF16)
    d_gate = (d_hidden * up * sig * (1.0 + gate * (1.0 - sig))).astype(BF16)
    inner = dot(jnp.concatenate([d_gate, d_up], 0), keys).astype(BF16)
    return inner, dot(hidden, grads).astype(BF16)


def first_partial(into, down, own, other, *outs):
    keys = jnp.concatenate([own[0], other[0]], 0)
    grads = jnp.concatenate([own[1], other[1]], 0)
    inner, outer = gradients(into[...], down[...], keys, grads)
    for i, out in enumerate(outs):
        rows = slice(i * UNITS, (i + 1) * UNITS)
        out[0:UNITS] = inner[rows]
        out[UNITS : 2 * UNITS] = inner[HALF:][rows]
        out[2 * UNITS :] = outer[rows]


def summed_x(*refs):
    blocks, out = refs[:-1], refs[-1]
    total = blocks[0][...].astype(F32)
    for block in blocks[1:]:
        total += block[...].astype(F32)
    out[0:PART] = total.astype(BF16)
    out[PART:] = jnp.zeros((PADDED - PART, WIDTH), BF16)


def summed(got, out):
    total = got[0].astype(F32)
    for i in range(1, NZ):
        total += got[i].astype(F32)
    total = total.astype(BF16)
    for i in range(NZ):
        out[i] = total


def statistics(weights, gradient, out):
    grad = gradient[...].astype(F32)
    old = weights[2 * UNITS :].astype(F32)
    down = grad[2 * UNITS : PART]
    lines = [old * old, old * down, down * down, grad * grad]
    lines = jnp.concatenate([jnp.sum(line, 0, keepdims=True) for line in lines], 0)
    for i in range(2 * NX):
        out[i] = lines


def second_partial(weights, gradient, stats, *refs):
    blocks, fresh, out = refs[:-2], refs[-2], refs[-1]
    total = stats[0]
    for i in range(1, 2 * NX):
        total += stats[i]
    rate = rate_of(total[3:4])
    old = weights[...].astype(F32)
    moved = old - rate * gradient[:PART].astype(F32)
    old_in, moved_in = old[: 2 * UNITS], moved[: 2 * UNITS]
    ratio_in = jnp.sqrt(jnp.sum(old_in * old_in, 1, keepdims=True)) / jnp.sqrt(
        jnp.sum(moved_in * moved_in, 1, keepdims=True) + epsilon
    )
    ratio_out = ratio_of(rate, total[0:1], total[1:2], total[2:3])
    new = jnp.concatenate([moved_in * ratio_in, moved[2 * UNITS :] * ratio_out], 0).astype(BF16)
    fresh[...] = new
    keys = jnp.concatenate([b[0] for b in blocks], 0)
    grads = jnp.concatenate([b[1] for b in blocks], 0)
    inner, outer = gradients(new[: 2 * UNITS], new[2 * UNITS :], keys, grads)
    out[0 : 2 * UNITS] = inner
    out[2 * UNITS : PART] = outer
    out[PART:] = jnp.zeros((PADDED - PART, WIDTH), BF16)


def rate_of(squares):
    return RATE / jnp.sqrt(jnp.sum(squares, 1, keepdims=True) / COUNT + epsilon)


def ratio_of(rate, old, cross, grad):
    moved = jnp.maximum(old - 2.0 * rate * cross + rate * rate * grad, 0.0)
    return jnp.sqrt(old) / jnp.sqrt(moved + epsilon)


def respond(group, queries, others, into, down, mine, theirs):
    rows = jnp.concatenate([queries[group], others[group]], 0)
    pre = dot(rows, into, 1, 1)
    gate, up = pre[:, :HALF], pre[:, HALF:]
    hidden = (gate * jax.nn.sigmoid(gate) * up).astype(BF16)
    result = dot(hidden, down)
    mine[...] = result[:ROWS]
    theirs[...] = result[ROWS:].astype(BF16)


def first_answer(queries, others, *refs):
    blocks, (mine, theirs) = refs[:NX], refs[NX:]
    parts = [
        jnp.concatenate([b[i * UNITS : (i + 1) * UNITS] for b in blocks], 0) for i in range(3)
    ]
    respond(0, queries, others, jnp.concatenate(parts[:2], 0), parts[2], mine, theirs)


def sums(weights, gradient, inner):
    old, grad = weights[...].astype(F32), gradient[:PART].astype(F32)
    products = [old * old, old * grad, grad * grad]
    for i, product in enumerate(products):
        inner[i] = jnp.sum(product[: 2 * UNITS], 1, keepdims=True)
    lines = [jnp.sum(p[2 * UNITS :], 0, keepdims=True) for p in products]
    return jnp.concatenate(lines + [jnp.sum(products[2], 0, keepdims=True)], 0)


def early_sums(*refs):
    held, blocks, (inner, lines) = refs[:2], refs[2:4], refs[4:]
    lines[0:4] = sum(sums(held[i], blocks[i], inner.at[i]) for i in range(2))
    lines[4:] = jnp.zeros((4, WIDTH), F32)


def late_sums(early, *refs):
    held, blocks, (inner, lines) = refs[:2], refs[2:4], refs[4:]
    lines[0:4] = early[0:4] + sum(sums(held[i], blocks[i], inner.at[i]) for i in range(2))
    lines[4:] = jnp.zeros((4, WIDTH), F32)


def second_answer(queries, others, own_lines, other_lines, early_in, late_in, *refs):
    held, blocks, (mine, theirs, into, down) = refs[:NX], refs[NX : 2 * NX], refs[2 * NX :]
    lines = own_lines[...] + other_lines[...]
    rate = rate_of(lines[3:4])
    ratio_out = ratio_of(rate, lines[0:1], lines[1:2], lines[2:3])
    inner = [early_in.at[0], late_in.at[0], late_in.at[1], early_in.at[1]]
    for i, (weights, block) in enumerate(zip(held, blocks)):
        moved = weights[...].astype(F32) - rate * block[:PART].astype(F32)
        ratio_in = ratio_of(rate, inner[i][0], inner[i][1], inner[i][2])
        fresh = (moved[: 2 * UNITS] * ratio_in).astype(BF16)
        into[i * UNITS : (i + 1) * UNITS] = fresh[:UNITS]
        into[HALF + i * UNITS : HALF + (i + 1) * UNITS] = fresh[UNITS:]
        down[i * UNITS : (i + 1) * UNITS] = (moved[2 * UNITS :] * ratio_out).astype(BF16)
    respond(1, queries, others, into[...], down[...], mine, theirs)


def joined(one, two, other_one, other_two, out):
    for group, (mine, theirs) in enumerate(((one, other_one), (two, other_two))):
        out[group] = (mine[...] + theirs[...].astype(F32)).astype(BF16)


def shifted(value, axis, size, shift):
    return lax.ppermute(value, axis, [(i, (i + shift) % size) for i in range(size)])


def along_x(block):
    return [block] + [shifted(block, "x", NX, shift) for shift in SHIFTS[1:]]


def from_core(near):
    return [shifted(b, "c", 2, 1) for b in near]


def reduce_z(partial):
    got = lax.all_to_all(partial.reshape(NZ, PADDED // NZ, WIDTH), "z", 0, 0, tiled=True)
    return kernel_call(summed, shape(*got.shape), [VMEM])(got)


def gather_z(shards):
    return lax.all_to_all(shards, "z", 0, 0, tiled=True).reshape(PADDED, WIDTH)


def under_z(partial, block):
    near = along_x(block)
    shards, near[:3] = lax.optimization_barrier((reduce_z(partial), near[:3]))
    return lax.optimization_barrier((gather_z(shards), near))


def body(queries, key_vectors, value_vectors, step_sizes, valid_rows, fast_init):
    held_inputs = (valid_rows, key_vectors[:, 0], value_vectors[:, 0], step_sizes)
    held_inputs += (queries[:, 0], fast_init[0])
    inputs = [pltpu.with_memory_space_constraint(i, pltpu.HBM) for i in held_inputs]
    pair, padded = shape(2, ROWS, WIDTH), shape(PADDED, WIDTH)
    scratch = [
        pltpu.SMEM(valid_rows.shape, jnp.int32),
        pltpu.VMEM((ROWS, WIDTH), BF16),
        pltpu.VMEM((1, ROWS), F32),
    ]
    window = shape(WIDTH, 384)
    first, *windows = kernel_call(
        prepare_first,
        (pair, window, window, shape(HALF, WIDTH)),
        [HBM] * 5,
        scratch + [pltpu.SemaphoreType.DMA((10,))],
    )(*inputs[:4], inputs[5])
    other = shifted(first, "c", 2, 1)
    into, own, queries = kernel_call(
        half_weights,
        (shape(2 * HALF, WIDTH), shape(PART, WIDTH), pair),
        [HBM] * 2 + [VMEM] * 3,
        [scratch[0], pltpu.VMEM(pair.shape, BF16), pltpu.SemaphoreType.DMA((2,))],
    )(inputs[0], inputs[4], *windows)
    parts = kernel_call(first_partial, (shape(PART, WIDTH),) * NX, [VMEM] * 4)(
        into, windows[2], first, other
    )
    mine, queries = lax.optimization_barrier((parts[0], queries))
    parts = [mine, *parts[1:]]
    others = shifted(queries, "c", 2, 1)
    parts = [parts[0]] + [shifted(p, "x", NX, s) for p, s in zip(parts[1:], SHIFTS[1:])]
    scratch += [pltpu.SemaphoreType.DMA((4,))]
    second = kernel_call(prepare_second, pair, [HBM] * 4, scratch)(*inputs[:4])
    *parts, second, others = lax.optimization_barrier((*parts, second, others))
    partial = kernel_call(summed_x, padded, [VMEM] * NX)(*parts)
    gradient, tokens = under_z(partial, second)
    tokens += from_core(tokens)
    stats = kernel_call(statistics, shape(2 * NX, 4, WIDTH, dtype=F32), [VMEM] * 2)(
        own, gradient
    )
    stats = lax.all_to_all(stats, ("x", "c"), 0, 0, tiled=True)
    fresh, partial = kernel_call(second_partial, (shape(PART, WIDTH), padded), [VMEM] * 11)(
        own, gradient, stats, *tokens
    )
    gradient, held = under_z(partial, fresh)
    gradient = gradient[:PART]
    near = along_x(gradient)
    share = (shape(ROWS, WIDTH, dtype=F32), shape(ROWS, WIDTH))
    one, theirs = kernel_call(first_answer, share, [VMEM] * 6)(queries, others, *held)
    found = (shape(2, 3, 2 * UNITS, 1, dtype=F32), shape(8, WIDTH, dtype=F32))
    early, lines = kernel_call(early_sums, found, [VMEM] * 4)(held[0], held[3], near[0], near[3])
    other_one = shifted(theirs, "c", 2, 1)
    near[1], near[2], lines, other_one = lax.optimization_barrier(
        (near[1], near[2], lines, other_one)
    )
    late, lines = kernel_call(late_sums, found, [VMEM] * 5)(lines, *held[1:3], *near[1:3])
    two, theirs = kernel_call(
        second_answer,
        share,
        [VMEM] * 14,
        [pltpu.VMEM((WIDTH, WIDTH), BF16), pltpu.VMEM((HALF, WIDTH), BF16)],
    )(queries, others, lines, shifted(lines, "c", 2, 1), early, late, *held, *near)
    other_two = shifted(theirs, "c", 2, 1)
    out = kernel_call(joined, shape(2, ROWS, WIDTH), [VMEM] * 4)(one, two, other_one, other_two)
    return out[:, None]


def solution(mesh):
    split = Mesh(mesh.devices.reshape(mesh.shape["head"], NZ, NX, 2), ("head", "z", "x", "c"))
    seq = ("z", "x", "c")
    rows = P(None, "head", seq, None)
    placed = (rows, rows, rows, P(None, "head", seq), P(), P("head", None, None))
    return jax.shard_map(body, mesh=split, in_specs=placed, out_specs=rows, check_vma=False)
```

```python
import jax
import jax.numpy as jnp
from jax import lax
from jax.experimental import pallas as pl
from jax.experimental.pallas import tpu as pltpu
from jax.sharding import Mesh
from jax.sharding import PartitionSpec as P

step_factor = 0.5
epsilon = 1e-06
NX = 4
NZ = 8
ROWS = 128
WIDTH = 640
UNITS = 80
HALF = NX * UNITS
SHIFTS = (0, 1, 3, 2)
PART = 3 * UNITS
PADDED = 256
RATE = step_factor / WIDTH**0.5
COUNT = 3 * WIDTH * WIDTH
F32 = jnp.float32
BF16 = jnp.bfloat16
VMEM = pl.BlockSpec(memory_space=pltpu.VMEM)
HBM = pl.BlockSpec(memory_space=pltpu.HBM)


def dot(a, b, ca=1, cb=0):
    return lax.dot_general(a, b, (((ca,), (cb,)), ((), ())), preferred_element_type=F32)


def shape(*dims, dtype=BF16):
    return jax.ShapeDtypeStruct(dims, dtype)


def kernel_call(body, outs, ins, scratch=()):
    return pl.pallas_call(
        body,
        out_shape=outs,
        in_specs=ins,
        out_specs=jax.tree.map(lambda _: VMEM, outs),
        scratch_shapes=list(scratch),
        compiler_params=pltpu.CompilerParams(vmem_limit_bytes=20 * 1024 * 1024),
    )


def own_count(valid, group):
    rank = (lax.axis_index("z") * NX + lax.axis_index("x")) * 2 + lax.axis_index("c")
    return valid[group, rank]


def fetch(pairs, sems):
    copies = [pltpu.make_async_copy(src, dst, sems.at[i]) for i, (src, dst) in enumerate(pairs)]
    for copy in copies:
        copy.start()
    for copy in copies:
        copy.wait()


def write_grads(live_rows, sizes, values, out):
    row = lax.broadcasted_iota(jnp.int32, (ROWS, ROWS), 0)
    col = lax.broadcasted_iota(jnp.int32, (ROWS, ROWS), 1)
    size = jnp.sum(jnp.where(row == col, sizes[...], 0.0), 1, keepdims=True)
    scaled = jnp.where(row[:, :1] < live_rows, size, 0.0)
    out[1] = (-(scaled * values[...].astype(F32))).astype(BF16)


def prepare_first(
    valid, keys, values, sizes, fast, out, gate_w, up_w, down_w, valid_s, value_s, size_s, sems
):
    x, c = lax.axis_index("x"), lax.axis_index("c")
    edge = pl.multiple_of(c * 256, 128)
    pairs = [
        (keys.at[0], out.at[0]),
        (values.at[0], value_s),
        (sizes.at[0], size_s),
        (valid, valid_s),
        (fast.at[:, pl.ds(edge, 384)], gate_w),
        (fast.at[:, pl.ds(WIDTH + edge, 384)], up_w),
    ]
    for i, shift in enumerate(SHIFTS):
        first = pl.multiple_of(c * HALF + lax.rem(x + shift, NX) * UNITS, UNITS)
        source = fast.at[pl.ds(first, UNITS), pl.ds(2 * WIDTH, WIDTH)]
        pairs.append((source, down_w.at[pl.ds(i * UNITS, UNITS)]))
    fetch(pairs, sems)
    write_grads(own_count(valid_s, 0), size_s, value_s, out)


def prepare_second(valid, keys, values, sizes, out, valid_s, value_s, size_s, sems):
    pairs = [
        (keys.at[1], out.at[0]),
        (values.at[1], value_s),
        (sizes.at[1], size_s),
        (valid, valid_s),
    ]
    fetch(pairs, sems)
    write_grads(own_count(valid_s, 1), size_s, value_s, out)


def half_weights(valid, queries, gate_w, up_w, down_w, into, own, live, valid_s, query_s, sems):
    copies = [
        pltpu.make_async_copy(valid, valid_s, sems.at[0]),
        pltpu.make_async_copy(queries, query_s, sems.at[1]),
    ]
    for copy in copies:
        copy.start()
    x, c = lax.axis_index("x"), lax.axis_index("c")
    row = lax.broadcasted_iota(jnp.int32, (HALF, 384), 0)
    col = lax.broadcasted_iota(jnp.int32, (HALF, 384), 1)
    wanted = row
    for i, shift in enumerate(SHIFTS):
        first = c * (HALF - 256) + lax.rem(x + shift, NX) * UNITS
        inside = (row >= i * UNITS) & (row < (i + 1) * UNITS)
        wanted = jnp.where(inside, first + row - i * UNITS, wanted)
    chosen = jnp.where(col == wanted, 1.0, 0.0).astype(BF16)
    for i, window in enumerate((gate_w, up_w)):
        found = dot(chosen, window[...], 1, 1).astype(BF16)
        into[i * HALF : (i + 1) * HALF] = found
        own[i * UNITS : (i + 1) * UNITS] = found[:UNITS]
    own[2 * UNITS :] = down_w[:UNITS]
    for copy in copies:
        copy.wait()
    row = lax.broadcasted_iota(jnp.int32, (ROWS, WIDTH), 0)
    for group in range(2):
        rows = query_s[group].astype(F32)
        live[group] = jnp.where(row < own_count(valid_s, group), rows, 0.0).astype(BF16)


def gradients(into, down, keys, grads):
    units = down.shape[0]
    pre = dot(into, keys, 1, 1)
    gate, up = pre[:units], pre[units:]
    d_hidden = dot(down, grads, 1, 1)
    sig = jax.nn.sigmoid(gate)
    hidden = (gate * sig * up).astype(BF16)
    d_up = (d_hidden * gate * sig).astype(BF16)
    d_gate = (d_hidden * up * sig * (1.0 + gate * (1.0 - sig))).astype(BF16)
    inner = dot(jnp.concatenate([d_gate, d_up], 0), keys).astype(BF16)
    return inner, dot(hidden, grads).astype(BF16)


def first_partial(into, down, own, other, *outs):
    keys = jnp.concatenate([own[0], other[0]], 0)
    grads = jnp.concatenate([own[1], other[1]], 0)
    inner, outer = gradients(into[...], down[...], keys, grads)
    for i, out in enumerate(outs):
        rows = slice(i * UNITS, (i + 1) * UNITS)
        out[0:UNITS] = inner[rows]
        out[UNITS : 2 * UNITS] = inner[HALF:][rows]
        out[2 * UNITS :] = outer[rows]


def summed_x(*refs):
    blocks, out = refs[:-1], refs[-1]
    total = blocks[0][...].astype(F32)
    for block in blocks[1:]:
        total += block[...].astype(F32)
    out[0:PART] = total.astype(BF16)
    out[PART:] = jnp.zeros((PADDED - PART, WIDTH), BF16)


def summed(got, out):
    total = got[0].astype(F32)
    for i in range(1, NZ):
        total += got[i].astype(F32)
    total = total.astype(BF16)
    for i in range(NZ):
        out[i] = total


def statistics(weights, gradient, out):
    grad = gradient[...].astype(F32)
    old = weights[2 * UNITS :].astype(F32)
    down = grad[2 * UNITS : PART]
    lines = [old * old, old * down, down * down, grad * grad]
    lines = jnp.concatenate([jnp.sum(line, 0, keepdims=True) for line in lines], 0)
    for i in range(2 * NX):
        out[i] = lines


def second_partial(weights, gradient, stats, *refs):
    blocks, fresh, out = refs[:-2], refs[-2], refs[-1]
    total = stats[0]
    for i in range(1, 2 * NX):
        total += stats[i]
    rate = rate_of(total[3:4])
    old = weights[...].astype(F32)
    moved = old - rate * gradient[:PART].astype(F32)
    old_in, moved_in = old[: 2 * UNITS], moved[: 2 * UNITS]
    ratio_in = jnp.sqrt(jnp.sum(old_in * old_in, 1, keepdims=True)) / jnp.sqrt(
        jnp.sum(moved_in * moved_in, 1, keepdims=True) + epsilon
    )
    ratio_out = ratio_of(rate, total[0:1], total[1:2], total[2:3])
    new = jnp.concatenate([moved_in * ratio_in, moved[2 * UNITS :] * ratio_out], 0).astype(BF16)
    fresh[...] = new
    keys = jnp.concatenate([b[0] for b in blocks], 0)
    grads = jnp.concatenate([b[1] for b in blocks], 0)
    inner, outer = gradients(new[: 2 * UNITS], new[2 * UNITS :], keys, grads)
    out[0 : 2 * UNITS] = inner
    out[2 * UNITS : PART] = outer
    out[PART:] = jnp.zeros((PADDED - PART, WIDTH), BF16)


def rate_of(squares):
    return RATE / jnp.sqrt(jnp.sum(squares, 1, keepdims=True) / COUNT + epsilon)


def ratio_of(rate, old, cross, grad):
    moved = jnp.maximum(old - 2.0 * rate * cross + rate * rate * grad, 0.0)
    return jnp.sqrt(old) / jnp.sqrt(moved + epsilon)


def respond(group, queries, others, into, down, mine, theirs):
    rows = jnp.concatenate([queries[group], others[group]], 0)
    pre = dot(rows, into, 1, 1)
    gate, up = pre[:, :HALF], pre[:, HALF:]
    hidden = (gate * jax.nn.sigmoid(gate) * up).astype(BF16)
    result = dot(hidden, down)
    mine[...] = result[:ROWS]
    theirs[...] = result[ROWS:].astype(BF16)


def first_answer(queries, others, *refs):
    blocks, (mine, theirs) = refs[:NX], refs[NX:]
    parts = [
        jnp.concatenate([b[i * UNITS : (i + 1) * UNITS] for b in blocks], 0) for i in range(3)
    ]
    respond(0, queries, others, jnp.concatenate(parts[:2], 0), parts[2], mine, theirs)


def sums(weights, gradient, inner):
    old, grad = weights[...].astype(F32), gradient[:PART].astype(F32)
    products = [old * old, old * grad, grad * grad]
    for i, product in enumerate(products):
        inner[i] = jnp.sum(product[: 2 * UNITS], 1, keepdims=True)
    lines = [jnp.sum(p[2 * UNITS :], 0, keepdims=True) for p in products]
    return jnp.concatenate(lines + [jnp.sum(products[2], 0, keepdims=True)], 0)


def early_sums(*refs):
    held, blocks, (inner, lines) = refs[:2], refs[2:4], refs[4:]
    lines[0:4] = sum(sums(held[i], blocks[i], inner.at[i]) for i in range(2))
    lines[4:] = jnp.zeros((4, WIDTH), F32)


def late_sums(early, *refs):
    held, blocks, (inner, lines) = refs[:2], refs[2:4], refs[4:]
    lines[0:4] = early[0:4] + sum(sums(held[i], blocks[i], inner.at[i]) for i in range(2))
    lines[4:] = jnp.zeros((4, WIDTH), F32)


def second_answer(queries, others, own_lines, other_lines, early_in, late_in, *refs):
    held, blocks, (mine, theirs, into, down) = refs[:NX], refs[NX : 2 * NX], refs[2 * NX :]
    lines = own_lines[...] + other_lines[...]
    rate = rate_of(lines[3:4])
    ratio_out = ratio_of(rate, lines[0:1], lines[1:2], lines[2:3])
    inner = [early_in.at[0], late_in.at[0], late_in.at[1], early_in.at[1]]
    for i, (weights, block) in enumerate(zip(held, blocks)):
        moved = weights[...].astype(F32) - rate * block[:PART].astype(F32)
        ratio_in = ratio_of(rate, inner[i][0], inner[i][1], inner[i][2])
        fresh = (moved[: 2 * UNITS] * ratio_in).astype(BF16)
        into[i * UNITS : (i + 1) * UNITS] = fresh[:UNITS]
        into[HALF + i * UNITS : HALF + (i + 1) * UNITS] = fresh[UNITS:]
        down[i * UNITS : (i + 1) * UNITS] = (moved[2 * UNITS :] * ratio_out).astype(BF16)
    respond(1, queries, others, into[...], down[...], mine, theirs)


def joined(one, two, other_one, other_two, out):
    for group, (mine, theirs) in enumerate(((one, other_one), (two, other_two))):
        out[group] = (mine[...] + theirs[...].astype(F32)).astype(BF16)


def shifted(value, axis, size, shift):
    return lax.ppermute(value, axis, [(i, (i + shift) % size) for i in range(size)])


def along_x(block):
    return [block] + [shifted(block, "x", NX, shift) for shift in SHIFTS[1:]]


def from_core(near):
    return [shifted(b, "c", 2, 1) for b in near]


def reduce_z(partial):
    got = lax.all_to_all(partial.reshape(NZ, PADDED // NZ, WIDTH), "z", 0, 0, tiled=True)
    return kernel_call(summed, shape(*got.shape), [VMEM])(got)


def gather_z(shards):
    return lax.all_to_all(shards, "z", 0, 0, tiled=True).reshape(PADDED, WIDTH)


def under_z(partial, block, tied):
    near = along_x(block)
    shards, near[:3] = lax.optimization_barrier((reduce_z(partial), near[:3]))
    total, near[:tied] = lax.optimization_barrier((gather_z(shards), near[:tied]))
    return total, near


def body(queries, key_vectors, value_vectors, step_sizes, valid_rows, fast_init):
    held_inputs = (valid_rows, key_vectors[:, 0], value_vectors[:, 0], step_sizes)
    held_inputs += (queries[:, 0], fast_init[0])
    inputs = [pltpu.with_memory_space_constraint(i, pltpu.HBM) for i in held_inputs]
    pair, padded = shape(2, ROWS, WIDTH), shape(PADDED, WIDTH)
    scratch = [
        pltpu.SMEM(valid_rows.shape, jnp.int32),
        pltpu.VMEM((ROWS, WIDTH), BF16),
        pltpu.VMEM((1, ROWS), F32),
    ]
    window = shape(WIDTH, 384)
    first, *windows = kernel_call(
        prepare_first,
        (pair, window, window, shape(HALF, WIDTH)),
        [HBM] * 5,
        scratch + [pltpu.SemaphoreType.DMA((10,))],
    )(*inputs[:4], inputs[5])
    other = shifted(first, "c", 2, 1)
    into, own, queries = kernel_call(
        half_weights,
        (shape(2 * HALF, WIDTH), shape(PART, WIDTH), pair),
        [HBM] * 2 + [VMEM] * 3,
        [scratch[0], pltpu.VMEM(pair.shape, BF16), pltpu.SemaphoreType.DMA((2,))],
    )(inputs[0], inputs[4], *windows)
    others = shifted(queries, "c", 2, 1)
    parts = kernel_call(first_partial, (shape(PART, WIDTH),) * NX, [VMEM] * 4)(
        into, windows[2], first, other
    )
    parts = [parts[0]] + [shifted(p, "x", NX, s) for p, s in zip(parts[1:], SHIFTS[1:])]
    scratch += [pltpu.SemaphoreType.DMA((4,))]
    second = kernel_call(prepare_second, pair, [HBM] * 4, scratch)(*inputs[:4])
    *parts, second, others = lax.optimization_barrier((*parts, second, others))
    partial = kernel_call(summed_x, padded, [VMEM] * NX)(*parts)
    gradient, tokens = under_z(partial, second, NX)
    tokens += from_core(tokens)
    stats = kernel_call(statistics, shape(2 * NX, 4, WIDTH, dtype=F32), [VMEM] * 2)(
        own, gradient
    )
    stats = lax.all_to_all(stats, ("x", "c"), 0, 0, tiled=True)
    fresh, partial = kernel_call(second_partial, (shape(PART, WIDTH), padded), [VMEM] * 11)(
        own, gradient, stats, *tokens
    )
    gradient, held = under_z(partial, fresh, 3)
    gradient = gradient[:PART]
    near = along_x(gradient)
    share = (shape(ROWS, WIDTH, dtype=F32), shape(ROWS, WIDTH))
    one, theirs = kernel_call(first_answer, share, [VMEM] * 6)(queries, others, *held)
    found = (shape(2, 3, 2 * UNITS, 1, dtype=F32), shape(8, WIDTH, dtype=F32))
    early, lines = kernel_call(early_sums, found, [VMEM] * 4)(held[0], held[3], near[0], near[3])
    other_one = shifted(theirs, "c", 2, 1)
    near[1], near[2], lines, other_one = lax.optimization_barrier(
        (near[1], near[2], lines, other_one)
    )
    late, lines = kernel_call(late_sums, found, [VMEM] * 5)(lines, *held[1:3], *near[1:3])
    two, theirs = kernel_call(
        second_answer,
        share,
        [VMEM] * 14,
        [pltpu.VMEM((WIDTH, WIDTH), BF16), pltpu.VMEM((HALF, WIDTH), BF16)],
    )(queries, others, lines, shifted(lines, "c", 2, 1), early, late, *held, *near)
    other_two = shifted(theirs, "c", 2, 1)
    out = kernel_call(joined, shape(2, ROWS, WIDTH), [VMEM] * 4)(one, two, other_one, other_two)
    return out[:, None]


def solution(mesh):
    split = Mesh(mesh.devices.reshape(mesh.shape["head"], NZ, NX, 2), ("head", "z", "x", "c"))
    seq = ("z", "x", "c")
    rows = P(None, "head", seq, None)
    placed = (rows, rows, rows, P(None, "head", seq), P(), P("head", None, None))
    return jax.shard_map(body, mesh=split, in_specs=placed, out_specs=rows, check_vma=False)
```

```python
import jax
import jax.numpy as jnp
from jax import lax
from jax.experimental import pallas as pl
from jax.experimental.pallas import tpu as pltpu
from jax.sharding import Mesh
from jax.sharding import PartitionSpec as P

step_factor = 0.5
epsilon = 1e-06
NX = 4
NZ = 8
ROWS = 128
WIDTH = 640
UNITS = 80
HALF = NX * UNITS
SHIFTS = (0, 1, 3, 2)
PART = 3 * UNITS
PADDED = 256
RATE = step_factor / WIDTH**0.5
COUNT = 3 * WIDTH * WIDTH
F32 = jnp.float32
BF16 = jnp.bfloat16
VMEM = pl.BlockSpec(memory_space=pltpu.VMEM)
HBM = pl.BlockSpec(memory_space=pltpu.HBM)


def dot(a, b, ca=1, cb=0):
    return lax.dot_general(a, b, (((ca,), (cb,)), ((), ())), preferred_element_type=F32)


def shape(*dims, dtype=BF16):
    return jax.ShapeDtypeStruct(dims, dtype)


def kernel_call(body, outs, ins, scratch=()):
    return pl.pallas_call(
        body,
        out_shape=outs,
        in_specs=ins,
        out_specs=jax.tree.map(lambda _: VMEM, outs),
        scratch_shapes=list(scratch),
        compiler_params=pltpu.CompilerParams(vmem_limit_bytes=20 * 1024 * 1024),
    )


def own_count(valid, group):
    rank = (lax.axis_index("z") * NX + lax.axis_index("x")) * 2 + lax.axis_index("c")
    return valid[group, rank]


def fetch(pairs, sems):
    copies = [pltpu.make_async_copy(src, dst, sems.at[i]) for i, (src, dst) in enumerate(pairs)]
    for copy in copies:
        copy.start()
    for copy in copies:
        copy.wait()


def write_grads(live_rows, sizes, values, out):
    row = lax.broadcasted_iota(jnp.int32, (ROWS, ROWS), 0)
    col = lax.broadcasted_iota(jnp.int32, (ROWS, ROWS), 1)
    size = jnp.sum(jnp.where(row == col, sizes[...], 0.0), 1, keepdims=True)
    scaled = jnp.where(row[:, :1] < live_rows, size, 0.0)
    out[1] = (-(scaled * values[...].astype(F32))).astype(BF16)


def prepare_first(
    valid, keys, values, sizes, fast, out, gate_w, up_w, down_w, valid_s, value_s, size_s, sems
):
    x, c = lax.axis_index("x"), lax.axis_index("c")
    edge = pl.multiple_of(c * 256, 128)
    pairs = [
        (keys.at[0], out.at[0]),
        (values.at[0], value_s),
        (sizes.at[0], size_s),
        (valid, valid_s),
        (fast.at[:, pl.ds(edge, 384)], gate_w),
        (fast.at[:, pl.ds(WIDTH + edge, 384)], up_w),
    ]
    for i, shift in enumerate(SHIFTS):
        first = pl.multiple_of(c * HALF + lax.rem(x + shift, NX) * UNITS, UNITS)
        source = fast.at[pl.ds(first, UNITS), pl.ds(2 * WIDTH, WIDTH)]
        pairs.append((source, down_w.at[pl.ds(i * UNITS, UNITS)]))
    fetch(pairs, sems)
    write_grads(own_count(valid_s, 0), size_s, value_s, out)


def prepare_second(valid, keys, values, sizes, out, valid_s, value_s, size_s, sems):
    pairs = [
        (keys.at[1], out.at[0]),
        (values.at[1], value_s),
        (sizes.at[1], size_s),
        (valid, valid_s),
    ]
    fetch(pairs, sems)
    write_grads(own_count(valid_s, 1), size_s, value_s, out)


def half_weights(valid, queries, gate_w, up_w, down_w, into, own, live, valid_s, query_s, sems):
    copies = [
        pltpu.make_async_copy(valid, valid_s, sems.at[0]),
        pltpu.make_async_copy(queries, query_s, sems.at[1]),
    ]
    for copy in copies:
        copy.start()
    x, c = lax.axis_index("x"), lax.axis_index("c")
    row = lax.broadcasted_iota(jnp.int32, (HALF, 384), 0)
    col = lax.broadcasted_iota(jnp.int32, (HALF, 384), 1)
    wanted = row
    for i, shift in enumerate(SHIFTS):
        first = c * (HALF - 256) + lax.rem(x + shift, NX) * UNITS
        inside = (row >= i * UNITS) & (row < (i + 1) * UNITS)
        wanted = jnp.where(inside, first + row - i * UNITS, wanted)
    chosen = jnp.where(col == wanted, 1.0, 0.0).astype(BF16)
    for i, window in enumerate((gate_w, up_w)):
        found = dot(chosen, window[...], 1, 1).astype(BF16)
        into[i * HALF : (i + 1) * HALF] = found
        own[i * UNITS : (i + 1) * UNITS] = found[:UNITS]
    own[2 * UNITS :] = down_w[:UNITS]
    for copy in copies:
        copy.wait()
    row = lax.broadcasted_iota(jnp.int32, (ROWS, WIDTH), 0)
    for group in range(2):
        rows = query_s[group].astype(F32)
        live[group] = jnp.where(row < own_count(valid_s, group), rows, 0.0).astype(BF16)


def gradients(into, down, keys, grads):
    units = down.shape[0]
    pre = dot(into, keys, 1, 1)
    gate, up = pre[:units], pre[units:]
    d_hidden = dot(down, grads, 1, 1)
    sig = jax.nn.sigmoid(gate)
    hidden = (gate * sig * up).astype(BF16)
    d_up = (d_hidden * gate * sig).astype(BF16)
    d_gate = (d_hidden * up * sig * (1.0 + gate * (1.0 - sig))).astype(BF16)
    inner = dot(jnp.concatenate([d_gate, d_up], 0), keys).astype(BF16)
    return inner, dot(hidden, grads).astype(BF16)


def first_partial(into, down, own, other, *outs):
    keys = jnp.concatenate([own[0], other[0]], 0)
    grads = jnp.concatenate([own[1], other[1]], 0)
    inner, outer = gradients(into[...], down[...], keys, grads)
    for i, out in enumerate(outs):
        rows = slice(i * UNITS, (i + 1) * UNITS)
        out[0:UNITS] = inner[rows]
        out[UNITS : 2 * UNITS] = inner[HALF:][rows]
        out[2 * UNITS :] = outer[rows]


def summed_x(*refs):
    blocks, out = refs[:-1], refs[-1]
    total = blocks[0][...].astype(F32)
    for block in blocks[1:]:
        total += block[...].astype(F32)
    out[0:PART] = total.astype(BF16)
    out[PART:] = jnp.zeros((PADDED - PART, WIDTH), BF16)


def summed(got, out):
    total = got[0].astype(F32)
    for i in range(1, NZ):
        total += got[i].astype(F32)
    total = total.astype(BF16)
    for i in range(NZ):
        out[i] = total


def statistics(weights, gradient, out):
    grad = gradient[...].astype(F32)
    old = weights[2 * UNITS :].astype(F32)
    down = grad[2 * UNITS : PART]
    lines = [old * old, old * down, down * down, grad * grad]
    lines = jnp.concatenate([jnp.sum(line, 0, keepdims=True) for line in lines], 0)
    for i in range(2 * NX):
        out[i] = lines


def second_partial(weights, gradient, stats, *refs):
    blocks, fresh, out = refs[:-2], refs[-2], refs[-1]
    total = stats[0]
    for i in range(1, 2 * NX):
        total += stats[i]
    rate = rate_of(total[3:4])
    old = weights[...].astype(F32)
    moved = old - rate * gradient[:PART].astype(F32)
    old_in, moved_in = old[: 2 * UNITS], moved[: 2 * UNITS]
    ratio_in = jnp.sqrt(jnp.sum(old_in * old_in, 1, keepdims=True)) / jnp.sqrt(
        jnp.sum(moved_in * moved_in, 1, keepdims=True) + epsilon
    )
    ratio_out = ratio_of(rate, total[0:1], total[1:2], total[2:3])
    new = jnp.concatenate([moved_in * ratio_in, moved[2 * UNITS :] * ratio_out], 0).astype(BF16)
    fresh[...] = new
    keys = jnp.concatenate([b[0] for b in blocks], 0)
    grads = jnp.concatenate([b[1] for b in blocks], 0)
    inner, outer = gradients(new[: 2 * UNITS], new[2 * UNITS :], keys, grads)
    out[0 : 2 * UNITS] = inner
    out[2 * UNITS : PART] = outer
    out[PART:] = jnp.zeros((PADDED - PART, WIDTH), BF16)


def rate_of(squares):
    return RATE / jnp.sqrt(jnp.sum(squares, 1, keepdims=True) / COUNT + epsilon)


def ratio_of(rate, old, cross, grad):
    moved = jnp.maximum(old - 2.0 * rate * cross + rate * rate * grad, 0.0)
    return jnp.sqrt(old) / jnp.sqrt(moved + epsilon)


def respond(group, queries, others, into, down, mine, theirs):
    rows = jnp.concatenate([queries[group], others[group]], 0)
    pre = dot(rows, into, 1, 1)
    gate, up = pre[:, :HALF], pre[:, HALF:]
    hidden = (gate * jax.nn.sigmoid(gate) * up).astype(BF16)
    result = dot(hidden, down)
    mine[...] = result[:ROWS]
    theirs[...] = result[ROWS:].astype(BF16)


def first_answer(queries, others, *refs):
    blocks, (mine, theirs) = refs[:NX], refs[NX:]
    parts = [
        jnp.concatenate([b[i * UNITS : (i + 1) * UNITS] for b in blocks], 0) for i in range(3)
    ]
    respond(0, queries, others, jnp.concatenate(parts[:2], 0), parts[2], mine, theirs)


def sums(weights, gradient, inner):
    old, grad = weights[...].astype(F32), gradient[:PART].astype(F32)
    products = [old * old, old * grad, grad * grad]
    for i, product in enumerate(products):
        inner[i] = jnp.sum(product[: 2 * UNITS], 1, keepdims=True)
    lines = [jnp.sum(p[2 * UNITS :], 0, keepdims=True) for p in products]
    return jnp.concatenate(lines + [jnp.sum(products[2], 0, keepdims=True)], 0)


def early_sums(*refs):
    held, blocks, (inner, lines) = refs[:2], refs[2:4], refs[4:]
    lines[0:4] = sum(sums(held[i], blocks[i], inner.at[i]) for i in range(2))


def late_sums(early, *refs):
    held, blocks, (inner, lines) = refs[:2], refs[2:4], refs[4:]
    lines[0:4] = early[0:4] + sum(sums(held[i], blocks[i], inner.at[i]) for i in range(2))


def second_answer(queries, others, own_lines, other_lines, early_in, late_in, *refs):
    held, blocks, (mine, theirs, into, down) = refs[:NX], refs[NX : 2 * NX], refs[2 * NX :]
    lines = own_lines[...] + other_lines[...]
    rate = rate_of(lines[3:4])
    ratio_out = ratio_of(rate, lines[0:1], lines[1:2], lines[2:3])
    inner = [early_in.at[0], late_in.at[0], late_in.at[1], early_in.at[1]]
    for i, (weights, block) in enumerate(zip(held, blocks)):
        moved = weights[...].astype(F32) - rate * block[:PART].astype(F32)
        ratio_in = ratio_of(rate, inner[i][0], inner[i][1], inner[i][2])
        fresh = (moved[: 2 * UNITS] * ratio_in).astype(BF16)
        into[i * UNITS : (i + 1) * UNITS] = fresh[:UNITS]
        into[HALF + i * UNITS : HALF + (i + 1) * UNITS] = fresh[UNITS:]
        down[i * UNITS : (i + 1) * UNITS] = (moved[2 * UNITS :] * ratio_out).astype(BF16)
    respond(1, queries, others, into[...], down[...], mine, theirs)


def joined(one, two, other_one, other_two, out):
    for group, (mine, theirs) in enumerate(((one, other_one), (two, other_two))):
        out[group] = (mine[...] + theirs[...].astype(F32)).astype(BF16)


def shifted(value, axis, size, shift):
    return lax.ppermute(value, axis, [(i, (i + shift) % size) for i in range(size)])


def along_x(block):
    return [block] + [shifted(block, "x", NX, shift) for shift in SHIFTS[1:]]


def from_core(near):
    return [shifted(b, "c", 2, 1) for b in near]


def reduce_z(partial):
    got = lax.all_to_all(partial.reshape(NZ, PADDED // NZ, WIDTH), "z", 0, 0, tiled=True)
    return kernel_call(summed, shape(*got.shape), [VMEM])(got)


def gather_z(shards):
    return lax.all_to_all(shards, "z", 0, 0, tiled=True).reshape(PADDED, WIDTH)


def under_z(partial, block, tied):
    near = along_x(block)
    shards, near[:3] = lax.optimization_barrier((reduce_z(partial), near[:3]))
    total, near[:tied] = lax.optimization_barrier((gather_z(shards), near[:tied]))
    return total, near


def body(queries, key_vectors, value_vectors, step_sizes, valid_rows, fast_init):
    held_inputs = (valid_rows, key_vectors[:, 0], value_vectors[:, 0], step_sizes)
    held_inputs += (queries[:, 0], fast_init[0])
    inputs = [pltpu.with_memory_space_constraint(i, pltpu.HBM) for i in held_inputs]
    pair, padded = shape(2, ROWS, WIDTH), shape(PADDED, WIDTH)
    scratch = [
        pltpu.SMEM(valid_rows.shape, jnp.int32),
        pltpu.VMEM((ROWS, WIDTH), BF16),
        pltpu.VMEM((1, ROWS), F32),
    ]
    window = shape(WIDTH, 384)
    first, *windows = kernel_call(
        prepare_first,
        (pair, window, window, shape(HALF, WIDTH)),
        [HBM] * 5,
        scratch + [pltpu.SemaphoreType.DMA((10,))],
    )(*inputs[:4], inputs[5])
    other = shifted(first, "c", 2, 1)
    into, own, queries = kernel_call(
        half_weights,
        (shape(2 * HALF, WIDTH), shape(PART, WIDTH), pair),
        [HBM] * 2 + [VMEM] * 3,
        [scratch[0], pltpu.VMEM(pair.shape, BF16), pltpu.SemaphoreType.DMA((2,))],
    )(inputs[0], inputs[4], *windows)
    others = shifted(queries, "c", 2, 1)
    parts = kernel_call(first_partial, (shape(PART, WIDTH),) * NX, [VMEM] * 4)(
        into, windows[2], first, other
    )
    parts = [parts[0]] + [shifted(p, "x", NX, s) for p, s in zip(parts[1:], SHIFTS[1:])]
    scratch += [pltpu.SemaphoreType.DMA((4,))]
    second = kernel_call(prepare_second, pair, [HBM] * 4, scratch)(*inputs[:4])
    *parts, second, others = lax.optimization_barrier((*parts, second, others))
    partial = kernel_call(summed_x, padded, [VMEM] * NX)(*parts)
    gradient, tokens = under_z(partial, second, NX)
    tokens += from_core(tokens)
    stats = kernel_call(statistics, shape(2 * NX, 4, WIDTH, dtype=F32), [VMEM] * 2)(
        own, gradient
    )
    stats = lax.all_to_all(stats, ("x", "c"), 0, 0, tiled=True)
    fresh, partial = kernel_call(second_partial, (shape(PART, WIDTH), padded), [VMEM] * 11)(
        own, gradient, stats, *tokens
    )
    gradient, held = under_z(partial, fresh, 3)
    gradient = gradient[:PART]
    near = along_x(gradient)
    share = (shape(ROWS, WIDTH, dtype=F32), shape(ROWS, WIDTH))
    one, theirs = kernel_call(first_answer, share, [VMEM] * 6)(queries, others, *held)
    found = (shape(2, 3, 2 * UNITS, 1, dtype=F32), shape(4, WIDTH, dtype=F32))
    early, lines = kernel_call(early_sums, found, [VMEM] * 4)(held[0], held[3], near[0], near[3])
    other_one = shifted(theirs, "c", 2, 1)
    near[1], near[2], lines, other_one = lax.optimization_barrier(
        (near[1], near[2], lines, other_one)
    )
    late, lines = kernel_call(late_sums, found, [VMEM] * 5)(lines, *held[1:3], *near[1:3])
    two, theirs = kernel_call(
        second_answer,
        share,
        [VMEM] * 14,
        [pltpu.VMEM((WIDTH, WIDTH), BF16), pltpu.VMEM((HALF, WIDTH), BF16)],
    )(queries, others, lines, shifted(lines, "c", 2, 1), early, late, *held, *near)
    other_two = shifted(theirs, "c", 2, 1)
    out = kernel_call(joined, shape(2, ROWS, WIDTH), [VMEM] * 4)(one, two, other_one, other_two)
    return out[:, None]


def solution(mesh):
    split = Mesh(mesh.devices.reshape(mesh.shape["head"], NZ, NX, 2), ("head", "z", "x", "c"))
    seq = ("z", "x", "c")
    rows = P(None, "head", seq, None)
    placed = (rows, rows, rows, P(None, "head", seq), P(), P("head", None, None))
    return jax.shard_map(body, mesh=split, in_specs=placed, out_specs=rows, check_vma=False)
```
